512 devices in a mesh: ax: 8 (over y), circ: 16 (over z, core), gap: 4 (over x).
Axes of the slice: x: 4, y: 8, z: 8, core: 2. Of those that a mesh axis runs over, the one named last changes fastest.
Arguments:
- w_old: float32 [64, 512, 512], P('ax', 'circ', 'gap'), may hold values from -3 to 3
- yield_stress: float32 [64, 512, 512], P('ax', 'circ', 'gap'), may hold values from 1 to 10
- force: float32 [64, 512, 512], P('ax', 'circ', 'gap'), may hold values from -9 to 9
- part_xi: float32 [8, 16, 4, 3, 8192], P('ax', 'circ', 'gap'), may hold values from -1 to 1
- part_vel: float32 [8, 16, 4, 3, 8192], P('ax', 'circ', 'gap'), may hold values from -3 to 3
- part_moment: float32 [8, 16, 4, 3, 8192], P('ax', 'circ', 'gap'), may hold values from -4 to 4
- elements: int32 [8, 16, 4, 8192], P('ax', 'circ', 'gap'), may hold values from 0 to 63
- new_elements: int32 [8, 16, 4, 8192], P('ax', 'circ', 'gap'), may hold values from 0 to 63
- send_slots: int32 [8, 16, 4, 6, 1024], P('ax', 'circ', 'gap'), may hold values from 0 to 8191, as said below
- counts: int32 [8, 16, 4, 6], P('ax', 'circ', 'gap'), may hold values from 1 to 1024, as said below
Outputs:
- w_new: float32 [64, 512, 512], P('ax', 'circ', 'gap')
- kept: float32 [8, 16, 4, 9, 8192], P('ax', 'circ', 'gap')
- arrived: float32 [8, 16, 4, 6, 9, 1024], P('ax', 'circ', 'gap')
The draws below stay inside these ranges and needn't reach their ends.
Inputs may be any that keep to these rules, and one draw needn't show every extreme that they name: `send_slots`: on each device the 6144 entries are distinct particle indices. `counts`: on every device one direction has exactly 1024 live slots.
All inputs are finite; a program needn't handle non-finite values.
Results may differ from the reference program's by a relative error of at most 0.0003.
Values sent between devices are 32-bit elements; how exact they have to be, the bound alone decides.
A program may use at most 64 MiB of HBM per device.

```python
import math
import jax
import jax.numpy as jnp
import numpy as np
from jax import lax

EA = 1
EC = 4
EG = 16
P_DEV = 8192
ITERS = 3
MIG = 1024
E_LOC = 64
NX = 64
NY = 512
NZ = 512
N_AX = 8
N_CIRC = 16
N_GAP = 4


def draw_force(key, part):
    axial_ramp = jnp.arange(NX, dtype=jnp.float32)[:, None, None] / NX
    circ_ramp = jnp.arange(NY, dtype=jnp.float32)[None, :, None] / NY
    ramp = (0.5 + axial_ramp) * (0.5 + circ_ramp)
    rough = jax.random.truncated_normal(key, -4.0, 4.0, (NX, NY, NZ), jnp.float32)
    return rough * ramp


def draw_send_slots(key, part):
    devices_all = N_AX * N_CIRC * N_GAP
    device_keys = jax.random.split(jax.random.fold_in(key, 17), devices_all)

    def leaving_of(device_key):
        return jax.random.permutation(device_key, P_DEV)[:6 * MIG]
    chosen = jax.vmap(leaving_of)(device_keys)
    return chosen.reshape(N_AX, N_CIRC, N_GAP, 6, MIG).astype(jnp.int32)


def draw_counts(key, part):
    base_key = jax.random.fold_in(key, 29)
    drawn = jax.random.randint(jax.random.fold_in(base_key, 1), (N_AX, N_CIRC, N_GAP, 6), 1, MIG + 1, jnp.int32)
    full_dir = jax.random.randint(jax.random.fold_in(base_key, 2), (N_AX, N_CIRC, N_GAP, 1), 0, 6, jnp.int32)
    return jnp.where(jnp.arange(6)[None, None, None, :] == full_dir, MIG, drawn).astype(jnp.int32)


def with_ends(entries, rng, least, largest):
    shape = entries.shape
    spot = [jax.random.randint(jax.random.fold_in(rng, axis), (), 0, shape[axis]) for axis in range(len(shape))]
    entries = entries.at[tuple(spot)].set(least)
    longest = shape.index(max(shape))
    spot[longest] = (spot[longest] + 1) % shape[longest]
    return entries.at[tuple(spot)].set(largest)


def levels(own_key, shape, shards, low, top_value):
    def one(dim, shards_of):
        heights = jax.random.uniform(jax.random.fold_in(jax.random.fold_in(own_key, 6), dim), (shards_of,), jnp.float32, low / len(shards), top_value / len(shards))
        return jnp.repeat(jnp.exp(heights), shape[dim] // shards_of).reshape((-1,) + (1,) * (len(shape) - dim - 1))

    factor_of = one(*shards[0])
    for cut in shards[1:]:
        factor_of = factor_of * one(*cut)
    return factor_of


def normal_values(rng, shape, scale, most, cuts=(), held_as=jnp.bfloat16):
    values = scale * jax.random.normal(rng, shape, jnp.float32)
    if cuts:
        values = values * levels(rng, shape, cuts, -0.22, 0.18)
    return jnp.clip(values, -most, most).astype(held_as)


def setup_inputs(seed: int = 0) -> dict:
    keys = jax.random.split(jax.random.key(seed), 11)
    return {
        "w_old": normal_values(keys[0], (NX, NY, NZ), 0.5, 3.0, ((0, 8), (1, 16), (2, 4)), jnp.float32),
        "yield_stress": jnp.clip(jnp.exp(math.log(10.0) - 2.3025851 * jax.random.uniform(keys[1], (NX, NY, NZ), jnp.float32) ** levels(keys[1], (NX, NY, NZ), ((0, 8), (1, 16), (2, 4)), -0.2, 0.2)), 1.0, 10.0),
        "force": draw_force(jax.random.fold_in(keys[10], 71), 0),
        "part_xi": jnp.clip(jax.random.uniform(keys[3], (N_AX, N_CIRC, N_GAP, 3, P_DEV), jnp.float32, -1.0, 1.0) * levels(keys[3], (N_AX, N_CIRC, N_GAP, 3, P_DEV), ((0, 8), (1, 16), (2, 4)), -0.4, 0.0), -1.0, 1.0),
        "part_vel": normal_values(keys[4], (N_AX, N_CIRC, N_GAP, 3, P_DEV), 0.5, 3.0, ((0, 8), (1, 16), (2, 4)), jnp.float32),
        "part_moment": normal_values(keys[5], (N_AX, N_CIRC, N_GAP, 3, P_DEV), 1.0, 4.0, ((0, 8), (1, 16), (2, 4)), jnp.float32),
        "elements": with_ends(jax.random.randint(keys[6], (N_AX, N_CIRC, N_GAP, P_DEV), 0, E_LOC), jax.random.fold_in(keys[6], 1), 0, E_LOC - 1).astype(jnp.int32),
        "new_elements": with_ends(jax.random.randint(keys[7], (N_AX, N_CIRC, N_GAP, P_DEV), 0, E_LOC), jax.random.fold_in(keys[7], 1), 0, E_LOC - 1).astype(jnp.int32),
        "send_slots": draw_send_slots(jax.random.fold_in(keys[10], 71), 0),
        "counts": draw_counts(jax.random.fold_in(keys[10], 71), 0),
    }


GLL_NODES = np.array([-1.0, -0.8717401485096066, -0.5917001814331423, -0.2092992179024789, 0.2092992179024789, 0.5917001814331423, 0.8717401485096066, 1.0])
GLL_WEIGHTS = np.array([0.03571428571428571, 0.2107042271435061, 0.3411226924835044, 0.4124587946587038, 0.4124587946587038, 0.3411226924835044, 0.2107042271435061, 0.03571428571428571])
TIME_STEP = 0.25
PLASTIC_VISC = 0.05
REGULAR_SHIFT = 1.0
DRAG_RELAX = 0.4
METRIC = (1.0, 1.0, 4.0)
JACOBIAN = 0.25

def bary_weights():
    identity_mask = np.eye(8, dtype=bool)
    differences = np.where(identity_mask, 1.0, GLL_NODES[:, None] - GLL_NODES[None, :])
    return (1.0 / np.prod(differences, axis=1), differences)

def diff_table():
    barycentric, differences = bary_weights()
    identity_mask = np.eye(8, dtype=bool)
    off_diag = np.where(identity_mask, 0.0, barycentric[None, :] / barycentric[:, None] / differences)
    diff_matrix = off_diag - np.eye(8) * np.sum(off_diag, axis=1)[:, None]
    return diff_matrix.astype(np.float32)

def lagrange_basis(points):
    barycentric, unused = bary_weights()
    columns = []
    for column in range(8):
        product_term = jnp.full(points.shape, np.float32(barycentric[column]), points.dtype)
        for other_node in range(8):
            if other_node != column:
                product_term = product_term * (points - np.float32(GLL_NODES[other_node]))
        columns.append(product_term)
    return jnp.stack(columns)

def sample_elements(element_table, element_ids, points):
    basis_first = lagrange_basis(points[0])
    basis_second = lagrange_basis(points[1])
    basis_third = lagrange_basis(points[2])
    combined = basis_first[:, None, None, :] * basis_second[None, :, None, :] * basis_third[None, None, :, :]
    combined = combined.reshape(512, points.shape[1])
    picked = jnp.take(element_table, element_ids, axis=1)
    return lax.optimization_barrier(jnp.sum(picked * combined, axis=0))

def advance(state, fluid):
    axial_vel = state[3] + DRAG_RELAX * (fluid - state[3])
    circ_vel = state[4] * (1.0 - DRAG_RELAX)
    radial_vel = state[5] * (1.0 - DRAG_RELAX)
    return jnp.stack([state[0] + TIME_STEP * METRIC[0] * axial_vel, state[1] + TIME_STEP * METRIC[1] * circ_vel, state[2] + TIME_STEP * METRIC[2] * radial_vel, axial_vel, circ_vel, radial_vel, state[6], state[7], state[8]])

def pack_leaving(state, new_ids, slots, live_counts):
    flat_slots = slots.reshape(-1)
    capacity = slots.shape[1]
    chosen = jnp.transpose(jnp.take(state, flat_slots, axis=1).reshape(9, 6, capacity), (1, 0, 2))
    targets = jnp.take(new_ids, flat_slots).reshape(6, 1, capacity).astype(state.dtype)
    live_flag = (jnp.arange(capacity)[None, :] < live_counts[:, None]).astype(state.dtype)
    buffers = jnp.concatenate([chosen, targets, jnp.ones_like(targets)], axis=1) * live_flag[:, None, :]
    departed = jnp.zeros((state.shape[1],), state.dtype).at[flat_slots].max(live_flag.reshape(-1))
    return (buffers, departed)

def settle_arrivals(arrivals, element_table):
    capacity = arrivals.shape[2]
    flattened = jnp.transpose(arrivals, (1, 0, 2)).reshape(11, 6 * capacity)
    element_ids = flattened[9].astype(jnp.int32)
    fluid = sample_elements(element_table, element_ids, flattened[0:3])
    moved = advance(flattened[0:9], fluid) * flattened[10][None, :]
    return jnp.transpose(moved.reshape(9, 6, capacity), (1, 0, 2))

def face_share(local_count, position, parts, open_ends):
    node_ids = jnp.arange(local_count) + position * local_count
    local_point = node_ids % 8
    on_face = (local_point == 0) | (local_point == 7)
    if open_ends:
        on_face = on_face & (node_ids != 0) & (node_ids != local_count * parts - 1)
    return jnp.where(on_face, 0.5, 1.0).astype(jnp.float32)

def wall_mask(local_count, position, parts):
    node_ids = jnp.arange(local_count) + position * local_count
    return jnp.where((node_ids == 0) | (node_ids == local_count * parts - 1), 0.0, 1.0).astype(jnp.float32)

def quad_weights(count_first, count_second, count_third):
    first_w = jnp.asarray(np.tile(GLL_WEIGHTS, count_first // 8).astype(np.float32))
    second_w = jnp.asarray(np.tile(GLL_WEIGHTS, count_second // 8).astype(np.float32))
    third_w = jnp.asarray(np.tile(GLL_WEIGHTS, count_third // 8).astype(np.float32))
    return first_w[:, None, None] * second_w[None, :, None] * third_w[None, None, :]

def element_derive(nodal_field, diff_matrix, axis_pos, transposed):
    extent = nodal_field.shape
    blocks = nodal_field.reshape(extent[0] // 8, 8, extent[1] // 8, 8, extent[2] // 8, 8)
    matrix = jnp.asarray(diff_matrix.T if transposed else diff_matrix)
    patterns = ('ij,ajbkcl->aibkcl', 'ij,akbjcl->akbicl', 'ij,akblcj->akblci')
    return jnp.einsum(patterns[axis_pos], matrix, blocks, precision=lax.Precision.HIGHEST).reshape(extent)

def assemble_axis(nodal_field, axis_pos, periodic):
    moved = jnp.moveaxis(nodal_field, axis_pos, 0)
    firsts = moved[0::8]
    lasts = moved[7::8]
    if periodic:
        before = jnp.concatenate([lasts[-1:], lasts[:-1]], axis=0)
        after = jnp.concatenate([firsts[1:], firsts[:1]], axis=0)
    else:
        before = jnp.concatenate([jnp.zeros_like(lasts[:1]), lasts[:-1]], axis=0)
        after = jnp.concatenate([firsts[1:], jnp.zeros_like(firsts[:1])], axis=0)
    moved = moved.at[0::8].add(before).at[7::8].add(after)
    return jnp.moveaxis(moved, 0, axis_pos)

def assemble(nodal_field):
    result_field = assemble_axis(nodal_field, 0, False)
    result_field = assemble_axis(result_field, 1, True)
    return assemble_axis(result_field, 2, False)

def shift_open(buffers, axis_pos, offset):
    length = buffers.shape[axis_pos]
    zeros_plane = jnp.zeros_like(lax.slice_in_dim(buffers, 0, 1, axis=axis_pos))
    if offset > 0:
        return jnp.concatenate([zeros_plane, lax.slice_in_dim(buffers, 0, length - 1, axis=axis_pos)], axis=axis_pos)
    return jnp.concatenate([lax.slice_in_dim(buffers, 1, length, axis=axis_pos), zeros_plane], axis=axis_pos)

def reference(w_old, yield_stress, force, part_xi, part_vel, part_moment, elements, new_elements, send_slots, counts):
    diff_matrix = diff_table()
    quadrature = quad_weights(NX, NY, NZ)
    node_share = face_share(NX, 0, 1, True)[:, None, None] * face_share(NY, 0, 1, False)[None, :, None] * face_share(NZ, 0, 1, True)[None, None, :]
    wall_gate = wall_mask(NZ, 0, 1)[None, None, :]
    squares = REGULAR_SHIFT ** 2
    for axis_pos in range(3):
        gradient = element_derive(w_old, diff_matrix, axis_pos, False) * METRIC[axis_pos]
        squares = squares + gradient * gradient
    viscosity = PLASTIC_VISC + yield_stress / jnp.sqrt(squares)
    weighted = quadrature * viscosity
    stiffness = [weighted * (JACOBIAN * METRIC[axis_pos] ** 2) for axis_pos in range(3)]
    mass_diag = quadrature * (JACOBIAN / TIME_STEP)

    def operate(direction):
        applied = mass_diag * direction
        for axis_pos in range(3):
            inner_grad = element_derive(direction, diff_matrix, axis_pos, False)
            applied = applied + element_derive(stiffness[axis_pos] * inner_grad, diff_matrix, axis_pos, True)
        return wall_gate * assemble(applied)

    def inner(left, right):
        return jnp.sum(node_share * left * right)
    rhs = wall_gate * assemble(quadrature * JACOBIAN * (w_old * (1.0 / TIME_STEP) + force))
    solution = jnp.zeros_like(rhs)
    residual = rhs
    direction = rhs
    norm_now = inner(residual, residual)
    for iteration in range(ITERS):
        image = operate(direction)
        alpha = norm_now / inner(direction, image)
        solution = solution + alpha * direction
        residual = residual - alpha * image
        norm_next = inner(residual, residual)
        direction = residual + norm_next / norm_now * direction
        norm_now = norm_next
    devices_all = N_AX * N_CIRC * N_GAP
    tables = jnp.transpose(solution.reshape(N_AX, EA, 8, N_CIRC, EC, 8, N_GAP, EG, 8), (0, 3, 6, 2, 5, 8, 1, 4, 7)).reshape(devices_all, 512, E_LOC)
    states = jnp.concatenate([part_xi, part_vel, part_moment], axis=3).reshape(devices_all, 9, P_DEV)
    buffers, departed = jax.vmap(pack_leaving)(states, new_elements.reshape(devices_all, P_DEV), send_slots.reshape(devices_all, 6, MIG), counts.reshape(devices_all, 6))
    buffers = buffers.reshape(N_AX, N_CIRC, N_GAP, 6, 11, MIG)
    arrivals = jnp.stack([shift_open(buffers[:, :, :, 0], 0, 1), shift_open(buffers[:, :, :, 1], 0, -1), jnp.roll(buffers[:, :, :, 2], 1, axis=1), jnp.roll(buffers[:, :, :, 3], -1, axis=1), shift_open(buffers[:, :, :, 4], 2, 1), shift_open(buffers[:, :, :, 5], 2, -1)], axis=3).reshape(devices_all, 6, 11, MIG)

    def keep_one(device_items):
        fluid = sample_elements(device_items[0], device_items[1], device_items[2][0:3])
        return advance(device_items[2], fluid) * (1.0 - device_items[3])[None, :]
    kept = lax.map(keep_one, (tables, elements.reshape(devices_all, P_DEV), states, departed))

    def arrive_one(device_items):
        return settle_arrivals(device_items[1], device_items[0])
    arrived = lax.map(arrive_one, (tables, arrivals))
    return (solution, kept.reshape(N_AX, N_CIRC, N_GAP, 9, P_DEV), arrived.reshape(N_AX, N_CIRC, N_GAP, 6, 9, MIG))
```

```python
import functools
import jax, jax.numpy as jnp, numpy as np
from jax import lax
from jax.experimental import pallas as pl
from jax.experimental.pallas import tpu as pltpu
from jax.sharding import PartitionSpec as P

MESH = pl.DeviceIdType.MESH
GLL_NODES = np.array([-1.0,-0.8717401485096066,-0.5917001814331423,-0.2092992179024789,0.2092992179024789,0.5917001814331423,0.8717401485096066,1.0])

GLL_WEIGHTS = np.array([0.03571428571428571,0.2107042271435061,0.3411226924835044,0.4124587946587038,0.4124587946587038,0.3411226924835044,0.2107042271435061,0.03571428571428571])

def bary_weights():
    eye = np.eye(8, dtype=bool)
    diff = np.where(eye, 1.0, GLL_NODES[:, None] - GLL_NODES[None, :])
    return 1.0 / np.prod(diff, axis=1)

def pick(rows, lanes):
    return jnp.take_along_axis(rows, lanes, axis=1, mode="promise_in_bounds")

def pack_kernel(counts_ref, xi_ref, vel_ref, mom_ref, new_ref, slots_ref, buf_ref, dep_ref, st_ref, rows_ref):
    st_ref[0:3, :] = xi_ref[...]
    st_ref[3:6, :] = vel_ref[...]
    st_ref[6:9, :] = mom_ref[...]
    st_ref[9:10, :] = new_ref[...].astype(jnp.float32)
    for row in range(6):
        rows_ref[row] = slots_ref[row:row + 1, :]
    st_ref[10:16, :] = jnp.ones((6, 8192), jnp.float32)
    lane = lax.broadcasted_iota(jnp.int32, (8, 128), 1)

    @pl.loop(0, 48)
    def _(group):
        row = group // 8
        start = pl.multiple_of((group % 8) * 128, 128)
        slot = jnp.broadcast_to(rows_ref[row, :, pl.ds(start, 128)], (8, 128))
        block = lax.shift_right_logical(slot, 7)
        within = lax.bitwise_and(slot, 127)
        first = jnp.zeros((8, 128), jnp.float32)
        second = jnp.zeros((8, 128), jnp.float32)
        for h in range(64):
            here = block == h
            cols = slice(h * 128, (h + 1) * 128)
            first = jnp.where(here, pick(st_ref[0:8, cols], within), first)
            second = jnp.where(here, pick(st_ref[8:16, cols], within), second)
        live = (lane + start < counts_ref[row]).astype(jnp.float32)
        first = first * live
        second = second * live
        buf_ref[row, 0:8, pl.ds(start, 128)] = first
        buf_ref[row, 8:11, pl.ds(start, 128)] = second[0:3]

    sub64 = lax.broadcasted_iota(jnp.int32, (64, 1024), 0)
    sub128 = lax.broadcasted_iota(jnp.int32, (128, 1024), 0)
    lanes = lax.broadcasted_iota(jnp.int32, (1, 1024), 1)
    total = jnp.zeros((64, 128), jnp.float32)
    for row in range(6):
        slot = slots_ref[row:row + 1, :]
        block = jnp.where(lanes < counts_ref[row], lax.shift_right_logical(slot, 7), 64)
        within = lax.bitwise_and(slot, 127)
        blocks = jnp.where(sub64 == block, 1.0, 0.0).astype(jnp.bfloat16)
        places = jnp.where(sub128 == within, 1.0, 0.0).astype(jnp.bfloat16)
        total = total + lax.dot_general(blocks, places, (((1,), (1,)), ((), ())), preferred_element_type=jnp.float32)
    for row in range(64):
        dep_ref[row] = total[row:row + 1]

def pack(xi, vel, mom, new, slots, counts):
    return pl.pallas_call(
        pack_kernel,
        out_shape=(jax.ShapeDtypeStruct((6, 11, 1024), jnp.float32), jax.ShapeDtypeStruct((64, 1, 128), jnp.float32)),
        in_specs=[pl.BlockSpec(memory_space=pltpu.SMEM)] + [pl.BlockSpec(memory_space=pltpu.VMEM)] * 5,
        out_specs=(pl.BlockSpec(memory_space=pltpu.VMEM),) * 2,
        scratch_shapes=[pltpu.VMEM((16, 8192), jnp.float32), pltpu.VMEM((6, 1, 1024), jnp.int32)],
        name="pack",
    )(counts, xi, vel, mom, new, slots)

def ladder(x):
    d = [x - np.float32(n) for n in GLL_NODES]
    pre = [None] * 8
    suf = [None] * 8
    pre[1] = d[0]
    for k in range(2, 8):
        pre[k] = pre[k - 1] * d[k - 1]
    suf[6] = d[7]
    for k in range(5, -1, -1):
        suf[k] = suf[k + 1] * d[k + 1]
    return [suf[0]] + [pre[k] * suf[k] for k in range(1, 7)] + [pre[7]]

def settle_kernel(gate_ref, w_ref, perm_ref, bary_ref, other_ref, xi_ref, vel_ref, mom_ref, el_ref, dep_ref, arr_ref, w_out, kept_ref, arrived_ref, table_ref):
    w = w_ref[...]
    w_out[...] = w
    moved = jnp.dot(w, perm_ref[...], precision=lax.Precision.HIGHEST, preferred_element_type=jnp.float32)
    lane = lax.broadcasted_iota(jnp.int32, (8, 128), 1)
    region = lane // 16
    for i in range(8):
        for k in range(8):
            entry = jnp.zeros((8, 128), jnp.float32)
            for c in range(4):
                part = moved[i * 32 + c * 8:i * 32 + c * 8 + 8]
                shift = ((c - k) * 16) % 128
                if shift:
                    part = pltpu.roll(part, shift, 1)
                entry = jnp.where(region == c, part, entry)
            table_ref[i * 8 + k] = entry * bary_ref[i * 8 + k]

    def sample(ids, x1, x2, x3):
        ids = jnp.broadcast_to(ids, (8, 128))
        l1 = ladder(jnp.broadcast_to(x1, (8, 128)))
        l3 = ladder(jnp.broadcast_to(x3, (8, 128)))
        x2 = jnp.broadcast_to(x2, (8, 128))
        l2 = x2 - other_ref[0]
        for t in range(1, 7):
            l2 = l2 * (x2 - other_ref[t])
        total = None
        for i in range(8):
            line = None
            for k in range(8):
                term = pick(table_ref[i * 8 + k], ids) * l3[k]
                line = term if line is None else line + term
            line = line * l1[i]
            total = line if total is None else total + line
        return jnp.sum(total * l2, axis=0, keepdims=True)

    def update(xi, vel, fluid):
        axial = vel[0:1] + 0.4 * (fluid - vel[0:1])
        circ = vel[1:2] * (1.0 - 0.4)
        radial = vel[2:3] * (1.0 - 0.4)
        return [xi[0:1] + 0.25 * axial, xi[1:2] + 0.25 * circ, xi[2:3] + 1.0 * radial, axial, circ, radial]

    @pl.loop(0, 64)
    def _(group):
        cols = pl.ds(pl.multiple_of(group * 128, 128), 128)
        xi = xi_ref[:, cols]
        vel = vel_ref[:, cols]
        fluid = sample(el_ref[:, cols], xi[0:1], xi[1:2], xi[2:3])
        stay = 1.0 - dep_ref[group]
        for row, value in enumerate(update(xi, vel, fluid)):
            kept_ref[row:row + 1, cols] = value * stay
        kept_ref[6:9, cols] = mom_ref[:, cols] * stay

    @pl.loop(0, 48)
    def _(group):
        row = group // 8
        cols = pl.ds(pl.multiple_of((group % 8) * 128, 128), 128)
        state = arr_ref[row, 0:8, cols]
        rest = arr_ref[row, 8:11, cols]
        fluid = sample(rest[1:2].astype(jnp.int32), state[0:1], state[1:2], state[2:3])
        live = rest[2:3] * gate_ref[row]
        for at, value in enumerate(update(state[0:3], state[3:6], fluid)):
            arrived_ref[row, at:at + 1, cols] = value * live
        arrived_ref[row, 6:8, cols] = state[6:8] * live
        arrived_ref[row, 8:9, cols] = rest[0:1] * live

def settle_consts():
    perm = np.zeros((128, 128), np.float32)
    for g in range(16):
        for k in range(8):
            perm[g * 8 + k, k * 16 + g] = 1.0
    b = bary_weights()
    bary = np.broadcast_to((b[:, None, None] * b[None, :, None] * b[None, None, :]).reshape(64, 8, 1), (64, 8, 128)).astype(np.float32)
    other = np.stack([np.broadcast_to(np.roll(GLL_NODES, -t)[:, None], (8, 128)) for t in range(1, 8)]).astype(np.float32)
    return perm, bary, other

def settle(gate, w, xi, vel, mom, el, dep, arr):
    perm, bary, other = settle_consts()
    return pl.pallas_call(
        settle_kernel,
        out_shape=(jax.ShapeDtypeStruct((256, 128), jnp.float32), jax.ShapeDtypeStruct((9, 8192), jnp.float32), jax.ShapeDtypeStruct((6, 9, 1024), jnp.float32)),
        in_specs=[pl.BlockSpec(memory_space=pltpu.SMEM)] + [pl.BlockSpec(memory_space=pltpu.VMEM)] * 10,
        out_specs=(pl.BlockSpec(memory_space=pltpu.VMEM),) * 3,
        scratch_shapes=[pltpu.VMEM((64, 8, 128), jnp.float32)],
        name="settle",
    )(gate, w, perm, bary, other, xi, vel, mom, el, dep, arr)


def field_consts():
    b = bary_weights()
    eye = np.eye(8, dtype=bool)
    diff = np.where(eye, 1.0, GLL_NODES[:, None] - GLL_NODES[None, :])
    off = np.where(eye, 0.0, b[None, :] / b[:, None] / diff)
    d = (off - np.eye(8) * np.sum(off, axis=1)[:, None]).astype(np.float32)
    left = np.concatenate([np.kron(d, np.eye(32, dtype=np.float32)), np.kron(np.eye(32, dtype=np.float32), d)])
    right = 4.0 * np.kron(np.eye(16, dtype=np.float32), d.T)
    w8 = GLL_WEIGHTS.astype(np.float32)
    wr = (w8[:, None, None] * np.tile(w8, 4)[None, :, None]).reshape(256, 1)
    quad = wr * np.tile(w8, 16)[None, :]
    half = np.where((np.arange(8) == 0) | (np.arange(8) == 7), 0.5, 1.0)
    share = (half[:, None] * np.tile(half, 4)[None, :]).reshape(256, 1) * np.tile(half, 16)[None, :]
    r = np.arange(256)[:, None] % 32 + np.zeros((1, 128))
    c = np.arange(128)[None, :] + np.zeros((256, 1))
    masks = np.stack([(r % 8 == 0) & (r > 0), (r % 8 == 7) & (r < 31), (c % 8 == 0) & (c > 0), (c % 8 == 7) & (c < 127)])
    ends = np.zeros((8, 128))
    ends[0, 0] = 1.0
    ends[1, 127] = 1.0
    return [np.ascontiguousarray(t, dtype=np.float32) for t in (left, left.T, right, right.T, quad, share, masks, ends)]

def exact_dot(a, b, dims=((1,), (0,))):
    return lax.dot_general(a, b, (dims, ((), ())), precision=lax.Precision.HIGHEST, preferred_element_type=jnp.float32)

def flow_kernel(sizes, w_ref, yield_ref, force_ref, left_ref, left_t_ref, right_ref, right_t_ref, quad_ref, share_ref, masks_ref, ends_ref, buf_ref,
                out_ref, arr_ref, v_ref, f_ref, z_ref, edge_c, edge_e, edge_g, got_a, got_c, got_e, got_g, pair_ref, sum_ref, got_sum,
                send_sem, recv_sem, sum_send, sum_recv, mig_send, mig_recv):
    n_ax, n_circ, n_gap = sizes
    ax, circ, gap = lax.axis_index("ax"), lax.axis_index("circ"), lax.axis_index("gap")

    def at(da=0, dc=0, dg=0):
        place = {}
        if da:
            place["ax"] = lax.rem(ax + (da + n_ax), n_ax)
        if dc:
            place["circ"] = lax.rem(circ + (dc + n_circ), n_circ)
        if dg:
            place["gap"] = lax.rem(gap + (dg + n_gap), n_gap)
        return place

    peers = [at(da=o) for o in range(1, n_ax)] + [at(dc=o) for o in range(1, n_circ)] + [at(dg=o) for o in range(1, n_gap)]
    peers += [at(da=a, dc=c) for a in (-1, 1) for c in (-1, 1)]
    barrier = pltpu.get_barrier_semaphore()
    for peer in peers:
        pl.semaphore_signal(barrier, inc=1, device_id=peer, device_id_type=MESH)

    quad = quad_ref[...]
    row = lax.broadcasted_iota(jnp.int32, (256, 128), 0)
    col = lax.broadcasted_iota(jnp.int32, (256, 128), 1)
    at_wall = ((col == 0) & (gap == 0)) | ((col == 127) & (gap == n_gap - 1))
    wall = jnp.where(at_wall, 0.0, 1.0)
    share = share_ref[...] * jnp.where(at_wall, 2.0, 1.0)
    share = share * jnp.where(((row < 32) & (ax == 0)) | ((row >= 224) & (ax == n_ax - 1)), 2.0, 1.0)
    low_ax = jnp.where(ax == 0, 0.0, 1.0)
    high_ax = jnp.where(ax == n_ax - 1, 0.0, 1.0)
    low_gap = jnp.where(gap == 0, 0.0, 1.0)
    high_gap = jnp.where(gap == n_gap - 1, 0.0, 1.0)
    pair_ref[...] = jnp.zeros((8, 256), jnp.float32)

    def gather_inner(f):
        f = f + masks_ref[0] * pltpu.roll(f, 1, 0) + masks_ref[1] * pltpu.roll(f, 255, 0)
        return f + masks_ref[2] * pltpu.roll(f, 1, 1) + masks_ref[3] * pltpu.roll(f, 127, 1)

    def remote(src, dst, k, t, place):
        return pltpu.make_async_remote_copy(src_ref=src, dst_ref=dst, send_sem=send_sem.at[k, t], recv_sem=recv_sem.at[k, t],
                                            device_id=place, device_id_type=MESH)

    def first_phase(k, f):
        f = gather_inner(f)
        f_ref[k] = f
        z_ref[k] = f
        edge_c[k, 0] = f_ref[k, pl.ds(0, 8, stride=32), :]
        edge_c[k, 1] = f_ref[k, pl.ds(31, 8, stride=32), :]
        for e, at_row in enumerate((0, 31, 224, 255)):
            edge_e[k, e] = f_ref[k, at_row:at_row + 1, :]
        copies = [remote(f_ref.at[k, 0:32], got_a.at[k, 1], k, 0, at(da=-1)),
                  remote(f_ref.at[k, 224:256], got_a.at[k, 0], k, 1, at(da=1)),
                  remote(edge_c.at[k, 0], got_c.at[k, 1], k, 2, at(dc=-1)),
                  remote(edge_c.at[k, 1], got_c.at[k, 0], k, 3, at(dc=1))]
        for e in range(4):
            copies.append(remote(edge_e.at[k, e], got_e.at[k, 3 - e], k, 4 + e, at(da=1 if e >= 2 else -1, dc=1 if e % 2 else -1)))
        for copy in copies:
            copy.start()
        return copies

    def second_phase(k, copies):
        for copy in copies:
            copy.wait()
        z_ref[k, 0:32, :] = z_ref[k, 0:32, :] + got_a[k, 0] * low_ax
        z_ref[k, 224:256, :] = z_ref[k, 224:256, :] + got_a[k, 1] * high_ax
        z_ref[k, pl.ds(0, 8, stride=32), :] = z_ref[k, pl.ds(0, 8, stride=32), :] + got_c[k, 0]
        z_ref[k, pl.ds(31, 8, stride=32), :] = z_ref[k, pl.ds(31, 8, stride=32), :] + got_c[k, 1]
        for e, at_row in enumerate((0, 31, 224, 255)):
            z_ref[k, at_row:at_row + 1, :] = z_ref[k, at_row:at_row + 1, :] + got_e[k, e] * (low_ax if e < 2 else high_ax)
        z = z_ref[k]
        faces = exact_dot(ends_ref[...], z, ((1,), (1,)))
        edge_g[k, 0] = faces[0:1]
        edge_g[k, 1] = faces[1:2]
        copies = [remote(edge_g.at[k, 0], got_g.at[k, 1], k, 8, at(dg=-1)),
                  remote(edge_g.at[k, 1], got_g.at[k, 0], k, 9, at(dg=1))]
        for copy in copies:
            copy.start()
        for copy in copies:
            copy.wait()
        pair_ref[0:1, :] = got_g[k, 0] * low_gap
        pair_ref[1:2, :] = got_g[k, 1] * high_gap
        v_ref[k] = (z + exact_dot(pair_ref[...], ends_ref[...], ((0,), (0,)))) * wall

    rhs = quad * 0.25 * (4.0 * w_ref[...] + force_ref[...])
    pl.semaphore_wait(barrier, len(peers))
    moves = [at(da=1), at(da=-1), at(dc=1), at(dc=-1), at(dg=1), at(dg=-1)]
    moving = [pltpu.make_async_remote_copy(src_ref=buf_ref.at[r], dst_ref=arr_ref.at[r], send_sem=mig_send.at[r], recv_sem=mig_recv.at[r],
                                           device_id=place, device_id_type=MESH) for r, place in enumerate(moves)]
    copies = first_phase(0, rhs)
    for copy in moving:
        copy.start()

    w = w_ref[...]
    slopes = exact_dot(left_ref[...], w)
    slope_g = exact_dot(w, right_ref[...])
    squares = 1.0 + slopes[0:256] * slopes[0:256] + slopes[256:512] * slopes[256:512] + slope_g * slope_g
    stiff = quad * 0.25 * (0.05 + yield_ref[...] / jnp.sqrt(squares))
    second_phase(0, copies)

    def total(x):
        return jnp.sum(x, axis=0, keepdims=True)

    sums = []
    for k in range(3):
        v = v_ref[k]
        slopes = exact_dot(left_ref[...], v)
        slope_g = exact_dot(v, right_ref[...])
        first, second = slopes[0:256], slopes[256:512]
        sums.append(total(share * v * v))
        if k < 2:
            flux_g = stiff * slope_g
            flux = jnp.concatenate([stiff * first, stiff * second], axis=0)
            image = quad * v + exact_dot(left_t_ref[...], flux) + exact_dot(flux_g, right_t_ref[...])
            copies = first_phase(k + 1, image)
        sums.append(total(quad * v * v + stiff * (first * first + second * second + slope_g * slope_g)))
        if k < 2:
            second_phase(k + 1, copies)

    sub = lax.broadcasted_iota(jnp.int32, (8, 128), 0)
    part = lax.broadcasted_iota(jnp.int32, (8, 128), 1) // 16
    rows = jnp.zeros((8, 128), jnp.float32)
    for m, value in enumerate(sums):
        rows = jnp.where(sub == m, jnp.broadcast_to(value, (8, 128)), rows)
    for shift in (64, 32, 16):
        rows = rows + pltpu.roll(rows, shift, 1)
    line = jnp.sum(jnp.where(sub == part, rows, 0.0), axis=0, keepdims=True)
    slot = 0
    for stage, (name, count) in enumerate((("circ", n_circ), ("ax", n_ax), ("gap", n_gap))):
        sum_ref[stage] = line
        copies = []
        for o in range(1, count):
            place = {"circ": at(dc=o), "ax": at(da=o), "gap": at(dg=o)}[name]
            copies.append(pltpu.make_async_remote_copy(src_ref=sum_ref.at[stage], dst_ref=got_sum.at[slot], send_sem=sum_send.at[slot],
                                                       recv_sem=sum_recv.at[slot], device_id=place, device_id_type=MESH))
            slot += 1
        for copy in copies:
            copy.start()
        for copy in copies:
            copy.wait()
        for o in range(1, count):
            line = line + got_sum[slot - o]
    m = jnp.sum(jnp.where(sub == part, jnp.broadcast_to(line, (8, 128)), 0.0), axis=1, keepdims=True)
    m0, m1, m2, m3, m4, m5 = [m[i:i + 1, :] for i in range(6)]
    scale = m0 / m1
    m1 = m1 * scale
    m2 = m2 * scale * scale
    m3 = m3 * scale * scale * scale
    m4 = m4 * scale * scale * scale * scale
    m5 = m5 * scale * scale * scale * scale * scale

    def ratio(a, b):
        return jnp.where((a > 0.0) & (b > 0.0), a / b, 0.0)

    a0 = m0 / m1
    rr1 = a0 * a0 * m2 - m0
    e = 1.0 + rr1 / m0
    p1 = e * e * m1 - 2.0 * e * a0 * m2 + a0 * a0 * m3
    a1 = ratio(rr1, p1)
    c1 = a0 + a1 * e
    c2 = a0 * a1
    rr2 = m0 - 2.0 * c1 * m1 + (c1 * c1 + 2.0 * c2) * m2 - 2.0 * c1 * c2 * m3 + c2 * c2 * m4
    ra2 = m1 - 2.0 * c1 * m2 + (c1 * c1 + 2.0 * c2) * m3 - 2.0 * c1 * c2 * m4 + c2 * c2 * m5
    b1 = ratio(rr2, rr1)
    a2 = ratio(rr2, ra2 - b1 * ratio(rr2, a1))
    x0 = scale * (a0 + a1 * e + a2 * (1.0 + b1 * e))
    x1 = scale * scale * (-(c2 + a2 * (c1 + b1 * a0)))
    x2 = scale * scale * scale * (a2 * c2)
    out_ref[...] = x0 * v_ref[0] + x1 * v_ref[1] + x2 * v_ref[2]
    for copy in moving:
        copy.wait()

def flow(sizes, w, yld, force, buf):
    consts = field_consts()
    vm = lambda *s: pltpu.VMEM(s, jnp.float32)
    return pl.pallas_call(
        functools.partial(flow_kernel, sizes),
        out_shape=(jax.ShapeDtypeStruct((256, 128), jnp.float32), jax.ShapeDtypeStruct(buf.shape, jnp.float32)),
        in_specs=[pl.BlockSpec(memory_space=pltpu.VMEM)] * (3 + len(consts)) + [pl.BlockSpec(memory_space=pl.ANY)],
        out_specs=(pl.BlockSpec(memory_space=pltpu.VMEM), pl.BlockSpec(memory_space=pl.ANY)),
        scratch_shapes=[vm(3, 256, 128), vm(3, 256, 128), vm(3, 256, 128), vm(3, 2, 8, 128), vm(3, 4, 1, 128), vm(3, 2, 1, 256),
                        vm(3, 2, 32, 128), vm(3, 2, 8, 128), vm(3, 4, 1, 128), vm(3, 2, 1, 256), vm(8, 256), vm(3, 1, 128), vm(25, 1, 128),
                        pltpu.SemaphoreType.DMA((3, 10)), pltpu.SemaphoreType.DMA((3, 10)), pltpu.SemaphoreType.DMA((25,)),
                        pltpu.SemaphoreType.DMA((25,)), pltpu.SemaphoreType.DMA((6,)), pltpu.SemaphoreType.DMA((6,))],
        compiler_params=pltpu.CompilerParams(collective_id=0, has_side_effects=True),
        name="flow",
    )(w, yld, force, *consts, buf)


def solution(mesh):
    sizes = (mesh.shape["ax"], mesh.shape["circ"], mesh.shape["gap"])

    def shards(w_old, yield_stress, force, xi, vel, mom, el, new, slots, counts):
        flat = lambda t: t.reshape(256, 128)
        xi, vel, mom = [t.reshape(3, 8192) for t in (xi, vel, mom)]
        buf, dep = pack(xi, vel, mom, new.reshape(1, 8192), slots.reshape(6, 1024), counts.reshape(6))
        w, arr = flow(sizes, flat(w_old), flat(yield_stress), flat(force), buf)
        ax, gap = lax.axis_index("ax"), lax.axis_index("gap")
        ok = jnp.stack([ax > 0, ax < sizes[0] - 1, ax >= 0, ax >= 0, gap > 0, gap < sizes[2] - 1]).astype(jnp.float32)
        w_new, kept, arrived = settle(ok, w, xi, vel, mom, el.reshape(1, 8192), dep, arr)
        return w_new.reshape(w_old.shape), kept[None, None, None], arrived[None, None, None]

    spec = lambda n: P("ax", "circ", "gap", *([None] * n))
    return jax.shard_map(
        shards,
        mesh=mesh,
        in_specs=(spec(0), spec(0), spec(0), spec(2), spec(2), spec(2), spec(1), spec(1), spec(2), spec(1)),
        out_specs=(spec(0), spec(2), spec(3)),
        check_vma=False,
    )
```

```python
import functools
import jax, jax.numpy as jnp, numpy as np
from jax import lax
from jax.experimental import pallas as pl
from jax.experimental.pallas import tpu as pltpu
from jax.sharding import PartitionSpec as P

MESH = pl.DeviceIdType.MESH
GLL_NODES = np.array([-1.0,-0.8717401485096066,-0.5917001814331423,-0.2092992179024789,0.2092992179024789,0.5917001814331423,0.8717401485096066,1.0])
GLL_WEIGHTS = np.array([0.03571428571428571,0.2107042271435061,0.3411226924835044,0.4124587946587038,0.4124587946587038,0.3411226924835044,0.2107042271435061,0.03571428571428571])

def bary_weights():
    eye = np.eye(8, dtype=bool)
    diff = np.where(eye, 1.0, GLL_NODES[:, None] - GLL_NODES[None, :])
    return 1.0 / np.prod(diff, axis=1)

def pick(rows, lanes):
    return jnp.take_along_axis(rows, lanes, axis=1, mode="promise_in_bounds")

def pick_row(rows, at):
    return jnp.take_along_axis(rows, at, axis=0, mode="promise_in_bounds")

def leaving_row(fields, slots_ref, count, row, buf_ref):
    lane = lax.broadcasted_iota(jnp.int32, (8, 128), 1)
    for s in range(8):
        slot = jnp.broadcast_to(slots_ref[row, s:s + 1, :], (8, 128))
        block = lax.shift_right_logical(slot, 10)
        inner = lax.bitwise_and(lax.shift_right_logical(slot, 7), 7)
        within = lax.bitwise_and(slot, 127)
        live = (lane + s * 128 < count).astype(jnp.float32)
        for f, field in enumerate(fields):
            found = None
            for b in range(8):
                got = pick(field(b), within)
                found = got if found is None else jnp.where(block == b, got, found)
            found = pick_row(found, inner) * live
            buf_ref[row, f, s:s + 1, :] = found[0:1]
        buf_ref[row, 10, s:s + 1, :] = live[0:1]

def departed_flags(slots_ref, counts_ref):
    sub64 = lax.broadcasted_iota(jnp.int32, (64, 128), 0)
    sub128 = lax.broadcasted_iota(jnp.int32, (128, 128), 0)
    lanes = lax.broadcasted_iota(jnp.int32, (1, 128), 1)

    def one(row, total):
        count = counts_ref[row]
        blocks, places = [], []
        for s in range(8):
            slot = slots_ref[row, s:s + 1, :]
            block = jnp.where(lanes + s * 128 < count, lax.shift_right_logical(slot, 7), 64)
            within = lax.bitwise_and(slot, 127)
            blocks.append(jnp.where(sub64 == block, 1.0, 0.0).astype(jnp.bfloat16))
            places.append(jnp.where(sub128 == within, 1.0, 0.0).astype(jnp.bfloat16))
        return total + lax.dot_general(jnp.concatenate(blocks, 1), jnp.concatenate(places, 1), (((1,), (1,)), ((), ())), preferred_element_type=jnp.float32)

    return lax.fori_loop(0, 6, one, jnp.zeros((64, 128), jnp.float32))

def pack_kernel(counts_ref, xi_ref, vel_ref, mom_ref, new_ref, slots_ref, buf_ref, dep_ref, id_ref):
    id_ref[...] = new_ref[...].astype(jnp.float32)
    fields = [lambda b, ref=ref, d=d: ref[d, b * 8:b * 8 + 8, :] for ref in (xi_ref, vel_ref, mom_ref) for d in range(3)]
    fields.append(lambda b: id_ref[b * 8:b * 8 + 8, :])

    @pl.loop(0, 6)
    def _(row):
        leaving_row(fields, slots_ref, counts_ref[row], row, buf_ref)

    dep_ref[...] = departed_flags(slots_ref, counts_ref)

def pack(xi, vel, mom, new, slots, counts):
    return pl.pallas_call(
        pack_kernel,
        out_shape=(jax.ShapeDtypeStruct((6, 11, 8, 128), jnp.float32), jax.ShapeDtypeStruct((64, 128), jnp.float32)),
        in_specs=[pl.BlockSpec(memory_space=pltpu.SMEM)] + [pl.BlockSpec(memory_space=pltpu.VMEM)] * 5,
        out_specs=(pl.BlockSpec(memory_space=pltpu.VMEM),) * 2,
        scratch_shapes=[pltpu.VMEM((64, 128), jnp.float32)],
        name="pack",
    )(counts, xi, vel, mom, new, slots)

def ladder(x):
    d = [x - np.float32(n) for n in GLL_NODES]
    pre = [None] * 8
    suf = [None] * 8
    pre[1] = d[0]
    for k in range(2, 8):
        pre[k] = pre[k - 1] * d[k - 1]
    suf[6] = d[7]
    for k in range(5, -1, -1):
        suf[k] = suf[k + 1] * d[k + 1]
    return [suf[0]] + [pre[k] * suf[k] for k in range(1, 7)] + [pre[7]]

def settle_kernel(gate_ref, w_ref, bary_ref, xi_ref, vel_ref, mom_ref, el_ref, dep_ref, arr_ref, w_out, kept_ref, arrived_ref, table_ref, basis_ref, fluid_ref):
    w = w_ref[...]
    w_out[...] = w
    w = w * bary_ref[...]
    high = w.astype(jnp.bfloat16)
    low = (w - high.astype(jnp.float32)).astype(jnp.bfloat16)
    table_ref[:, 0:128] = high
    table_ref[:, 128:256] = low
    table_ref[:, 256:384] = high
    lane_g = lax.broadcasted_iota(jnp.int32, (128, 128), 0) // 8

    def sample(ids, x1, x2, x3):
        for k, value in enumerate(ladder(x1)):
            basis_ref[0, k * 8:k * 8 + 8, :] = value
        for k, value in enumerate(ladder(x2)):
            basis_ref[1, k * 8:k * 8 + 8, :] = value
        for k, value in enumerate(ladder(x3)):
            rounded = value.astype(jnp.bfloat16).astype(jnp.float32)
            basis_ref[2, k * 8:k * 8 + 8, :] = rounded
            basis_ref[3, k * 8:k * 8 + 8, :] = value - rounded
        circ = lax.shift_right_logical(ids, 4)
        radial = lax.bitwise_and(ids, 15)
        for q in range(4):
            right, weights = [], []
            for s in (2 * q, 2 * q + 1):
                mine = lane_g == jnp.broadcast_to(radial[s:s + 1], (128, 128))
                b_high = jnp.where(mine, jnp.concatenate([basis_ref[2, pl.ds(s, 8, stride=8), :]] * 16, axis=0), 0.0).astype(jnp.bfloat16)
                b_low = jnp.where(mine, jnp.concatenate([basis_ref[3, pl.ds(s, 8, stride=8), :]] * 16, axis=0), 0.0).astype(jnp.bfloat16)
                right.append(jnp.concatenate([b_high, b_high, b_low], axis=0))
                second = basis_ref[1, pl.ds(s, 8, stride=8), :]
                cc = jnp.broadcast_to(circ[s:s + 1], (8, 128))
                weights.append([jnp.where(cc == c, second, 0.0) for c in range(4)])
            values = jnp.dot(table_ref[...], jnp.concatenate(right, axis=1), preferred_element_type=jnp.float32)
            for h, s in enumerate((2 * q, 2 * q + 1)):
                total = None
                for i in range(8):
                    line = None
                    for c in range(4):
                        term = values[i * 32 + c * 8:i * 32 + c * 8 + 8, h * 128:h * 128 + 128] * weights[h][c]
                        line = term if line is None else line + term
                    line = line * jnp.broadcast_to(basis_ref[0, i * 8 + s:i * 8 + s + 1, :], (8, 128))
                    total = line if total is None else total + line
                fluid_ref[s:s + 1, :] = jnp.sum(total, axis=0, keepdims=True)
        return fluid_ref[...]

    def update(xi, vel, fluid):
        axial = vel[0] + 0.4 * (fluid - vel[0])
        circ = vel[1] * (1.0 - 0.4)
        radial = vel[2] * (1.0 - 0.4)
        return [xi[0] + 0.25 * axial, xi[1] + 0.25 * circ, xi[2] + 1.0 * radial, axial, circ, radial]

    @pl.loop(0, 8)
    def _(block):
        rows = pl.ds(pl.multiple_of(block * 8, 8), 8)
        xi = [xi_ref[d, rows, :] for d in range(3)]
        fluid = sample(el_ref[rows, :], *xi)
        stay = 1.0 - dep_ref[rows, :]
        for at, value in enumerate(update(xi, [vel_ref[d, rows, :] for d in range(3)], fluid)):
            kept_ref[at, rows, :] = value * stay
        for d in range(3):
            kept_ref[6 + d, rows, :] = mom_ref[d, rows, :] * stay

    @pl.loop(0, 6)
    def _(row):
        state = [arr_ref[row, d] for d in range(11)]
        fluid = sample(state[9].astype(jnp.int32), *state[0:3])
        live = state[10] * gate_ref[row]
        for at, value in enumerate(update(state[0:3], state[3:6], fluid) + state[6:9]):
            arrived_ref[row, at] = value * live

def settle(gate, w, xi, vel, mom, el, dep, arr):
    b = bary_weights()
    rows = (b[:, None, None] * np.ones((1, 4, 1)) * b[None, None, :]).reshape(256, 1)
    bary = np.ascontiguousarray(rows * np.tile(b, 16)[None, :], dtype=np.float32)
    return pl.pallas_call(
        settle_kernel,
        out_shape=(jax.ShapeDtypeStruct((256, 128), jnp.float32), jax.ShapeDtypeStruct((9, 64, 128), jnp.float32), jax.ShapeDtypeStruct((6, 9, 8, 128), jnp.float32)),
        in_specs=[pl.BlockSpec(memory_space=pltpu.SMEM)] + [pl.BlockSpec(memory_space=pltpu.VMEM)] * 8,
        out_specs=(pl.BlockSpec(memory_space=pltpu.VMEM),) * 3,
        scratch_shapes=[pltpu.VMEM((256, 384), jnp.bfloat16), pltpu.VMEM((4, 64, 128), jnp.float32), pltpu.VMEM((8, 128), jnp.float32)],
        name="settle",
    )(gate, w, bary, xi, vel, mom, el, dep, arr)

def diff_table():
    b = bary_weights()
    eye = np.eye(8, dtype=bool)
    diff = np.where(eye, 1.0, GLL_NODES[:, None] - GLL_NODES[None, :])
    off = np.where(eye, 0.0, b[None, :] / b[:, None] / diff)
    return (off - np.eye(8) * np.sum(off, axis=1)[:, None]).astype(np.float32)

def pieces(a, count=2):
    parts = []
    rest = a.astype(np.float32)
    for _ in range(count):
        part = rest.astype(jnp.bfloat16)
        parts.append(part)
        rest = rest - part.astype(np.float32)
    return parts

def field_consts():
    d = diff_table()
    eye = np.eye(16, dtype=np.float32)

    def left(m):
        h, l = pieces(np.kron(eye, m))
        return np.block([[h, h], [l, l]])

    def right(m):
        h, l = pieces(4.0 * np.kron(eye, m))
        return np.block([[h, l], [h, l]])

    w8 = GLL_WEIGHTS.astype(np.float32)
    half = np.where((np.arange(8) == 0) | (np.arange(8) == 7), 0.5, 1.0)
    r = np.arange(32)[:, None] + np.zeros((1, 128))
    c = np.arange(128)[None, :] + np.zeros((32, 1))
    small = np.stack([np.tile(w8, 4)[:, None] * np.tile(w8, 16)[None, :], np.tile(half, 4)[:, None] * np.tile(half, 16)[None, :],
                      (r % 8 == 0) & (r > 0), (r % 8 == 7) & (r < 31), (c % 8 == 0) & (c > 0), (c % 8 == 7) & (c < 127)]).astype(np.float32)
    ends = np.zeros((8, 384), np.float32)
    for piece in range(3):
        ends[0, piece * 128] = 1.0
        ends[1, piece * 128 + 127] = 1.0
    spread = np.zeros((32, 128), np.float32)
    for piece in range(3):
        spread[piece * 8, 0] = 1.0
        spread[piece * 8 + 1, 127] = 1.0
    bf = lambda t: np.ascontiguousarray(t).astype(jnp.bfloat16)
    return [bf(left(d)), bf(left(d.T)), bf(right(d.T)), bf(right(d)), small, bf(ends), bf(spread)]

def halves(x):
    high = x.astype(jnp.bfloat16)
    return high, (x - high.astype(jnp.float32)).astype(jnp.bfloat16)

def thirds(x):
    high, rest = x.astype(jnp.bfloat16), None
    rest = x - high.astype(jnp.float32)
    mid = rest.astype(jnp.bfloat16)
    return high, mid, (rest - mid.astype(jnp.float32)).astype(jnp.bfloat16)

def mix(a, b, dims=((1,), (0,))):
    return lax.dot_general(a, b, (dims, ((), ())), preferred_element_type=jnp.float32)

def along_circ(x, left):
    x = jnp.concatenate([x[0:128], x[128:256]], axis=1)
    y = mix(left, jnp.concatenate(halves(x), axis=0))
    y = y[0:128] + y[128:256]
    return jnp.concatenate([y[:, 0:128], y[:, 128:256]], axis=0)

def along_gap(x, right):
    y = mix(jnp.concatenate(halves(x), axis=1), right)
    return y[:, 0:128] + y[:, 128:256]

def along_ax(x, d):
    x = [x[i * 32:i * 32 + 32] for i in range(8)]
    even = [x[j] + x[7 - j] for j in range(4)]
    odd = [x[j] - x[7 - j] for j in range(4)]
    out = [None] * 8
    for i in range(4):
        a = b = None
        for j in range(4):
            p = np.float32(0.5 * (float(d[i, j]) - float(d[i, 7 - j]))) * odd[j]
            q = np.float32(0.5 * (float(d[i, j]) + float(d[i, 7 - j]))) * even[j]
            a = p if a is None else a + p
            b = q if b is None else b + q
        out[i] = a + b
        out[7 - i] = a - b
    return jnp.concatenate(out, axis=0)

def flow_kernel(sizes, w_ref, yield_ref, force_ref, lc_ref, lct_ref, rg_ref, rgt_ref, small_ref, ends_ref, spread_ref, buf_ref,
                out_ref, arr_ref, v_ref, f_ref, z_ref, quad_ref, stiff_ref, edge_c, edge_e, edge_g, got_a, got_c, got_e, got_g, pair_ref, sum_ref, got_sum,
                send_sem, recv_sem, sum_send, sum_recv, mig_send, mig_recv):
    n_ax, n_circ, n_gap = sizes
    d8 = diff_table()
    ax, circ, gap = lax.axis_index("ax"), lax.axis_index("circ"), lax.axis_index("gap")

    def at(da=0, dc=0, dg=0):
        place = {}
        if da:
            place["ax"] = lax.rem(ax + (da + n_ax), n_ax)
        if dc:
            place["circ"] = lax.rem(circ + (dc + n_circ), n_circ)
        if dg:
            place["gap"] = lax.rem(gap + (dg + n_gap), n_gap)
        return place

    peers = [at(da=o) for o in range(1, n_ax)] + [at(dc=o) for o in range(1, n_circ)] + [at(dg=o) for o in range(1, n_gap)]
    peers += [at(da=a, dc=c) for a in (-1, 1) for c in (-1, 1)]
    barrier = pltpu.get_barrier_semaphore()
    for peer in peers:
        pl.semaphore_signal(barrier, inc=1, device_id=peer, device_id_type=MESH)

    weights = GLL_WEIGHTS.astype(np.float32)
    quad = jnp.concatenate([small_ref[0] * weights[i] for i in range(8)], axis=0)
    quad_ref[...] = quad
    col = lax.broadcasted_iota(jnp.int32, (32, 128), 1)
    at_wall = ((col == 0) & (gap == 0)) | ((col == 127) & (gap == n_gap - 1))
    wall = jnp.where(at_wall, 0.0, 1.0)
    share = small_ref[1] * jnp.where(at_wall, 2.0, 1.0)
    low_ax = jnp.where(ax == 0, 0.0, 1.0)
    high_ax = jnp.where(ax == n_ax - 1, 0.0, 1.0)
    low_gap = jnp.where(gap == 0, 0.0, 1.0)
    high_gap = jnp.where(gap == n_gap - 1, 0.0, 1.0)
    ax_share = [jnp.where(ax == 0, 1.0, 0.5)] + [1.0] * 6 + [jnp.where(ax == n_ax - 1, 1.0, 0.5)]
    pair_ref[...] = jnp.zeros((8, 256), jnp.float32)

    def every(tile):
        return jnp.concatenate([tile] * 8, axis=0)

    def gather_inner(f):
        f = f + every(small_ref[2]) * pltpu.roll(f, 1, 0) + every(small_ref[3]) * pltpu.roll(f, 255, 0)
        return f + every(small_ref[4]) * pltpu.roll(f, 1, 1) + every(small_ref[5]) * pltpu.roll(f, 127, 1)

    def remote(src, dst, k, t, place):
        return pltpu.make_async_remote_copy(src_ref=src, dst_ref=dst, send_sem=send_sem.at[k, t], recv_sem=recv_sem.at[k, t],
                                            device_id=place, device_id_type=MESH)

    def stage(k, f):
        f = gather_inner(f)
        f_ref[k] = f
        z_ref[k] = f
        edge_c[k, 0] = f_ref[k, pl.ds(0, 8, stride=32), :]
        edge_c[k, 1] = f_ref[k, pl.ds(31, 8, stride=32), :]
        for e, at_row in enumerate((0, 31, 224, 255)):
            edge_e[k, e] = f_ref[k, at_row:at_row + 1, :]

    def first_phase(k):
        copies = [remote(edge_e.at[k, e], got_e.at[k, 3 - e], k, 4 + e, at(da=1 if e >= 2 else -1, dc=1 if e % 2 else -1)) for e in range(4)]
        copies += [remote(edge_c.at[k, 0], got_c.at[k, 1], k, 2, at(dc=-1)),
                   remote(edge_c.at[k, 1], got_c.at[k, 0], k, 3, at(dc=1)),
                   remote(f_ref.at[k, 0:32], got_a.at[k, 1], k, 0, at(da=-1)),
                   remote(f_ref.at[k, 224:256], got_a.at[k, 0], k, 1, at(da=1))]
        for copy in copies:
            copy.start()
        return copies

    def second_phase(k, copies):
        for copy in copies:
            copy.wait()
        z_ref[k, 0:32, :] = z_ref[k, 0:32, :] + got_a[k, 0] * low_ax
        z_ref[k, 224:256, :] = z_ref[k, 224:256, :] + got_a[k, 1] * high_ax
        z_ref[k, pl.ds(0, 8, stride=32), :] = z_ref[k, pl.ds(0, 8, stride=32), :] + got_c[k, 0]
        z_ref[k, pl.ds(31, 8, stride=32), :] = z_ref[k, pl.ds(31, 8, stride=32), :] + got_c[k, 1]
        for e, at_row in enumerate((0, 31, 224, 255)):
            z_ref[k, at_row:at_row + 1, :] = z_ref[k, at_row:at_row + 1, :] + got_e[k, e] * (low_ax if e < 2 else high_ax)
        z = z_ref[k]
        faces = mix(ends_ref[...], jnp.concatenate(thirds(z), axis=1), ((1,), (1,)))
        edge_g[k, 0] = faces[0:1]
        edge_g[k, 1] = faces[1:2]
        copies = [remote(edge_g.at[k, 0], got_g.at[k, 1], k, 8, at(dg=-1)),
                  remote(edge_g.at[k, 1], got_g.at[k, 0], k, 9, at(dg=1))]
        for copy in copies:
            copy.start()
        for copy in copies:
            copy.wait()
        pair_ref[0:1, :] = got_g[k, 0] * low_gap
        pair_ref[1:2, :] = got_g[k, 1] * high_gap
        pair = pair_ref[...]
        pair = jnp.concatenate(thirds(pair) + (jnp.zeros((8, 256), jnp.bfloat16),), axis=0)
        v_ref[k] = (z_ref[k] + mix(pair, spread_ref[...], ((0,), (0,)))) * every(wall)

    stage(0, quad * 0.25 * (4.0 * w_ref[...] + force_ref[...]))
    pl.semaphore_wait(barrier, len(peers))
    moves = [at(da=1), at(da=-1), at(dc=1), at(dc=-1), at(dg=1), at(dg=-1)]
    moving = [pltpu.make_async_remote_copy(src_ref=buf_ref.at[r], dst_ref=arr_ref.at[r], send_sem=mig_send.at[r], recv_sem=mig_recv.at[r],
                                           device_id=place, device_id_type=MESH) for r, place in enumerate(moves)]
    copies = first_phase(0)
    for copy in moving:
        copy.start()

    w = w_ref[...]
    slope_a, slope_c, slope_g = along_ax(w, d8), along_circ(w, lc_ref[...]), along_gap(w, rg_ref[...])
    squares = 1.0 + slope_a * slope_a + slope_c * slope_c + slope_g * slope_g
    stiff_ref[...] = quad * 0.25 * (0.05 + yield_ref[...] / jnp.sqrt(squares))
    second_phase(0, copies)

    def total(x):
        return jnp.sum(x.reshape(32, 8, 128), axis=0)

    sums = []
    for k in range(3):
        v = v_ref[k]
        stiff = stiff_ref[...]
        slope_a, slope_c, slope_g = along_ax(v, d8), along_circ(v, lc_ref[...]), along_gap(v, rg_ref[...])
        if k < 2:
            image = quad_ref[...] * v + along_ax(stiff * slope_a, d8.T)
            image = image + along_circ(stiff * slope_c, lct_ref[...]) + along_gap(stiff * slope_g, rgt_ref[...])
            stage(k + 1, image)
            copies = first_phase(k + 1)
        square = v * v
        sums.append(total(jnp.concatenate([square[i * 32:i * 32 + 32] * (share * ax_share[i]) for i in range(8)], axis=0)))
        sums.append(total(quad_ref[...] * square + stiff * (slope_a * slope_a + slope_c * slope_c + slope_g * slope_g)))
        if k < 2:
            second_phase(k + 1, copies)

    sub = lax.broadcasted_iota(jnp.int32, (8, 128), 0)
    part = lax.broadcasted_iota(jnp.int32, (8, 128), 1) // 16
    rows = jnp.zeros((8, 128), jnp.float32)
    for m, value in enumerate(sums):
        rows = jnp.where(sub == m, jnp.broadcast_to(jnp.sum(value, axis=0, keepdims=True), (8, 128)), rows)
    for shift in (64, 32, 16):
        rows = rows + pltpu.roll(rows, shift, 1)
    line = jnp.sum(jnp.where(sub == part, rows, 0.0), axis=0, keepdims=True)
    slot = 0
    for step, (name, count) in enumerate((("circ", n_circ), ("ax", n_ax), ("gap", n_gap))):
        sum_ref[step] = line
        copies = []
        for o in range(1, count):
            place = {"circ": at(dc=o), "ax": at(da=o), "gap": at(dg=o)}[name]
            copies.append(pltpu.make_async_remote_copy(src_ref=sum_ref.at[step], dst_ref=got_sum.at[slot], send_sem=sum_send.at[slot],
                                                       recv_sem=sum_recv.at[slot], device_id=place, device_id_type=MESH))
            slot += 1
        for copy in copies:
            copy.start()
        for copy in copies:
            copy.wait_recv()
        for o in range(1, count):
            line = line + got_sum[slot - o]
        for copy in copies:
            copy.wait_send()
    m = jnp.sum(jnp.where(sub == part, jnp.broadcast_to(line, (8, 128)), 0.0), axis=1, keepdims=True)
    m0, m1, m2, m3, m4, m5 = [m[i:i + 1, :] for i in range(6)]
    scale = m0 / m1
    m1 = m1 * scale
    m2 = m2 * scale * scale
    m3 = m3 * scale * scale * scale
    m4 = m4 * scale * scale * scale * scale
    m5 = m5 * scale * scale * scale * scale * scale

    def ratio(a, b):
        return jnp.where((a > 0.0) & (b > 0.0), a / b, 0.0)

    a0 = m0 / m1
    rr1 = a0 * a0 * m2 - m0
    e = 1.0 + rr1 / m0
    p1 = e * e * m1 - 2.0 * e * a0 * m2 + a0 * a0 * m3
    a1 = ratio(rr1, p1)
    c1 = a0 + a1 * e
    c2 = a0 * a1
    rr2 = m0 - 2.0 * c1 * m1 + (c1 * c1 + 2.0 * c2) * m2 - 2.0 * c1 * c2 * m3 + c2 * c2 * m4
    ra2 = m1 - 2.0 * c1 * m2 + (c1 * c1 + 2.0 * c2) * m3 - 2.0 * c1 * c2 * m4 + c2 * c2 * m5
    b1 = ratio(rr2, rr1)
    a2 = ratio(rr2, ra2 - b1 * ratio(rr2, a1))
    x0 = scale * (a0 + a1 * e + a2 * (1.0 + b1 * e))
    x1 = scale * scale * (-(c2 + a2 * (c1 + b1 * a0)))
    x2 = scale * scale * scale * (a2 * c2)
    out_ref[...] = x0 * v_ref[0] + x1 * v_ref[1] + x2 * v_ref[2]
    for copy in moving:
        copy.wait()

def flow(sizes, w, yld, force, buf):
    consts = field_consts()
    vm = lambda *s: pltpu.VMEM(s, jnp.float32)
    sums = sum(sizes) - 3
    return pl.pallas_call(
        functools.partial(flow_kernel, sizes),
        out_shape=(jax.ShapeDtypeStruct((256, 128), jnp.float32), jax.ShapeDtypeStruct(buf.shape, jnp.float32)),
        in_specs=[pl.BlockSpec(memory_space=pltpu.VMEM)] * (3 + len(consts)) + [pl.BlockSpec(memory_space=pl.ANY)],
        out_specs=(pl.BlockSpec(memory_space=pltpu.VMEM), pl.BlockSpec(memory_space=pl.ANY)),
        scratch_shapes=[vm(3, 256, 128), vm(3, 256, 128), vm(3, 256, 128), vm(256, 128), vm(256, 128), vm(3, 2, 8, 128), vm(3, 4, 1, 128), vm(3, 2, 1, 256),
                        vm(3, 2, 32, 128), vm(3, 2, 8, 128), vm(3, 4, 1, 128), vm(3, 2, 1, 256), vm(8, 256), vm(3, 1, 128), vm(sums, 1, 128),
                        pltpu.SemaphoreType.DMA((3, 10)), pltpu.SemaphoreType.DMA((3, 10)), pltpu.SemaphoreType.DMA((sums,)),
                        pltpu.SemaphoreType.DMA((sums,)), pltpu.SemaphoreType.DMA((6,)), pltpu.SemaphoreType.DMA((6,))],
        compiler_params=pltpu.CompilerParams(collective_id=0, has_side_effects=True),
        name="flow",
    )(w, yld, force, *consts, buf)

def solution(mesh):
    sizes = (mesh.shape["ax"], mesh.shape["circ"], mesh.shape["gap"])

    def shards(w_old, yield_stress, force, xi, vel, mom, el, new, slots, counts):
        flat = lambda t: t.reshape(256, 128)
        xi, vel, mom = [t.reshape(3, 64, 128) for t in (xi, vel, mom)]
        buf, dep = pack(xi, vel, mom, new.reshape(64, 128), slots.reshape(6, 8, 128), counts.reshape(6))
        w, arr = flow(sizes, flat(w_old), flat(yield_stress), flat(force), buf)
        ax, gap = lax.axis_index("ax"), lax.axis_index("gap")
        ok = jnp.stack([ax > 0, ax < sizes[0] - 1, ax >= 0, ax >= 0, gap > 0, gap < sizes[2] - 1]).astype(jnp.float32)
        w_new, kept, arrived = settle(ok, w, xi, vel, mom, el.reshape(64, 128), dep, arr)
        return w_new.reshape(w_old.shape), kept.reshape(1, 1, 1, 9, 8192), arrived.reshape(1, 1, 1, 6, 9, 1024)

    spec = lambda n: P("ax", "circ", "gap", *([None] * n))
    return jax.shard_map(
        shards,
        mesh=mesh,
        in_specs=(spec(0), spec(0), spec(0), spec(2), spec(2), spec(2), spec(1), spec(1), spec(2), spec(1)),
        out_specs=(spec(0), spec(2), spec(3)),
        check_vma=False,
    )
```

```python
import functools
import jax, jax.numpy as jnp, numpy as np
from jax import lax
from jax.experimental import pallas as pl
from jax.experimental.pallas import tpu as pltpu
from jax.sharding import PartitionSpec as P

MESH = pl.DeviceIdType.MESH
GLL_NODES = np.array([-1.0,-0.8717401485096066,-0.5917001814331423,-0.2092992179024789,0.2092992179024789,0.5917001814331423,0.8717401485096066,1.0])
GLL_WEIGHTS = np.array([0.03571428571428571,0.2107042271435061,0.3411226924835044,0.4124587946587038,0.4124587946587038,0.3411226924835044,0.2107042271435061,0.03571428571428571])

def bary_weights():
    eye = np.eye(8, dtype=bool)
    diff = np.where(eye, 1.0, GLL_NODES[:, None] - GLL_NODES[None, :])
    return 1.0 / np.prod(diff, axis=1)

def pick(rows, lanes):
    return jnp.take_along_axis(rows, lanes, axis=1, mode="promise_in_bounds")

def pick_row(rows, at):
    return jnp.take_along_axis(rows, at, axis=0, mode="promise_in_bounds")

def leaving_row(fields, slots_ref, count, row, buf_ref):
    lane = lax.broadcasted_iota(jnp.int32, (8, 128), 1)
    for s in range(8):
        slot = jnp.broadcast_to(slots_ref[row, s:s + 1, :], (8, 128))
        block = lax.shift_right_logical(slot, 10)
        inner = lax.bitwise_and(lax.shift_right_logical(slot, 7), 7)
        within = lax.bitwise_and(slot, 127)
        live = (lane + s * 128 < count).astype(jnp.float32)
        for f, field in enumerate(fields):
            found = None
            for b in range(8):
                got = pick(field(b), within)
                found = got if found is None else jnp.where(block == b, got, found)
            found = pick_row(found, inner) * live
            buf_ref[row, f, s:s + 1, :] = found[0:1]
        buf_ref[row, 10, s:s + 1, :] = live[0:1]

def departed_flags(slots_ref, counts_ref):
    sub64 = lax.broadcasted_iota(jnp.int32, (64, 128), 0)
    sub128 = lax.broadcasted_iota(jnp.int32, (128, 128), 0)
    lanes = lax.broadcasted_iota(jnp.int32, (1, 128), 1)

    def one(row, total):
        count = counts_ref[row]
        blocks, places = [], []
        for s in range(8):
            slot = slots_ref[row, s:s + 1, :]
            block = jnp.where(lanes + s * 128 < count, lax.shift_right_logical(slot, 7), 64)
            within = lax.bitwise_and(slot, 127)
            blocks.append(jnp.where(sub64 == block, 1.0, 0.0).astype(jnp.bfloat16))
            places.append(jnp.where(sub128 == within, 1.0, 0.0).astype(jnp.bfloat16))
        return total + lax.dot_general(jnp.concatenate(blocks, 1), jnp.concatenate(places, 1), (((1,), (1,)), ((), ())), preferred_element_type=jnp.float32)

    return lax.fori_loop(0, 6, one, jnp.zeros((64, 128), jnp.float32))

def ladder(x):
    d = [x - np.float32(n) for n in GLL_NODES]
    pre = [None] * 8
    suf = [None] * 8
    pre[1] = d[0]
    for k in range(2, 8):
        pre[k] = pre[k - 1] * d[k - 1]
    suf[6] = d[7]
    for k in range(5, -1, -1):
        suf[k] = suf[k + 1] * d[k + 1]
    return [suf[0]] + [pre[k] * suf[k] for k in range(1, 7)] + [pre[7]]

def settle_kernel(sizes, w_ref, bary_ref, xi_ref, vel_ref, mom_ref, el_ref, dep_ref, arr_ref, w_out, kept_ref, arrived_ref, table_ref, basis_ref, fluid_ref):
    w = w_ref[...]
    w_out[...] = w
    w = w * bary_ref[...]
    high = w.astype(jnp.bfloat16)
    low = (w - high.astype(jnp.float32)).astype(jnp.bfloat16)
    table_ref[:, 0:128] = high
    table_ref[:, 128:256] = low
    table_ref[:, 256:384] = high
    lane_g = lax.broadcasted_iota(jnp.int32, (128, 128), 0) // 8

    def sample(ids, x1, x2, x3):
        for k, value in enumerate(ladder(x1)):
            basis_ref[0, k * 8:k * 8 + 8, :] = value
        for k, value in enumerate(ladder(x2)):
            basis_ref[1, k * 8:k * 8 + 8, :] = value
        for k, value in enumerate(ladder(x3)):
            rounded = value.astype(jnp.bfloat16).astype(jnp.float32)
            basis_ref[2, k * 8:k * 8 + 8, :] = rounded
            basis_ref[3, k * 8:k * 8 + 8, :] = value - rounded
        circ = lax.shift_right_logical(ids, 4)
        radial = lax.bitwise_and(ids, 15)
        for q in range(4):
            right, weights = [], []
            for s in (2 * q, 2 * q + 1):
                mine = lane_g == jnp.broadcast_to(radial[s:s + 1], (128, 128))
                b_high = jnp.where(mine, jnp.concatenate([basis_ref[2, pl.ds(s, 8, stride=8), :]] * 16, axis=0), 0.0).astype(jnp.bfloat16)
                b_low = jnp.where(mine, jnp.concatenate([basis_ref[3, pl.ds(s, 8, stride=8), :]] * 16, axis=0), 0.0).astype(jnp.bfloat16)
                right.append(jnp.concatenate([b_high, b_high, b_low], axis=0))
                second = basis_ref[1, pl.ds(s, 8, stride=8), :]
                cc = jnp.broadcast_to(circ[s:s + 1], (8, 128))
                weights.append([jnp.where(cc == c, second, 0.0) for c in range(4)])
            values = jnp.dot(table_ref[...], jnp.concatenate(right, axis=1), preferred_element_type=jnp.float32)
            for h, s in enumerate((2 * q, 2 * q + 1)):
                total = None
                for i in range(8):
                    line = None
                    for c in range(4):
                        term = values[i * 32 + c * 8:i * 32 + c * 8 + 8, h * 128:h * 128 + 128] * weights[h][c]
                        line = term if line is None else line + term
                    line = line * jnp.broadcast_to(basis_ref[0, i * 8 + s:i * 8 + s + 1, :], (8, 128))
                    total = line if total is None else total + line
                fluid_ref[s:s + 1, :] = jnp.sum(total, axis=0, keepdims=True)
        return fluid_ref[...]

    def update(xi, vel, fluid):
        axial = vel[0] + 0.4 * (fluid - vel[0])
        circ = vel[1] * (1.0 - 0.4)
        radial = vel[2] * (1.0 - 0.4)
        return [xi[0] + 0.25 * axial, xi[1] + 0.25 * circ, xi[2] + 1.0 * radial, axial, circ, radial]

    @pl.loop(0, 8)
    def _(block):
        rows = pl.ds(pl.multiple_of(block * 8, 8), 8)
        xi = [xi_ref[d, rows, :] for d in range(3)]
        fluid = sample(el_ref[rows, :], *xi)
        stay = 1.0 - dep_ref[rows, :]
        for at, value in enumerate(update(xi, [vel_ref[d, rows, :] for d in range(3)], fluid)):
            kept_ref[at, rows, :] = value * stay
        for d in range(3):
            kept_ref[6 + d, rows, :] = mom_ref[d, rows, :] * stay

    ax, gap = lax.axis_index("ax"), lax.axis_index("gap")

    @pl.loop(0, 6)
    def _(row):
        absent = ((row == 0) & (ax == 0)) | ((row == 1) & (ax == sizes[0] - 1)) | ((row == 4) & (gap == 0)) | ((row == 5) & (gap == sizes[2] - 1))
        state = [arr_ref[row, d] for d in range(11)]
        fluid = sample(state[9].astype(jnp.int32), *state[0:3])
        live = state[10] * jnp.where(absent, 0.0, 1.0)
        for at, value in enumerate(update(state[0:3], state[3:6], fluid) + state[6:9]):
            arrived_ref[row, at] = value * live

def settle(sizes, w, xi, vel, mom, el, dep, arr):
    b = bary_weights()
    rows = (b[:, None, None] * np.ones((1, 4, 1)) * b[None, None, :]).reshape(256, 1)
    bary = np.ascontiguousarray(rows * np.tile(b, 16)[None, :], dtype=np.float32)
    return pl.pallas_call(
        functools.partial(settle_kernel, sizes),
        out_shape=(jax.ShapeDtypeStruct((256, 128), jnp.float32), jax.ShapeDtypeStruct((9, 64, 128), jnp.float32), jax.ShapeDtypeStruct((6, 9, 8, 128), jnp.float32)),
        in_specs=[pl.BlockSpec(memory_space=pltpu.VMEM)] * 8,
        out_specs=(pl.BlockSpec(memory_space=pltpu.VMEM),) * 3,
        scratch_shapes=[pltpu.VMEM((256, 384), jnp.bfloat16), pltpu.VMEM((4, 64, 128), jnp.float32), pltpu.VMEM((8, 128), jnp.float32)],
        name="settle",
    )(w, bary, xi, vel, mom, el, dep, arr)

def diff_table():
    b = bary_weights()
    eye = np.eye(8, dtype=bool)
    diff = np.where(eye, 1.0, GLL_NODES[:, None] - GLL_NODES[None, :])
    off = np.where(eye, 0.0, b[None, :] / b[:, None] / diff)
    return (off - np.eye(8) * np.sum(off, axis=1)[:, None]).astype(np.float32)

def pieces(a, count=2):
    parts = []
    rest = a.astype(np.float32)
    for _ in range(count):
        part = rest.astype(jnp.bfloat16)
        parts.append(part)
        rest = rest - part.astype(np.float32)
    return parts

def field_consts():
    d = diff_table()
    eye = np.eye(16, dtype=np.float32)

    def left(m):
        h, l = pieces(np.kron(eye, m))
        return np.block([[h, h], [l, l]])

    def right(m):
        h, l = pieces(4.0 * np.kron(eye, m))
        return np.block([[h, l], [h, l]])

    w8 = GLL_WEIGHTS.astype(np.float32)
    half = np.where((np.arange(8) == 0) | (np.arange(8) == 7), 0.5, 1.0)
    r = np.arange(32)[:, None] + np.zeros((1, 128))
    c = np.arange(128)[None, :] + np.zeros((32, 1))
    small = np.stack([np.tile(w8, 4)[:, None] * np.tile(w8, 16)[None, :], np.tile(half, 4)[:, None] * np.tile(half, 16)[None, :],
                      (r % 8 == 0) & (r > 0), (r % 8 == 7) & (r < 31), (c % 8 == 0) & (c > 0), (c % 8 == 7) & (c < 127)]).astype(np.float32)
    ends = np.zeros((8, 384), np.float32)
    for piece in range(3):
        ends[0, piece * 128] = 1.0
        ends[1, piece * 128 + 127] = 1.0
    spread = np.zeros((32, 128), np.float32)
    for piece in range(3):
        spread[piece * 8, 0] = 1.0
        spread[piece * 8 + 1, 127] = 1.0
    bf = lambda t: np.ascontiguousarray(t).astype(jnp.bfloat16)
    return [bf(left(d)), bf(left(d.T)), bf(right(d.T)), bf(right(d)), small, bf(ends), bf(spread)]

def halves(x):
    high = x.astype(jnp.bfloat16)
    return high, (x - high.astype(jnp.float32)).astype(jnp.bfloat16)

def thirds(x):
    high, rest = x.astype(jnp.bfloat16), None
    rest = x - high.astype(jnp.float32)
    mid = rest.astype(jnp.bfloat16)
    return high, mid, (rest - mid.astype(jnp.float32)).astype(jnp.bfloat16)

def mix(a, b, dims=((1,), (0,))):
    return lax.dot_general(a, b, (dims, ((), ())), preferred_element_type=jnp.float32)

def along_circ(x, left):
    x = jnp.concatenate([x[0:128], x[128:256]], axis=1)
    y = mix(left, jnp.concatenate(halves(x), axis=0))
    y = y[0:128] + y[128:256]
    return jnp.concatenate([y[:, 0:128], y[:, 128:256]], axis=0)

def along_gap(x, right):
    y = mix(jnp.concatenate(halves(x), axis=1), right)
    return y[:, 0:128] + y[:, 128:256]

def along_ax(x, d):
    x = [x[i * 32:i * 32 + 32] for i in range(8)]
    even = [x[j] + x[7 - j] for j in range(4)]
    odd = [x[j] - x[7 - j] for j in range(4)]
    out = [None] * 8
    for i in range(4):
        a = b = None
        for j in range(4):
            p = np.float32(0.5 * (float(d[i, j]) - float(d[i, 7 - j]))) * odd[j]
            q = np.float32(0.5 * (float(d[i, j]) + float(d[i, 7 - j]))) * even[j]
            a = p if a is None else a + p
            b = q if b is None else b + q
        out[i] = a + b
        out[7 - i] = a - b
    return jnp.concatenate(out, axis=0)

def flow_kernel(sizes, w_ref, yield_ref, force_ref, lc_ref, lct_ref, rg_ref, rgt_ref, small_ref, ends_ref, spread_ref, counts_ref, xi_ref, vel_ref, mom_ref, new_ref, slots_ref,
                out_ref, arr_ref, dep_ref, v_ref, f_ref, z_ref, quad_ref, stiff_ref, edge_c, edge_e, edge_g, got_a, got_c, got_e, got_g, pair_ref, sum_ref, got_sum, buf_ref, id_ref,
                send_sem, recv_sem, sum_send, sum_recv, mig_send, mig_recv):
    n_ax, n_circ, n_gap = sizes
    d8 = diff_table()
    ax, circ, gap = lax.axis_index("ax"), lax.axis_index("circ"), lax.axis_index("gap")

    def at(da=0, dc=0, dg=0):
        place = {}
        if da:
            place["ax"] = lax.rem(ax + (da + n_ax), n_ax)
        if dc:
            place["circ"] = lax.rem(circ + (dc + n_circ), n_circ)
        if dg:
            place["gap"] = lax.rem(gap + (dg + n_gap), n_gap)
        return place

    around = [(a, c, g) for a in (0, -1, 1) for c in (0, -1, 1) for g in (0, -1, 1) if (a, c, g) != (0, 0, 0)]
    peers = [at(*d) for d in around] + [at(da=o) for o in range(2, n_ax - 1)] + [at(dc=o) for o in range(2, n_circ - 1)] + [at(dg=o) for o in range(2, n_gap - 1)]
    barrier = pltpu.get_barrier_semaphore()
    for peer in peers:
        pl.semaphore_signal(barrier, inc=1, device_id=peer, device_id_type=MESH)

    weights = GLL_WEIGHTS.astype(np.float32)
    quad = jnp.concatenate([small_ref[0] * weights[i] for i in range(8)], axis=0)
    quad_ref[...] = quad
    col = lax.broadcasted_iota(jnp.int32, (32, 128), 1)
    at_wall = ((col == 0) & (gap == 0)) | ((col == 127) & (gap == n_gap - 1))
    wall = jnp.where(at_wall, 0.0, 1.0)
    share = small_ref[1] * jnp.where(at_wall, 2.0, 1.0)
    low_ax = jnp.where(ax == 0, 0.0, 1.0)
    high_ax = jnp.where(ax == n_ax - 1, 0.0, 1.0)
    low_gap = jnp.where(gap == 0, 0.0, 1.0)
    high_gap = jnp.where(gap == n_gap - 1, 0.0, 1.0)
    ax_share = [jnp.where(ax == 0, 1.0, 0.5)] + [1.0] * 6 + [jnp.where(ax == n_ax - 1, 1.0, 0.5)]
    pair_ref[...] = jnp.zeros((8, 256), jnp.float32)

    def every(tile):
        return jnp.concatenate([tile] * 8, axis=0)

    def gather_inner(f):
        f = f + every(small_ref[2]) * pltpu.roll(f, 1, 0) + every(small_ref[3]) * pltpu.roll(f, 255, 0)
        return f + every(small_ref[4]) * pltpu.roll(f, 1, 1) + every(small_ref[5]) * pltpu.roll(f, 127, 1)

    def remote(src, dst, k, t, place):
        return pltpu.make_async_remote_copy(src_ref=src, dst_ref=dst, send_sem=send_sem.at[k, t], recv_sem=recv_sem.at[k, t],
                                            device_id=place, device_id_type=MESH)

    def stage(k, f):
        f = gather_inner(f)
        f_ref[k] = f
        z_ref[k] = f
        edge_c[k, 0] = f_ref[k, pl.ds(0, 8, stride=32), :]
        edge_c[k, 1] = f_ref[k, pl.ds(31, 8, stride=32), :]
        for e, at_row in enumerate((0, 31, 224, 255)):
            edge_e[k, e] = f_ref[k, at_row:at_row + 1, :]

    def send(k):
        copies = [remote(edge_e.at[k, e], got_e.at[k, 3 - e], k, 4 + e, at(da=1 if e >= 2 else -1, dc=1 if e % 2 else -1)) for e in range(4)]
        copies += [remote(edge_c.at[k, 0], got_c.at[k, 1], k, 2, at(dc=-1)),
                   remote(edge_c.at[k, 1], got_c.at[k, 0], k, 3, at(dc=1)),
                   remote(f_ref.at[k, 0:32], got_a.at[k, 1], k, 0, at(da=-1)),
                   remote(f_ref.at[k, 224:256], got_a.at[k, 0], k, 1, at(da=1))]
        for copy in copies:
            copy.start()
        faces = mix(ends_ref[...], jnp.concatenate(thirds(f_ref[k]), axis=1), ((1,), (1,)))
        for s in range(2):
            for h in range(2):
                edge_g[k, s, h] = faces[s:s + 1, h * 128:h * 128 + 128]
        later = []
        for s in range(2):
            dg = 1 if s else -1
            t = 8 + 9 * s
            for a in (-1, 1):
                for c in (-1, 1):
                    slot = 8 + (2 if a < 0 else 0) + (1 if c < 0 else 0)
                    later.append(remote(edge_g.at[k, s, 1 if a > 0 else 0], got_g.at[k, 1 - s, slot], k, t + slot - 3, at(da=a, dc=c, dg=dg)))
            for a in (-1, 1):
                slot = 7 if a < 0 else 6
                later.append(remote(edge_g.at[k, s, 1 if a > 0 else 0], got_g.at[k, 1 - s, slot], k, t + slot - 3, at(da=a, dg=dg)))
            for c in (0, -1, 1):
                slot = {0: 0, 1: 1, -1: 2}[c]
                later.append(remote(edge_g.at[k, s], got_g.at[k, 1 - s, 2 * slot:2 * slot + 2], k, t + slot, at(dc=c, dg=dg)))
        for copy in later:
            copy.start()
        return copies + later

    lane = lax.broadcasted_iota(jnp.int32, (1, 128), 1)
    place_of = lax.bitwise_and(lane, 31)

    def receive(k, copies):
        for copy in copies:
            copy.wait_recv()
        z_ref[k, 0:32, :] = z_ref[k, 0:32, :] + got_a[k, 0] * low_ax
        z_ref[k, 224:256, :] = z_ref[k, 224:256, :] + got_a[k, 1] * high_ax
        z_ref[k, pl.ds(0, 8, stride=32), :] = z_ref[k, pl.ds(0, 8, stride=32), :] + got_c[k, 0]
        z_ref[k, pl.ds(31, 8, stride=32), :] = z_ref[k, pl.ds(31, 8, stride=32), :] + got_c[k, 1]
        for e, at_row in enumerate((0, 31, 224, 255)):
            z_ref[k, at_row:at_row + 1, :] = z_ref[k, at_row:at_row + 1, :] + got_e[k, e] * (low_ax if e < 2 else high_ax)
        for s in range(2):
            def moved(slot, shift, keep):
                return jnp.where(keep, pltpu.roll(got_g[k, s, slot], shift, 1), 0.0)

            low = moved(6, 32, lane < 32) + moved(8, 1, lane == 0) + moved(9, 63, lane == 31)
            high = moved(7, 96, lane >= 96) + moved(10, 65, lane == 96) + moved(11, 127, lane == 127)
            sides = []
            for h, extra in ((0, low * low_ax), (1, high * high_ax)):
                sides.append(got_g[k, s, h] + moved(2 + h, 97, place_of == 0) + moved(4 + h, 31, place_of == 31) + extra)
            for h in range(2):
                pair_ref[s:s + 1, h * 128:h * 128 + 128] = sides[h] * (high_gap if s else low_gap)
        pair = pair_ref[...]
        pair = jnp.concatenate(thirds(pair) + (jnp.zeros((8, 256), jnp.bfloat16),), axis=0)
        v_ref[k] = (z_ref[k] + mix(pair, spread_ref[...], ((0,), (0,)))) * every(wall)

    id_ref[...] = new_ref[...].astype(jnp.float32)
    fields = [lambda b, ref=ref, d=d: ref[d, b * 8:b * 8 + 8, :] for ref in (xi_ref, vel_ref, mom_ref) for d in range(3)]
    fields.append(lambda b: id_ref[b * 8:b * 8 + 8, :])
    moves = [at(da=1), at(da=-1), at(dc=1), at(dc=-1), at(dg=1), at(dg=-1)]
    moving = [pltpu.make_async_remote_copy(src_ref=buf_ref.at[r], dst_ref=arr_ref.at[r], send_sem=mig_send.at[r], recv_sem=mig_recv.at[r],
                                           device_id=place, device_id_type=MESH) for r, place in enumerate(moves)]

    def pack_rows(first, last):
        @pl.loop(first, last)
        def _(row):
            leaving_row(fields, slots_ref, counts_ref[row], row, buf_ref)

        for copy in moving[first:last]:
            copy.start()

    stage(0, quad * 0.25 * (4.0 * w_ref[...] + force_ref[...]))
    pl.semaphore_wait(barrier, len(peers))
    copies = send(0)
    w = w_ref[...]
    slope_a, slope_c, slope_g = along_ax(w, d8), along_circ(w, lc_ref[...]), along_gap(w, rg_ref[...])
    squares = 1.0 + slope_a * slope_a + slope_c * slope_c + slope_g * slope_g
    stiff_ref[...] = quad * 0.25 * (0.05 + yield_ref[...] / jnp.sqrt(squares))
    pack_rows(0, 3)
    receive(0, copies)

    def total(x):
        return jnp.sum(x.reshape(32, 8, 128), axis=0)

    sums = []
    for k in range(3):
        v = v_ref[k]
        stiff = stiff_ref[...]
        slope_a, slope_c, slope_g = along_ax(v, d8), along_circ(v, lc_ref[...]), along_gap(v, rg_ref[...])
        if k < 2:
            image = quad_ref[...] * v + along_ax(stiff * slope_a, d8.T)
            image = image + along_circ(stiff * slope_c, lct_ref[...]) + along_gap(stiff * slope_g, rgt_ref[...])
            stage(k + 1, image)
            sent, copies = copies, send(k + 1)
        square = v * v
        sums.append(total(jnp.concatenate([square[i * 32:i * 32 + 32] * (share * ax_share[i]) for i in range(8)], axis=0)))
        sums.append(total(quad_ref[...] * square + stiff * (slope_a * slope_a + slope_c * slope_c + slope_g * slope_g)))
        if k == 0:
            pack_rows(3, 6)
        if k == 1:
            dep_ref[...] = departed_flags(slots_ref, counts_ref)
        if k < 2:
            for copy in sent:
                copy.wait_send()
            receive(k + 1, copies)

    sub = lax.broadcasted_iota(jnp.int32, (8, 128), 0)
    part = lax.broadcasted_iota(jnp.int32, (8, 128), 1) // 16
    rows = jnp.zeros((8, 128), jnp.float32)
    for m, value in enumerate(sums):
        rows = jnp.where(sub == m, jnp.broadcast_to(jnp.sum(value, axis=0, keepdims=True), (8, 128)), rows)
    for shift in (64, 32, 16):
        rows = rows + pltpu.roll(rows, shift, 1)
    line = jnp.sum(jnp.where(sub == part, rows, 0.0), axis=0, keepdims=True)
    slot = 0
    for step, (name, count) in enumerate((("circ", n_circ), ("ax", n_ax), ("gap", n_gap))):
        sum_ref[step] = line
        rounds = []
        for o in range(1, count):
            place = {"circ": at(dc=o), "ax": at(da=o), "gap": at(dg=o)}[name]
            rounds.append(pltpu.make_async_remote_copy(src_ref=sum_ref.at[step], dst_ref=got_sum.at[slot], send_sem=sum_send.at[slot],
                                                       recv_sem=sum_recv.at[slot], device_id=place, device_id_type=MESH))
            slot += 1
        for copy in rounds:
            copy.start()
        if step == 0:
            for copy in copies:
                copy.wait_send()
        for copy in rounds:
            copy.wait_recv()
        for o in range(1, count):
            line = line + got_sum[slot - o]
        for copy in rounds:
            copy.wait_send()
    m = jnp.sum(jnp.where(sub == part, jnp.broadcast_to(line, (8, 128)), 0.0), axis=1, keepdims=True)
    m0, m1, m2, m3, m4, m5 = [m[i:i + 1, :] for i in range(6)]
    scale = m0 / m1
    m1 = m1 * scale
    m2 = m2 * scale * scale
    m3 = m3 * scale * scale * scale
    m4 = m4 * scale * scale * scale * scale
    m5 = m5 * scale * scale * scale * scale * scale

    def ratio(a, b):
        return jnp.where((a > 0.0) & (b > 0.0), a / b, 0.0)

    a0 = m0 / m1
    rr1 = a0 * a0 * m2 - m0
    e = 1.0 + rr1 / m0
    p1 = e * e * m1 - 2.0 * e * a0 * m2 + a0 * a0 * m3
    a1 = ratio(rr1, p1)
    c1 = a0 + a1 * e
    c2 = a0 * a1
    rr2 = m0 - 2.0 * c1 * m1 + (c1 * c1 + 2.0 * c2) * m2 - 2.0 * c1 * c2 * m3 + c2 * c2 * m4
    ra2 = m1 - 2.0 * c1 * m2 + (c1 * c1 + 2.0 * c2) * m3 - 2.0 * c1 * c2 * m4 + c2 * c2 * m5
    b1 = ratio(rr2, rr1)
    a2 = ratio(rr2, ra2 - b1 * ratio(rr2, a1))
    x0 = scale * (a0 + a1 * e + a2 * (1.0 + b1 * e))
    x1 = scale * scale * (-(c2 + a2 * (c1 + b1 * a0)))
    x2 = scale * scale * scale * (a2 * c2)
    out_ref[...] = x0 * v_ref[0] + x1 * v_ref[1] + x2 * v_ref[2]
    for copy in moving:
        copy.wait()

def flow(sizes, w, yld, force, xi, vel, mom, new, slots, counts):
    consts = field_consts()
    vm = lambda *s: pltpu.VMEM(s, jnp.float32)
    sums = sum(sizes) - 3
    whole = pl.BlockSpec(memory_space=pltpu.VMEM)
    return pl.pallas_call(
        functools.partial(flow_kernel, sizes),
        out_shape=(jax.ShapeDtypeStruct((256, 128), jnp.float32), jax.ShapeDtypeStruct((6, 11, 8, 128), jnp.float32), jax.ShapeDtypeStruct((64, 128), jnp.float32)),
        in_specs=[whole] * (3 + len(consts)) + [pl.BlockSpec(memory_space=pltpu.SMEM)] + [whole] * 5,
        out_specs=(whole, pl.BlockSpec(memory_space=pl.ANY), whole),
        scratch_shapes=[vm(3, 256, 128), vm(3, 256, 128), vm(3, 256, 128), vm(256, 128), vm(256, 128), vm(3, 2, 8, 128), vm(3, 4, 1, 128), vm(3, 2, 2, 1, 128),
                        vm(3, 2, 32, 128), vm(3, 2, 8, 128), vm(3, 4, 1, 128), vm(3, 2, 12, 1, 128), vm(8, 256), vm(3, 1, 128), vm(sums, 1, 128),
                        vm(6, 11, 8, 128), vm(64, 128),
                        pltpu.SemaphoreType.DMA((3, 26)), pltpu.SemaphoreType.DMA((3, 26)), pltpu.SemaphoreType.DMA((sums,)),
                        pltpu.SemaphoreType.DMA((sums,)), pltpu.SemaphoreType.DMA((6,)), pltpu.SemaphoreType.DMA((6,))],
        compiler_params=pltpu.CompilerParams(collective_id=0, has_side_effects=True),
        name="flow",
    )(w, yld, force, *consts, counts, xi, vel, mom, new, slots)

def solution(mesh):
    sizes = (mesh.shape["ax"], mesh.shape["circ"], mesh.shape["gap"])

    def shards(w_old, yield_stress, force, xi, vel, mom, el, new, slots, counts):
        flat = lambda t: t.reshape(256, 128)
        xi, vel, mom = [t.reshape(3, 64, 128) for t in (xi, vel, mom)]
        w, arr, dep = flow(sizes, flat(w_old), flat(yield_stress), flat(force), xi, vel, mom, new.reshape(64, 128), slots.reshape(6, 8, 128), counts.reshape(6))
        w_new, kept, arrived = settle(sizes, w, xi, vel, mom, el.reshape(64, 128), dep, arr)
        return w_new.reshape(w_old.shape), kept.reshape(1, 1, 1, 9, 8192), arrived.reshape(1, 1, 1, 6, 9, 1024)

    spec = lambda n: P("ax", "circ", "gap", *([None] * n))
    return jax.shard_map(
        shards,
        mesh=mesh,
        in_specs=(spec(0), spec(0), spec(0), spec(2), spec(2), spec(2), spec(1), spec(1), spec(2), spec(1)),
        out_specs=(spec(0), spec(2), spec(3)),
        check_vma=False,
    )
```

```python
import functools
import jax, jax.numpy as jnp, numpy as np
from jax import lax
from jax.experimental import pallas as pl
from jax.experimental.pallas import tpu as pltpu
from jax.sharding import PartitionSpec as P

MESH = pl.DeviceIdType.MESH
GLL_NODES = np.array([-1.0,-0.8717401485096066,-0.5917001814331423,-0.2092992179024789,0.2092992179024789,0.5917001814331423,0.8717401485096066,1.0])
GLL_WEIGHTS = np.array([0.03571428571428571,0.2107042271435061,0.3411226924835044,0.4124587946587038,0.4124587946587038,0.3411226924835044,0.2107042271435061,0.03571428571428571])

def bary_weights():
    eye = np.eye(8, dtype=bool)
    diff = np.where(eye, 1.0, GLL_NODES[:, None] - GLL_NODES[None, :])
    return 1.0 / np.prod(diff, axis=1)

def pick(rows, lanes):
    return jnp.take_along_axis(rows, lanes, axis=1, mode="promise_in_bounds")

def pick_row(rows, at):
    return jnp.take_along_axis(rows, at, axis=0, mode="promise_in_bounds")

def leaving_row(fields, slots_ref, count, row, buf_ref):
    lane = lax.broadcasted_iota(jnp.int32, (8, 128), 1)
    for s in range(8):
        slot = jnp.broadcast_to(slots_ref[row, s:s + 1, :], (8, 128))
        block = lax.shift_right_logical(slot, 10)
        inner = lax.bitwise_and(lax.shift_right_logical(slot, 7), 7)
        within = lax.bitwise_and(slot, 127)
        live = (lane + s * 128 < count).astype(jnp.float32)
        for f, field in enumerate(fields):
            found = None
            for b in range(8):
                got = pick(field(b), within)
                found = got if found is None else jnp.where(block == b, got, found)
            found = pick_row(found, inner) * live
            buf_ref[row, f, s:s + 1, :] = found[0:1]
        buf_ref[row, 10, s:s + 1, :] = live[0:1]

def departed_flags(slots_ref, counts_ref):
    sub64 = lax.broadcasted_iota(jnp.int32, (64, 128), 0)
    sub128 = lax.broadcasted_iota(jnp.int32, (128, 128), 0)
    lanes = lax.broadcasted_iota(jnp.int32, (1, 128), 1)

    def one(row, total):
        count = counts_ref[row]
        blocks, places = [], []
        for s in range(8):
            slot = slots_ref[row, s:s + 1, :]
            block = jnp.where(lanes + s * 128 < count, lax.shift_right_logical(slot, 7), 64)
            within = lax.bitwise_and(slot, 127)
            blocks.append(jnp.where(sub64 == block, 1.0, 0.0).astype(jnp.bfloat16))
            places.append(jnp.where(sub128 == within, 1.0, 0.0).astype(jnp.bfloat16))
        return total + lax.dot_general(jnp.concatenate(blocks, 1), jnp.concatenate(places, 1), (((1,), (1,)), ((), ())), preferred_element_type=jnp.float32)

    return lax.fori_loop(0, 6, one, jnp.zeros((64, 128), jnp.float32))

STEP = 2

def ladder(x):
    d = [x - np.float32(n) for n in GLL_NODES]
    pre = [None] * 8
    suf = [None] * 8
    pre[1] = d[0]
    for k in range(2, 8):
        pre[k] = pre[k - 1] * d[k - 1]
    suf[6] = d[7]
    for k in range(5, -1, -1):
        suf[k] = suf[k + 1] * d[k + 1]
    return [suf[0]] + [pre[k] * suf[k] for k in range(1, 7)] + [pre[7]]

def settle_kernel(sizes, w_ref, bary_ref, xi_ref, vel_ref, mom_ref, el_ref, dep_ref, arr_ref, w_out, kept_ref, arrived_ref, table_ref, basis_ref, fluid_ref):
    w = w_ref[...]
    w_out[...] = w
    w = w * bary_ref[...]
    high = w.astype(jnp.bfloat16)
    low = (w - high.astype(jnp.float32)).astype(jnp.bfloat16)
    table_ref[:, 0:128] = high
    table_ref[:, 128:256] = low
    table_ref[:, 256:384] = high
    lane_g = lax.broadcasted_iota(jnp.int32, (128, 128), 0) // 8

    def sample(ids, x1, x2, x3, basis_ref, fluid_ref):
        for k, value in enumerate(ladder(x1)):
            basis_ref[0, k * 8:k * 8 + 8, :] = value
        for k, value in enumerate(ladder(x2)):
            basis_ref[1, k * 8:k * 8 + 8, :] = value
        for k, value in enumerate(ladder(x3)):
            rounded = value.astype(jnp.bfloat16).astype(jnp.float32)
            basis_ref[2, k * 8:k * 8 + 8, :] = rounded
            basis_ref[3, k * 8:k * 8 + 8, :] = value - rounded
        circ = lax.shift_right_logical(ids, 4)
        radial = lax.bitwise_and(ids, 15)
        for q in range(4):
            right, weights = [], []
            for s in (2 * q, 2 * q + 1):
                mine = lane_g == jnp.broadcast_to(radial[s:s + 1], (128, 128))
                b_high = jnp.where(mine, jnp.concatenate([basis_ref[2, pl.ds(s, 8, stride=8), :]] * 16, axis=0), 0.0).astype(jnp.bfloat16)
                b_low = jnp.where(mine, jnp.concatenate([basis_ref[3, pl.ds(s, 8, stride=8), :]] * 16, axis=0), 0.0).astype(jnp.bfloat16)
                right.append(jnp.concatenate([b_high, b_high, b_low], axis=0))
                second = basis_ref[1, pl.ds(s, 8, stride=8), :]
                cc = jnp.broadcast_to(circ[s:s + 1], (8, 128))
                weights.append([jnp.where(cc == c, second, 0.0) for c in range(4)])
            values = jnp.dot(table_ref[...], jnp.concatenate(right, axis=1), preferred_element_type=jnp.float32)
            for h, s in enumerate((2 * q, 2 * q + 1)):
                total = None
                for i in range(8):
                    line = None
                    for c in range(4):
                        term = values[i * 32 + c * 8:i * 32 + c * 8 + 8, h * 128:h * 128 + 128] * weights[h][c]
                        line = term if line is None else line + term
                    line = line * jnp.broadcast_to(basis_ref[0, i * 8 + s:i * 8 + s + 1, :], (8, 128))
                    total = line if total is None else total + line
                fluid_ref[s:s + 1, :] = jnp.sum(total, axis=0, keepdims=True)
        return fluid_ref[...]

    def update(xi, vel, fluid):
        axial = vel[0] + 0.4 * (fluid - vel[0])
        circ = vel[1] * (1.0 - 0.4)
        radial = vel[2] * (1.0 - 0.4)
        return [xi[0] + 0.25 * axial, xi[1] + 0.25 * circ, xi[2] + 1.0 * radial, axial, circ, radial]

    def stay_block(block, half):
        rows = pl.ds(pl.multiple_of(block * 8, 8), 8)
        xi = [xi_ref[d, rows, :] for d in range(3)]
        fluid = sample(el_ref[rows, :], *xi, basis_ref.at[half], fluid_ref.at[half])
        stay = 1.0 - dep_ref[rows, :]
        for at, value in enumerate(update(xi, [vel_ref[d, rows, :] for d in range(3)], fluid)):
            kept_ref[at, rows, :] = value * stay
        for d in range(3):
            kept_ref[6 + d, rows, :] = mom_ref[d, rows, :] * stay

    ax, gap = lax.axis_index("ax"), lax.axis_index("gap")

    def arrive_block(row, half):
        absent = ((row == 0) & (ax == 0)) | ((row == 1) & (ax == sizes[0] - 1)) | ((row == 4) & (gap == 0)) | ((row == 5) & (gap == sizes[2] - 1))
        state = [arr_ref[row, d] for d in range(11)]
        fluid = sample(state[9].astype(jnp.int32), *state[0:3], basis_ref.at[half], fluid_ref.at[half])
        live = state[10] * jnp.where(absent, 0.0, 1.0)
        for at, value in enumerate(update(state[0:3], state[3:6], fluid) + state[6:9]):
            arrived_ref[row, at] = value * live

    @pl.loop(0, 8 // STEP)
    def _(block):
        for half in range(STEP):
            stay_block(block * STEP + half, half)

    @pl.loop(0, 6 // STEP)
    def _(row):
        for half in range(STEP):
            arrive_block(row * STEP + half, half)

def settle(sizes, w, xi, vel, mom, el, dep, arr):
    b = bary_weights()
    rows = (b[:, None, None] * np.ones((1, 4, 1)) * b[None, None, :]).reshape(256, 1)
    bary = np.ascontiguousarray(rows * np.tile(b, 16)[None, :], dtype=np.float32)
    return pl.pallas_call(
        functools.partial(settle_kernel, sizes),
        out_shape=(jax.ShapeDtypeStruct((256, 128), jnp.float32), jax.ShapeDtypeStruct((9, 64, 128), jnp.float32), jax.ShapeDtypeStruct((6, 9, 8, 128), jnp.float32)),
        in_specs=[pl.BlockSpec(memory_space=pltpu.VMEM)] * 8,
        out_specs=(pl.BlockSpec(memory_space=pltpu.VMEM),) * 3,
        scratch_shapes=[pltpu.VMEM((256, 384), jnp.bfloat16), pltpu.VMEM((STEP, 4, 64, 128), jnp.float32), pltpu.VMEM((STEP, 8, 128), jnp.float32)],
        name="settle",
    )(w, bary, xi, vel, mom, el, dep, arr)

def diff_table():
    b = bary_weights()
    eye = np.eye(8, dtype=bool)
    diff = np.where(eye, 1.0, GLL_NODES[:, None] - GLL_NODES[None, :])
    off = np.where(eye, 0.0, b[None, :] / b[:, None] / diff)
    return (off - np.eye(8) * np.sum(off, axis=1)[:, None]).astype(np.float32)

def pieces(a, count=2):
    parts = []
    rest = a.astype(np.float32)
    for _ in range(count):
        part = rest.astype(jnp.bfloat16)
        parts.append(part)
        rest = rest - part.astype(np.float32)
    return parts

def field_consts():
    d = diff_table()
    eye = np.eye(16, dtype=np.float32)

    def left(m):
        h, l = pieces(np.kron(eye, m))
        return np.block([[h, h], [l, l]])

    def right(m):
        h, l = pieces(4.0 * np.kron(eye, m))
        return np.block([[h, l], [h, l]])

    w8 = GLL_WEIGHTS.astype(np.float32)
    half = np.where((np.arange(8) == 0) | (np.arange(8) == 7), 0.5, 1.0)
    r = np.arange(32)[:, None] + np.zeros((1, 128))
    c = np.arange(128)[None, :] + np.zeros((32, 1))
    small = np.stack([np.tile(w8, 4)[:, None] * np.tile(w8, 16)[None, :], np.tile(half, 4)[:, None] * np.tile(half, 16)[None, :],
                      (r % 8 == 0) & (r > 0), (r % 8 == 7) & (r < 31), (c % 8 == 0) & (c > 0), (c % 8 == 7) & (c < 127)]).astype(np.float32)
    ends = np.zeros((8, 384), np.float32)
    for piece in range(3):
        ends[0, piece * 128] = 1.0
        ends[1, piece * 128 + 127] = 1.0
    spread = np.zeros((32, 128), np.float32)
    for piece in range(3):
        spread[piece * 8, 0] = 1.0
        spread[piece * 8 + 1, 127] = 1.0
    bf = lambda t: np.ascontiguousarray(t).astype(jnp.bfloat16)
    return [bf(left(d)), bf(left(d.T)), bf(right(d.T)), bf(right(d)), small, bf(ends), bf(spread)]

def halves(x):
    high = x.astype(jnp.bfloat16)
    return high, (x - high.astype(jnp.float32)).astype(jnp.bfloat16)

def thirds(x):
    high, rest = x.astype(jnp.bfloat16), None
    rest = x - high.astype(jnp.float32)
    mid = rest.astype(jnp.bfloat16)
    return high, mid, (rest - mid.astype(jnp.float32)).astype(jnp.bfloat16)

def mix(a, b, dims=((1,), (0,))):
    return lax.dot_general(a, b, (dims, ((), ())), preferred_element_type=jnp.float32)

def along_circ(x, left):
    x = jnp.concatenate([x[0:128], x[128:256]], axis=1)
    y = mix(left, jnp.concatenate(halves(x), axis=0))
    y = y[0:128] + y[128:256]
    return jnp.concatenate([y[:, 0:128], y[:, 128:256]], axis=0)

def along_gap(x, right):
    y = mix(jnp.concatenate(halves(x), axis=1), right)
    return y[:, 0:128] + y[:, 128:256]

def along_ax(x, d):
    x = [x[i * 32:i * 32 + 32] for i in range(8)]
    even = [x[j] + x[7 - j] for j in range(4)]
    odd = [x[j] - x[7 - j] for j in range(4)]
    out = [None] * 8
    for i in range(4):
        a = b = None
        for j in range(4):
            p = np.float32(0.5 * (float(d[i, j]) - float(d[i, 7 - j]))) * odd[j]
            q = np.float32(0.5 * (float(d[i, j]) + float(d[i, 7 - j]))) * even[j]
            a = p if a is None else a + p
            b = q if b is None else b + q
        out[i] = a + b
        out[7 - i] = a - b
    return jnp.concatenate(out, axis=0)

def flow_kernel(sizes, *refs):
    sources, (out_ref, arr_ref, dep_ref), held, rest = refs[0:16], refs[16:19], refs[19:35], refs[35:]
    small_ref, w_ref, force_ref, yield_ref, lc_ref, rg_ref, ends_ref, spread_ref, slots_ref, counts_ref, xi_ref, vel_ref, mom_ref, new_ref, lct_ref, rgt_ref = held
    (v_ref, f_ref, z_ref, quad_ref, stiff_ref, edge_c, edge_e, edge_g, got_a, got_c, got_e, got_g, pair_ref, sum_ref, got_sum, buf_ref, id_ref,
     send_sem, recv_sem, sum_send, sum_recv, mig_send, mig_recv, load_sem) = rest
    loads = [pltpu.make_async_copy(source, mine, load_sem.at[i]) for i, (source, mine) in enumerate(zip(sources, held))]
    for load in loads:
        load.start()
    n_ax, n_circ, n_gap = sizes
    d8 = diff_table()
    ax, circ, gap = lax.axis_index("ax"), lax.axis_index("circ"), lax.axis_index("gap")

    def at(da=0, dc=0, dg=0):
        place = {}
        if da:
            place["ax"] = lax.rem(ax + (da + n_ax), n_ax)
        if dc:
            place["circ"] = lax.rem(circ + (dc + n_circ), n_circ)
        if dg:
            place["gap"] = lax.rem(gap + (dg + n_gap), n_gap)
        return place

    around = [(a, c, g) for a in (0, -1, 1) for c in (0, -1, 1) for g in (0, -1, 1) if (a, c, g) != (0, 0, 0)]
    plane = [(a, g) for a in range(n_ax) for g in range(n_gap) if (a, g) != (0, 0)]
    near = [(a % n_ax, g % n_gap) for a in (0, -1, 1) for g in (0, -1, 1)]
    peers = [at(*d) for d in around] + [at(dc=o) for o in range(2, n_circ - 1)] + [at(da=o[0], dg=o[1]) for o in plane if o not in near]
    barrier = pltpu.get_barrier_semaphore()
    for peer in peers:
        pl.semaphore_signal(barrier, inc=1, device_id=peer, device_id_type=MESH)

    for load in loads[0:3]:
        load.wait()
    weights = GLL_WEIGHTS.astype(np.float32)
    quad = jnp.concatenate([small_ref[0] * weights[i] for i in range(8)], axis=0)
    quad_ref[...] = quad
    col = lax.broadcasted_iota(jnp.int32, (32, 128), 1)
    at_wall = ((col == 0) & (gap == 0)) | ((col == 127) & (gap == n_gap - 1))
    wall = jnp.where(at_wall, 0.0, 1.0)
    share = small_ref[1] * jnp.where(at_wall, 2.0, 1.0)
    low_ax = jnp.where(ax == 0, 0.0, 1.0)
    high_ax = jnp.where(ax == n_ax - 1, 0.0, 1.0)
    low_gap = jnp.where(gap == 0, 0.0, 1.0)
    high_gap = jnp.where(gap == n_gap - 1, 0.0, 1.0)
    ax_share = [jnp.where(ax == 0, 1.0, 0.5)] + [1.0] * 6 + [jnp.where(ax == n_ax - 1, 1.0, 0.5)]
    pair_ref[...] = jnp.zeros((8, 256), jnp.float32)

    def every(tile):
        return jnp.concatenate([tile] * 8, axis=0)

    def gather_inner(f):
        f = f + every(small_ref[2]) * pltpu.roll(f, 1, 0) + every(small_ref[3]) * pltpu.roll(f, 255, 0)
        return f + every(small_ref[4]) * pltpu.roll(f, 1, 1) + every(small_ref[5]) * pltpu.roll(f, 127, 1)

    def remote(src, dst, k, t, place):
        return pltpu.make_async_remote_copy(src_ref=src, dst_ref=dst, send_sem=send_sem.at[k, t], recv_sem=recv_sem.at[k, t],
                                            device_id=place, device_id_type=MESH)

    def stage(k, f):
        f = gather_inner(f)
        f_ref[k] = f
        z_ref[k] = f
        edge_c[k, 0] = f_ref[k, pl.ds(0, 8, stride=32), :]
        edge_c[k, 1] = f_ref[k, pl.ds(31, 8, stride=32), :]
        for e, at_row in enumerate((0, 31, 224, 255)):
            edge_e[k, e] = f_ref[k, at_row:at_row + 1, :]

    def send(k):
        copies = [remote(edge_e.at[k, e], got_e.at[k, 3 - e], k, 4 + e, at(da=1 if e >= 2 else -1, dc=1 if e % 2 else -1)) for e in range(4)]
        copies += [remote(edge_c.at[k, 0], got_c.at[k, 1], k, 2, at(dc=-1)),
                   remote(edge_c.at[k, 1], got_c.at[k, 0], k, 3, at(dc=1)),
                   remote(f_ref.at[k, 0:32], got_a.at[k, 1], k, 0, at(da=-1)),
                   remote(f_ref.at[k, 224:256], got_a.at[k, 0], k, 1, at(da=1))]
        for copy in copies:
            copy.start()
        faces = mix(ends_ref[...], jnp.concatenate(thirds(f_ref[k]), axis=1), ((1,), (1,)))
        for s in range(2):
            for h in range(2):
                edge_g[k, s, h] = faces[s:s + 1, h * 128:h * 128 + 128]
        later = []
        for s in range(2):
            dg = 1 if s else -1
            t = 8 + 9 * s
            for a in (-1, 1):
                for c in (-1, 1):
                    slot = 8 + (2 if a < 0 else 0) + (1 if c < 0 else 0)
                    later.append(remote(edge_g.at[k, s, 1 if a > 0 else 0], got_g.at[k, 1 - s, slot], k, t + slot - 3, at(da=a, dc=c, dg=dg)))
            for a in (-1, 1):
                slot = 7 if a < 0 else 6
                later.append(remote(edge_g.at[k, s, 1 if a > 0 else 0], got_g.at[k, 1 - s, slot], k, t + slot - 3, at(da=a, dg=dg)))
            for c in (0, -1, 1):
                slot = {0: 0, 1: 1, -1: 2}[c]
                later.append(remote(edge_g.at[k, s], got_g.at[k, 1 - s, 2 * slot:2 * slot + 2], k, t + slot, at(dc=c, dg=dg)))
        for copy in later:
            copy.start()
        return copies + later

    lane = lax.broadcasted_iota(jnp.int32, (1, 128), 1)
    place_of = lax.bitwise_and(lane, 31)

    def receive(k, copies):
        for copy in copies:
            copy.wait_recv()
        z_ref[k, 0:32, :] = z_ref[k, 0:32, :] + got_a[k, 0] * low_ax
        z_ref[k, 224:256, :] = z_ref[k, 224:256, :] + got_a[k, 1] * high_ax
        z_ref[k, pl.ds(0, 8, stride=32), :] = z_ref[k, pl.ds(0, 8, stride=32), :] + got_c[k, 0]
        z_ref[k, pl.ds(31, 8, stride=32), :] = z_ref[k, pl.ds(31, 8, stride=32), :] + got_c[k, 1]
        for e, at_row in enumerate((0, 31, 224, 255)):
            z_ref[k, at_row:at_row + 1, :] = z_ref[k, at_row:at_row + 1, :] + got_e[k, e] * (low_ax if e < 2 else high_ax)
        for s in range(2):
            def moved(slot, shift, keep):
                return jnp.where(keep, pltpu.roll(got_g[k, s, slot], shift, 1), 0.0)

            low = moved(6, 32, lane < 32) + moved(8, 1, lane == 0) + moved(9, 63, lane == 31)
            high = moved(7, 96, lane >= 96) + moved(10, 65, lane == 96) + moved(11, 127, lane == 127)
            sides = []
            for h, extra in ((0, low * low_ax), (1, high * high_ax)):
                sides.append(got_g[k, s, h] + moved(2 + h, 97, place_of == 0) + moved(4 + h, 31, place_of == 31) + extra)
            for h in range(2):
                pair_ref[s:s + 1, h * 128:h * 128 + 128] = sides[h] * (high_gap if s else low_gap)
        pair = pair_ref[...]
        pair = jnp.concatenate(thirds(pair) + (jnp.zeros((8, 256), jnp.bfloat16),), axis=0)
        v_ref[k] = (z_ref[k] + mix(pair, spread_ref[...], ((0,), (0,)))) * every(wall)

    fields = [lambda b, ref=ref, d=d: ref[d, b * 8:b * 8 + 8, :] for ref in (xi_ref, vel_ref, mom_ref) for d in range(3)]
    fields.append(lambda b: id_ref[b * 8:b * 8 + 8, :])
    moves = [at(da=1), at(da=-1), at(dc=1), at(dc=-1), at(dg=1), at(dg=-1)]
    moving = [pltpu.make_async_remote_copy(src_ref=buf_ref.at[r], dst_ref=arr_ref.at[r], send_sem=mig_send.at[r], recv_sem=mig_recv.at[r],
                                           device_id=place, device_id_type=MESH) for r, place in enumerate(moves)]

    def pack_rows(first, last):
        @pl.loop(first, last)
        def _(row):
            leaving_row(fields, slots_ref, counts_ref[row], row, buf_ref)

        for copy in moving[first:last]:
            copy.start()

    stage(0, quad * 0.25 * (4.0 * w_ref[...] + force_ref[...]))
    pl.semaphore_wait(barrier, len(peers))
    for load in loads[3:7]:
        load.wait()
    copies = send(0)
    w = w_ref[...]
    slope_a, slope_c, slope_g = along_ax(w, d8), along_circ(w, lc_ref[...]), along_gap(w, rg_ref[...])
    squares = 1.0 + slope_a * slope_a + slope_c * slope_c + slope_g * slope_g
    stiff_ref[...] = quad * 0.25 * (0.05 + yield_ref[...] / jnp.sqrt(squares))
    for load in loads[7:]:
        load.wait()
    id_ref[...] = new_ref[...].astype(jnp.float32)
    pack_rows(0, 3)
    receive(0, copies)

    def total(x):
        return jnp.sum(x.reshape(32, 8, 128), axis=0)

    sums = []
    for k in range(3):
        v = v_ref[k]
        stiff = stiff_ref[...]
        slope_a, slope_c, slope_g = along_ax(v, d8), along_circ(v, lc_ref[...]), along_gap(v, rg_ref[...])
        if k < 2:
            image = quad_ref[...] * v + along_ax(stiff * slope_a, d8.T)
            image = image + along_circ(stiff * slope_c, lct_ref[...]) + along_gap(stiff * slope_g, rgt_ref[...])
            stage(k + 1, image)
            sent, copies = copies, send(k + 1)
        square = v * v
        sums.append(total(jnp.concatenate([square[i * 32:i * 32 + 32] * (share * ax_share[i]) for i in range(8)], axis=0)))
        sums.append(total(quad_ref[...] * square + stiff * (slope_a * slope_a + slope_c * slope_c + slope_g * slope_g)))
        if k == 0:
            pack_rows(3, 6)
        if k == 1:
            dep_ref[...] = departed_flags(slots_ref, counts_ref)
        if k < 2:
            for copy in sent:
                copy.wait_send()
            receive(k + 1, copies)

    sub = lax.broadcasted_iota(jnp.int32, (8, 128), 0)
    part = lax.broadcasted_iota(jnp.int32, (8, 128), 1) // 16
    rows = jnp.zeros((8, 128), jnp.float32)
    for m, value in enumerate(sums):
        rows = jnp.where(sub == m, jnp.broadcast_to(jnp.sum(value, axis=0, keepdims=True), (8, 128)), rows)
    for shift in (64, 32, 16):
        rows = rows + pltpu.roll(rows, shift, 1)
    line = jnp.sum(jnp.where(sub == part, rows, 0.0), axis=0, keepdims=True)
    slot = 0
    for step, places in enumerate(([at(dc=o) for o in range(1, n_circ)], [at(da=a, dg=g) for a, g in plane])):
        sum_ref[step] = line
        rounds = []
        for place in places:
            rounds.append(pltpu.make_async_remote_copy(src_ref=sum_ref.at[step], dst_ref=got_sum.at[slot], send_sem=sum_send.at[slot],
                                                       recv_sem=sum_recv.at[slot], device_id=place, device_id_type=MESH))
            slot += 1
        for copy in rounds:
            copy.start()
        if step == 0:
            for copy in copies:
                copy.wait_send()
        for copy in rounds:
            copy.wait_recv()
        for o in range(len(places)):
            line = line + got_sum[slot - 1 - o]
        for copy in rounds:
            copy.wait_send()
    m = jnp.sum(jnp.where(sub == part, jnp.broadcast_to(line, (8, 128)), 0.0), axis=1, keepdims=True)
    m0, m1, m2, m3, m4, m5 = [m[i:i + 1, :] for i in range(6)]
    scale = m0 / m1
    m1 = m1 * scale
    m2 = m2 * scale * scale
    m3 = m3 * scale * scale * scale
    m4 = m4 * scale * scale * scale * scale
    m5 = m5 * scale * scale * scale * scale * scale

    def ratio(a, b):
        return jnp.where((a > 0.0) & (b > 0.0), a / b, 0.0)

    a0 = m0 / m1
    rr1 = a0 * a0 * m2 - m0
    e = 1.0 + rr1 / m0
    p1 = e * e * m1 - 2.0 * e * a0 * m2 + a0 * a0 * m3
    a1 = ratio(rr1, p1)
    c1 = a0 + a1 * e
    c2 = a0 * a1
    rr2 = m0 - 2.0 * c1 * m1 + (c1 * c1 + 2.0 * c2) * m2 - 2.0 * c1 * c2 * m3 + c2 * c2 * m4
    ra2 = m1 - 2.0 * c1 * m2 + (c1 * c1 + 2.0 * c2) * m3 - 2.0 * c1 * c2 * m4 + c2 * c2 * m5
    b1 = ratio(rr2, rr1)
    a2 = ratio(rr2, ra2 - b1 * ratio(rr2, a1))
    x0 = scale * (a0 + a1 * e + a2 * (1.0 + b1 * e))
    x1 = scale * scale * (-(c2 + a2 * (c1 + b1 * a0)))
    x2 = scale * scale * scale * (a2 * c2)
    out_ref[...] = x0 * v_ref[0] + x1 * v_ref[1] + x2 * v_ref[2]
    for copy in moving:
        copy.wait()

def flow(sizes, w, yld, force, xi, vel, mom, new, slots, counts):
    lc, lct, rg, rgt, small, ends, spread = field_consts()
    args = (small, w, force, yld, lc, rg, ends, spread, slots, counts, xi, vel, mom, new, lct, rgt)
    vm = lambda *s: pltpu.VMEM(s, jnp.float32)
    sums = sizes[1] - 1 + sizes[0] * sizes[2] - 1
    whole = pl.BlockSpec(memory_space=pltpu.VMEM)
    kept = [pltpu.SMEM(t.shape, t.dtype) if t is counts else pltpu.VMEM(t.shape, t.dtype) for t in args]
    return pl.pallas_call(
        functools.partial(flow_kernel, sizes),
        out_shape=(jax.ShapeDtypeStruct((256, 128), jnp.float32), jax.ShapeDtypeStruct((6, 11, 8, 128), jnp.float32), jax.ShapeDtypeStruct((64, 128), jnp.float32)),
        in_specs=[pl.BlockSpec(memory_space=pl.ANY)] * 16,
        out_specs=(whole, pl.BlockSpec(memory_space=pl.ANY), whole),
        scratch_shapes=kept + [vm(3, 256, 128), vm(3, 256, 128), vm(3, 256, 128), vm(256, 128), vm(256, 128), vm(3, 2, 8, 128), vm(3, 4, 1, 128), vm(3, 2, 2, 1, 128),
                        vm(3, 2, 32, 128), vm(3, 2, 8, 128), vm(3, 4, 1, 128), vm(3, 2, 12, 1, 128), vm(8, 256), vm(2, 1, 128), vm(sums, 1, 128),
                        vm(6, 11, 8, 128), vm(64, 128),
                        pltpu.SemaphoreType.DMA((3, 26)), pltpu.SemaphoreType.DMA((3, 26)), pltpu.SemaphoreType.DMA((sums,)),
                        pltpu.SemaphoreType.DMA((sums,)), pltpu.SemaphoreType.DMA((6,)), pltpu.SemaphoreType.DMA((6,)), pltpu.SemaphoreType.DMA((16,))],
        compiler_params=pltpu.CompilerParams(collective_id=0, has_side_effects=True),
        name="flow",
    )(*args)

def solution(mesh):
    sizes = (mesh.shape["ax"], mesh.shape["circ"], mesh.shape["gap"])

    def shards(w_old, yield_stress, force, xi, vel, mom, el, new, slots, counts):
        flat = lambda t: t.reshape(256, 128)
        xi, vel, mom = [t.reshape(3, 64, 128) for t in (xi, vel, mom)]
        w, arr, dep = flow(sizes, flat(w_old), flat(yield_stress), flat(force), xi, vel, mom, new.reshape(64, 128), slots.reshape(6, 8, 128), counts.reshape(6))
        w_new, kept, arrived = settle(sizes, w, xi, vel, mom, el.reshape(64, 128), dep, arr)
        return w_new.reshape(w_old.shape), kept.reshape(1, 1, 1, 9, 8192), arrived.reshape(1, 1, 1, 6, 9, 1024)

    spec = lambda n: P("ax", "circ", "gap", *([None] * n))
    return jax.shard_map(
        shards,
        mesh=mesh,
        in_specs=(spec(0), spec(0), spec(0), spec(2), spec(2), spec(2), spec(1), spec(1), spec(2), spec(1)),
        out_specs=(spec(0), spec(2), spec(3)),
        check_vma=False,
    )
```

```python
import functools
import jax, jax.numpy as jnp, numpy as np
from jax import lax
from jax.experimental import pallas as pl
from jax.experimental.pallas import tpu as pltpu
from jax.sharding import PartitionSpec as P

MESH = pl.DeviceIdType.MESH
GLL_NODES = np.array([-1.0,-0.8717401485096066,-0.5917001814331423,-0.2092992179024789,0.2092992179024789,0.5917001814331423,0.8717401485096066,1.0])
GLL_WEIGHTS = np.array([0.03571428571428571,0.2107042271435061,0.3411226924835044,0.4124587946587038,0.4124587946587038,0.3411226924835044,0.2107042271435061,0.03571428571428571])

def bary_weights():
    eye = np.eye(8, dtype=bool)
    diff = np.where(eye, 1.0, GLL_NODES[:, None] - GLL_NODES[None, :])
    return 1.0 / np.prod(diff, axis=1)

def pick(rows, lanes):
    return jnp.take_along_axis(rows, lanes, axis=1, mode="promise_in_bounds")

def pick_row(rows, at):
    return jnp.take_along_axis(rows, at, axis=0, mode="promise_in_bounds")

def leaving_row(fields, slots_ref, count, row, buf_ref):
    lane = lax.broadcasted_iota(jnp.int32, (8, 128), 1)
    for s in range(8):
        slot = jnp.broadcast_to(slots_ref[row, s:s + 1, :], (8, 128))
        block = lax.shift_right_logical(slot, 10)
        inner = lax.bitwise_and(lax.shift_right_logical(slot, 7), 7)
        within = lax.bitwise_and(slot, 127)
        live = (lane + s * 128 < count).astype(jnp.float32)
        for f, field in enumerate(fields):
            found = None
            for b in range(8):
                got = pick(field(b), within)
                found = got if found is None else jnp.where(block == b, got, found)
            found = pick_row(found, inner) * live
            buf_ref[row, f, s:s + 1, :] = found[0:1]
        buf_ref[row, 10, s:s + 1, :] = live[0:1]

def departed_flags(slots_ref, counts_ref):
    sub64 = lax.broadcasted_iota(jnp.int32, (64, 128), 0)
    sub128 = lax.broadcasted_iota(jnp.int32, (128, 128), 0)
    lanes = lax.broadcasted_iota(jnp.int32, (1, 128), 1)

    def one(row, total):
        count = counts_ref[row]
        blocks, places = [], []
        for s in range(8):
            slot = slots_ref[row, s:s + 1, :]
            block = jnp.where(lanes + s * 128 < count, lax.shift_right_logical(slot, 7), 64)
            within = lax.bitwise_and(slot, 127)
            blocks.append(jnp.where(sub64 == block, 1.0, 0.0).astype(jnp.bfloat16))
            places.append(jnp.where(sub128 == within, 1.0, 0.0).astype(jnp.bfloat16))
        return total + lax.dot_general(jnp.concatenate(blocks, 1), jnp.concatenate(places, 1), (((1,), (1,)), ((), ())), preferred_element_type=jnp.float32)

    return lax.fori_loop(0, 6, one, jnp.zeros((64, 128), jnp.float32))

def ladder(x):
    d = [x - np.float32(n) for n in GLL_NODES]
    pre = [None] * 8
    suf = [None] * 8
    pre[1] = d[0]
    for k in range(2, 8):
        pre[k] = pre[k - 1] * d[k - 1]
    suf[6] = d[7]
    for k in range(5, -1, -1):
        suf[k] = suf[k + 1] * d[k + 1]
    return [suf[0]] + [pre[k] * suf[k] for k in range(1, 7)] + [pre[7]]

LATE = 3

def bary_table():
    b = bary_weights()
    rows = (b[:, None, None] * np.ones((1, 4, 1)) * b[None, None, :]).reshape(256, 1)
    return np.ascontiguousarray(rows * np.tile(b, 16)[None, :], dtype=np.float32)

def make_table(table_ref, k, v, bary):
    v = (v * bary).reshape(16, 2, 8, 128)
    v = jnp.concatenate([v[:, 0].reshape(128, 128), v[:, 1].reshape(128, 128)], axis=1)
    high = v.astype(jnp.bfloat16)
    low = (v - high.astype(jnp.float32)).astype(jnp.bfloat16)
    table_ref[k, :, 0:256] = high
    table_ref[k, :, 256:512] = low
    table_ref[k, :, 512:768] = high

def sample(table_ref, first, count, ids, points, basis_ref, put):
    for d in range(2):
        for k, value in enumerate(ladder(points[d])):
            basis_ref[d, k * 8:k * 8 + 8, :] = value
    for k, value in enumerate(ladder(points[2])):
        rounded = value.astype(jnp.bfloat16).astype(jnp.float32)
        basis_ref[2, k * 8:k * 8 + 8, :] = rounded
        basis_ref[3, k * 8:k * 8 + 8, :] = value - rounded
    second_half = jnp.where(lax.broadcasted_iota(jnp.int32, (16, 128), 0) >= 8, 1.0, 0.0)
    zero = jnp.zeros((16, 128), jnp.bfloat16)
    circ = lax.shift_right_logical(ids, 5)
    radial = lax.bitwise_and(ids, 31).astype(jnp.float32)
    table = table_ref[first:first + count].reshape(count * 128, 768)
    for q in range(4):
        right, weights = [], []
        for s in (2 * q, 2 * q + 1):
            mine = (jnp.broadcast_to(radial[s:s + 1], (16, 128)) - second_half).astype(jnp.bfloat16)
            high16 = jnp.concatenate([basis_ref[2, pl.ds(s, 8, stride=8), :]] * 2, axis=0).astype(jnp.bfloat16)
            low16 = jnp.concatenate([basis_ref[3, pl.ds(s, 8, stride=8), :]] * 2, axis=0).astype(jnp.bfloat16)
            same = [mine == jnp.bfloat16(2 * t) for t in range(16)]
            b_high = jnp.concatenate([jnp.where(m, high16, zero) for m in same], axis=0)
            b_low = jnp.concatenate([jnp.where(m, low16, zero) for m in same], axis=0)
            right.append(jnp.concatenate([b_high, b_high, b_low], axis=0))
            second = basis_ref[1, pl.ds(s, 8, stride=8), :]
            cc = jnp.broadcast_to(circ[s:s + 1], (8, 128))
            weights.append([jnp.where(cc == c, second, 0.0) for c in range(2)])
        values = jnp.dot(table, jnp.concatenate(right, axis=1), preferred_element_type=jnp.float32)
        for h, s in enumerate((2 * q, 2 * q + 1)):
            for n in range(count):
                total = None
                for i in range(8):
                    line = None
                    for c in range(2):
                        at = n * 128 + i * 16 + c * 8
                        term = values[at:at + 8, h * 128:h * 128 + 128] * weights[h][c]
                        line = term if line is None else line + term
                    line = line * jnp.broadcast_to(basis_ref[0, i * 8 + s:i * 8 + s + 1, :], (8, 128))
                    total = line if total is None else total + line
                put(first + n, s, jnp.sum(total, axis=0, keepdims=True))

def finish_kernel(sizes, w_ref, bary_ref, fluid_ref, xi_ref, vel_ref, mom_ref, dep_ref, arr_ref, w_out, kept_ref, arrived_ref, table_ref, basis_ref, late_ref):
    w_out[...] = w_ref[...]
    make_table(table_ref, 0, w_ref[...], bary_ref[...])

    def keeper(row):
        def put(k, s, value):
            late_ref[row, s:s + 1, :] = value

        return put

    for row in range(LATE):
        at = 6 - LATE + row
        sample(table_ref, 0, 1, arr_ref[at, 9].astype(jnp.int32), [arr_ref[at, d] for d in range(3)], basis_ref.at[row], keeper(row))
    ax, gap = lax.axis_index("ax"), lax.axis_index("gap")
    absent = [ax == 0, ax == sizes[0] - 1, None, None, gap == 0, gap == sizes[2] - 1]

    def update(xi, vel, fluid):
        axial = vel[0] + 0.4 * (fluid - vel[0])
        circ = vel[1] * (1.0 - 0.4)
        radial = vel[2] * (1.0 - 0.4)
        return [xi[0] + 0.25 * axial, xi[1] + 0.25 * circ, xi[2] + 1.0 * radial, axial, circ, radial]

    stay = 1.0 - dep_ref[...]
    state = update([xi_ref[d] for d in range(3)], [vel_ref[d] for d in range(3)], fluid_ref[0:64]) + [mom_ref[d] for d in range(3)]
    for at, value in enumerate(state):
        kept_ref[at] = value * stay
    for row in range(6):
        state = [arr_ref[row, d] for d in range(11)]
        live = state[10] if absent[row] is None else state[10] * jnp.where(absent[row], 0.0, 1.0)
        fluid = fluid_ref[64 + 8 * row:72 + 8 * row] if row < 6 - LATE else late_ref[row - 6 + LATE]
        for at, value in enumerate(update(state[0:3], state[3:6], fluid) + state[6:9]):
            arrived_ref[row, at] = value * live

def finish(sizes, w, bary, fluid, xi, vel, mom, dep, arr):
    return pl.pallas_call(
        functools.partial(finish_kernel, sizes),
        out_shape=(jax.ShapeDtypeStruct((256, 128), jnp.float32), jax.ShapeDtypeStruct((9, 64, 128), jnp.float32), jax.ShapeDtypeStruct((6, 9, 8, 128), jnp.float32)),
        in_specs=[pl.BlockSpec(memory_space=pltpu.VMEM)] * 8,
        out_specs=(pl.BlockSpec(memory_space=pltpu.VMEM),) * 3,
        scratch_shapes=[pltpu.VMEM((1, 128, 768), jnp.bfloat16), pltpu.VMEM((LATE, 4, 64, 128), jnp.float32), pltpu.VMEM((LATE, 8, 128), jnp.float32)],
        name="finish",
    )(w, bary, fluid, xi, vel, mom, dep, arr)


def diff_table():
    b = bary_weights()
    eye = np.eye(8, dtype=bool)
    diff = np.where(eye, 1.0, GLL_NODES[:, None] - GLL_NODES[None, :])
    off = np.where(eye, 0.0, b[None, :] / b[:, None] / diff)
    return (off - np.eye(8) * np.sum(off, axis=1)[:, None]).astype(np.float32)

def pieces(a, count=2):
    parts = []
    rest = a.astype(np.float32)
    for _ in range(count):
        part = rest.astype(jnp.bfloat16)
        parts.append(part)
        rest = rest - part.astype(np.float32)
    return parts

def field_consts():
    d = diff_table()
    eye = np.eye(16, dtype=np.float32)

    def left(m):
        h, l = pieces(np.kron(eye, m))
        return np.block([[h, h], [l, l]])

    def right(m):
        h, l = pieces(4.0 * np.kron(eye, m))
        return np.block([[h, l], [h, l]])

    w8 = GLL_WEIGHTS.astype(np.float32)
    half = np.where((np.arange(8) == 0) | (np.arange(8) == 7), 0.5, 1.0)
    r = np.arange(32)[:, None] + np.zeros((1, 128))
    c = np.arange(128)[None, :] + np.zeros((32, 1))
    small = np.stack([np.tile(w8, 4)[:, None] * np.tile(w8, 16)[None, :], np.tile(half, 4)[:, None] * np.tile(half, 16)[None, :],
                      (r % 8 == 0) & (r > 0), (r % 8 == 7) & (r < 31), (c % 8 == 0) & (c > 0), (c % 8 == 7) & (c < 127)]).astype(np.float32)
    ends = np.zeros((8, 384), np.float32)
    for piece in range(3):
        ends[0, piece * 128] = 1.0
        ends[1, piece * 128 + 127] = 1.0
    spread = np.zeros((32, 128), np.float32)
    for piece in range(3):
        spread[piece * 8, 0] = 1.0
        spread[piece * 8 + 1, 127] = 1.0
    bf = lambda t: np.ascontiguousarray(t).astype(jnp.bfloat16)
    return [bf(left(d)), bf(left(d.T)), bf(right(d.T)), bf(right(d)), small, bf(ends), bf(spread)]

def halves(x):
    high = x.astype(jnp.bfloat16)
    return high, (x - high.astype(jnp.float32)).astype(jnp.bfloat16)

def thirds(x):
    high, rest = x.astype(jnp.bfloat16), None
    rest = x - high.astype(jnp.float32)
    mid = rest.astype(jnp.bfloat16)
    return high, mid, (rest - mid.astype(jnp.float32)).astype(jnp.bfloat16)

def mix(a, b, dims=((1,), (0,))):
    return lax.dot_general(a, b, (dims, ((), ())), preferred_element_type=jnp.float32)

def along_circ(x, left):
    x = jnp.concatenate([x[0:128], x[128:256]], axis=1)
    y = mix(left, jnp.concatenate(halves(x), axis=0))
    y = y[0:128] + y[128:256]
    return jnp.concatenate([y[:, 0:128], y[:, 128:256]], axis=0)

def along_gap(x, right):
    y = mix(jnp.concatenate(halves(x), axis=1), right)
    return y[:, 0:128] + y[:, 128:256]

def along_ax(x, d):
    x = [x[i * 32:i * 32 + 32] for i in range(8)]
    even = [x[j] + x[7 - j] for j in range(4)]
    odd = [x[j] - x[7 - j] for j in range(4)]
    out = [None] * 8
    for i in range(4):
        a = b = None
        for j in range(4):
            p = np.float32(0.5 * (float(d[i, j]) - float(d[i, 7 - j]))) * odd[j]
            q = np.float32(0.5 * (float(d[i, j]) + float(d[i, 7 - j]))) * even[j]
            a = p if a is None else a + p
            b = q if b is None else b + q
        out[i] = a + b
        out[7 - i] = a - b
    return jnp.concatenate(out, axis=0)

def flow_kernel(sizes, *refs):
    sources, (out_ref, arr_out, dep_ref, fluid_ref), held, rest = refs[0:18], refs[18:22], refs[22:40], refs[40:]
    small_ref, w_ref, force_ref, yield_ref, lc_ref, rg_ref, ends_ref, spread_ref, slots_ref, counts_ref, xi_ref, vel_ref, mom_ref, new_ref, lct_ref, rgt_ref, bary_ref, el_ref = held
    (v_ref, f_ref, z_ref, quad_ref, stiff_ref, edge_c, edge_e, edge_g, got_a, got_c, got_e, got_g, pair_ref, sum_ref, got_sum, buf_ref, id_ref, arr_ref, table_ref, basis_ref, part_ref,
     send_sem, recv_sem, sum_send, sum_recv, mig_send, mig_recv, load_sem, keep_sem) = rest
    loads = [pltpu.make_async_copy(source, mine, load_sem.at[i]) for i, (source, mine) in enumerate(zip(sources, held))]
    for load in loads:
        load.start()
    n_ax, n_circ, n_gap = sizes
    d8 = diff_table()
    ax, circ, gap = lax.axis_index("ax"), lax.axis_index("circ"), lax.axis_index("gap")

    def at(da=0, dc=0, dg=0):
        place = {}
        if da:
            place["ax"] = lax.rem(ax + (da + n_ax), n_ax)
        if dc:
            place["circ"] = lax.rem(circ + (dc + n_circ), n_circ)
        if dg:
            place["gap"] = lax.rem(gap + (dg + n_gap), n_gap)
        return place

    around = [(a, c, g) for a in (0, -1, 1) for c in (0, -1, 1) for g in (0, -1, 1) if (a, c, g) != (0, 0, 0)]
    plane = [(a, g) for a in range(n_ax) for g in range(n_gap) if (a, g) != (0, 0)]
    near = [(a % n_ax, g % n_gap) for a in (0, -1, 1) for g in (0, -1, 1)]
    peers = [at(*d) for d in around] + [at(dc=o) for o in range(2, n_circ - 1)] + [at(da=o[0], dg=o[1]) for o in plane if o not in near]
    barrier = pltpu.get_barrier_semaphore()
    for peer in peers:
        pl.semaphore_signal(barrier, inc=1, device_id=peer, device_id_type=MESH)

    for load in loads[0:3]:
        load.wait()
    weights = GLL_WEIGHTS.astype(np.float32)
    quad = jnp.concatenate([small_ref[0] * weights[i] for i in range(8)], axis=0)
    quad_ref[...] = quad
    col = lax.broadcasted_iota(jnp.int32, (32, 128), 1)
    at_wall = ((col == 0) & (gap == 0)) | ((col == 127) & (gap == n_gap - 1))
    wall = jnp.where(at_wall, 0.0, 1.0)
    share = small_ref[1] * jnp.where(at_wall, 2.0, 1.0)
    low_ax = jnp.where(ax == 0, 0.0, 1.0)
    high_ax = jnp.where(ax == n_ax - 1, 0.0, 1.0)
    low_gap = jnp.where(gap == 0, 0.0, 1.0)
    high_gap = jnp.where(gap == n_gap - 1, 0.0, 1.0)
    ax_share = [jnp.where(ax == 0, 1.0, 0.5)] + [1.0] * 6 + [jnp.where(ax == n_ax - 1, 1.0, 0.5)]
    pair_ref[...] = jnp.zeros((8, 256), jnp.float32)

    def every(tile):
        return jnp.concatenate([tile] * 8, axis=0)

    def gather_inner(f):
        f = f + every(small_ref[2]) * pltpu.roll(f, 1, 0) + every(small_ref[3]) * pltpu.roll(f, 255, 0)
        return f + every(small_ref[4]) * pltpu.roll(f, 1, 1) + every(small_ref[5]) * pltpu.roll(f, 127, 1)

    def remote(src, dst, k, t, place):
        return pltpu.make_async_remote_copy(src_ref=src, dst_ref=dst, send_sem=send_sem.at[k, t], recv_sem=recv_sem.at[k, t],
                                            device_id=place, device_id_type=MESH)

    def stage(k, f):
        f = gather_inner(f)
        f_ref[k] = f
        z_ref[k] = f
        edge_c[k, 0] = f_ref[k, pl.ds(0, 8, stride=32), :]
        edge_c[k, 1] = f_ref[k, pl.ds(31, 8, stride=32), :]
        for e, at_row in enumerate((0, 31, 224, 255)):
            edge_e[k, e] = f_ref[k, at_row:at_row + 1, :]

    def send(k):
        copies = [remote(edge_e.at[k, e], got_e.at[k, 3 - e], k, 4 + e, at(da=1 if e >= 2 else -1, dc=1 if e % 2 else -1)) for e in range(4)]
        copies += [remote(edge_c.at[k, 0], got_c.at[k, 1], k, 2, at(dc=-1)),
                   remote(edge_c.at[k, 1], got_c.at[k, 0], k, 3, at(dc=1)),
                   remote(f_ref.at[k, 0:32], got_a.at[k, 1], k, 0, at(da=-1)),
                   remote(f_ref.at[k, 224:256], got_a.at[k, 0], k, 1, at(da=1))]
        for copy in copies:
            copy.start()
        faces = mix(ends_ref[...], jnp.concatenate(thirds(f_ref[k]), axis=1), ((1,), (1,)))
        for s in range(2):
            for h in range(2):
                edge_g[k, s, h] = faces[s:s + 1, h * 128:h * 128 + 128]
        later = []
        for s in range(2):
            dg = 1 if s else -1
            t = 8 + 9 * s
            for a in (-1, 1):
                for c in (-1, 1):
                    slot = 8 + (2 if a < 0 else 0) + (1 if c < 0 else 0)
                    later.append(remote(edge_g.at[k, s, 1 if a > 0 else 0], got_g.at[k, 1 - s, slot], k, t + slot - 3, at(da=a, dc=c, dg=dg)))
            for a in (-1, 1):
                slot = 7 if a < 0 else 6
                later.append(remote(edge_g.at[k, s, 1 if a > 0 else 0], got_g.at[k, 1 - s, slot], k, t + slot - 3, at(da=a, dg=dg)))
            for c in (0, -1, 1):
                slot = {0: 0, 1: 1, -1: 2}[c]
                later.append(remote(edge_g.at[k, s], got_g.at[k, 1 - s, 2 * slot:2 * slot + 2], k, t + slot, at(dc=c, dg=dg)))
        for copy in later:
            copy.start()
        return copies + later

    lane = lax.broadcasted_iota(jnp.int32, (1, 128), 1)
    place_of = lax.bitwise_and(lane, 31)

    def receive(k, copies):
        for copy in copies:
            copy.wait_recv()
        z_ref[k, 0:32, :] = z_ref[k, 0:32, :] + got_a[k, 0] * low_ax
        z_ref[k, 224:256, :] = z_ref[k, 224:256, :] + got_a[k, 1] * high_ax
        z_ref[k, pl.ds(0, 8, stride=32), :] = z_ref[k, pl.ds(0, 8, stride=32), :] + got_c[k, 0]
        z_ref[k, pl.ds(31, 8, stride=32), :] = z_ref[k, pl.ds(31, 8, stride=32), :] + got_c[k, 1]
        for e, at_row in enumerate((0, 31, 224, 255)):
            z_ref[k, at_row:at_row + 1, :] = z_ref[k, at_row:at_row + 1, :] + got_e[k, e] * (low_ax if e < 2 else high_ax)
        for s in range(2):
            def moved(slot, shift, keep):
                return jnp.where(keep, pltpu.roll(got_g[k, s, slot], shift, 1), 0.0)

            low = moved(6, 32, lane < 32) + moved(8, 1, lane == 0) + moved(9, 63, lane == 31)
            high = moved(7, 96, lane >= 96) + moved(10, 65, lane == 96) + moved(11, 127, lane == 127)
            sides = []
            for h, extra in ((0, low * low_ax), (1, high * high_ax)):
                sides.append(got_g[k, s, h] + moved(2 + h, 97, place_of == 0) + moved(4 + h, 31, place_of == 31) + extra)
            for h in range(2):
                pair_ref[s:s + 1, h * 128:h * 128 + 128] = sides[h] * (high_gap if s else low_gap)
        pair = pair_ref[...]
        pair = jnp.concatenate(thirds(pair) + (jnp.zeros((8, 256), jnp.bfloat16),), axis=0)
        v_ref[k] = (z_ref[k] + mix(pair, spread_ref[...], ((0,), (0,)))) * every(wall)

    fields = [lambda b, ref=ref, d=d: ref[d, b * 8:b * 8 + 8, :] for ref in (xi_ref, vel_ref, mom_ref) for d in range(3)]
    fields.append(lambda b: id_ref[b * 8:b * 8 + 8, :])
    moves = [at(da=1), at(da=-1), at(dc=1), at(dc=-1), at(dg=1), at(dg=-1)]
    moving = [pltpu.make_async_remote_copy(src_ref=buf_ref.at[r], dst_ref=arr_ref.at[r], send_sem=mig_send.at[r], recv_sem=mig_recv.at[r],
                                           device_id=place, device_id_type=MESH) for r, place in enumerate(moves)]

    def pack_rows(first, last):
        @pl.loop(first, last)
        def _(row):
            leaving_row(fields, slots_ref, counts_ref[row], row, buf_ref)

        for copy in moving[first:last]:
            copy.start()

    stage(0, quad * 0.25 * (4.0 * w_ref[...] + force_ref[...]))
    pl.semaphore_wait(barrier, len(peers))
    for load in loads[3:7]:
        load.wait()
    copies = send(0)
    w = w_ref[...]
    slope_a, slope_c, slope_g = along_ax(w, d8), along_circ(w, lc_ref[...]), along_gap(w, rg_ref[...])
    squares = 1.0 + slope_a * slope_a + slope_c * slope_c + slope_g * slope_g
    stiff_ref[...] = quad * 0.25 * (0.05 + yield_ref[...] / jnp.sqrt(squares))
    for load in loads[7:]:
        load.wait()
    id_ref[...] = new_ref[...].astype(jnp.float32)
    pack_rows(0, 3)
    receive(0, copies)

    def keeper(base, half):
        def put(k, s, value):
            part_ref[k, base, s:s + 1, :] = value

        return put

    def sample_kept(first, count, block, half):
        rows = pl.ds(pl.multiple_of(block * 8, 8), 8)
        sample(table_ref, first, count, el_ref[rows, :], [xi_ref[d, rows, :] for d in range(3)], basis_ref.at[half], keeper(block, half))

    def sample_arrived(first, count, row, half):
        sample(table_ref, first, count, arr_ref[row, 9].astype(jnp.int32), [arr_ref[row, d] for d in range(3)], basis_ref.at[half], keeper(row + 8, half))

    def sample_pairs(first, count):
        @pl.loop(0, 3)
        def _(two):
            for half in range(2):
                sample_kept(first, count, two * 2 + half, half)

    def total(x):
        return jnp.sum(x.reshape(32, 8, 128), axis=0)

    sums = []
    for k in range(3):
        v = v_ref[k]
        stiff = stiff_ref[...]
        slope_a, slope_c, slope_g = along_ax(v, d8), along_circ(v, lc_ref[...]), along_gap(v, rg_ref[...])
        if k < 2:
            image = quad_ref[...] * v + along_ax(stiff * slope_a, d8.T)
            image = image + along_circ(stiff * slope_c, lct_ref[...]) + along_gap(stiff * slope_g, rgt_ref[...])
            stage(k + 1, image)
            sent, copies = copies, send(k + 1)
        square = v * v
        sums.append(total(jnp.concatenate([square[i * 32:i * 32 + 32] * (share * ax_share[i]) for i in range(8)], axis=0)))
        sums.append(total(quad_ref[...] * square + stiff * (slope_a * slope_a + slope_c * slope_c + slope_g * slope_g)))
        if k == 0:
            pack_rows(3, 6)
            dep_ref[...] = departed_flags(slots_ref, counts_ref)
            make_table(table_ref, 0, v_ref[0], bary_ref[...])
        if k == 1:
            make_table(table_ref, 1, v_ref[1], bary_ref[...])
            sample_pairs(0, 2)
        if k < 2:
            for copy in sent:
                copy.wait_send()
            receive(k + 1, copies)

    sub = lax.broadcasted_iota(jnp.int32, (8, 128), 0)
    part = lax.broadcasted_iota(jnp.int32, (8, 128), 1) // 16
    rows = jnp.zeros((8, 128), jnp.float32)
    for m, value in enumerate(sums):
        rows = jnp.where(sub == m, jnp.broadcast_to(jnp.sum(value, axis=0, keepdims=True), (8, 128)), rows)
    for shift in (64, 32, 16):
        rows = rows + pltpu.roll(rows, shift, 1)
    line = jnp.sum(jnp.where(sub == part, rows, 0.0), axis=0, keepdims=True)
    keep = pltpu.make_async_copy(arr_ref, arr_out, keep_sem)
    slot = 0
    for step, places in enumerate(([at(dc=o) for o in range(1, n_circ)], [at(da=a, dg=g) for a, g in plane])):
        sum_ref[step] = line
        rounds = []
        for place in places:
            rounds.append(pltpu.make_async_remote_copy(src_ref=sum_ref.at[step], dst_ref=got_sum.at[slot], send_sem=sum_send.at[slot],
                                                       recv_sem=sum_recv.at[slot], device_id=place, device_id_type=MESH))
            slot += 1
        for copy in rounds:
            copy.start()
        if step == 0:
            for copy in copies:
                copy.wait_send()
            make_table(table_ref, 2, v_ref[2], bary_ref[...])
            sample_pairs(2, 1)
            sample_kept(0, 3, 6, 0)
        else:
            for copy in moving:
                copy.wait()
            keep.start()
            sample_arrived(0, 3, 0, 0)
            sample_arrived(0, 3, 1, 1)
            sample_kept(0, 3, 7, 0)
            sample_arrived(0, 3, 2, 1)
        for copy in rounds:
            copy.wait_recv()
        for o in range(len(places)):
            line = line + got_sum[slot - 1 - o]
        for copy in rounds:
            copy.wait_send()
    m = jnp.sum(jnp.where(sub == part, jnp.broadcast_to(line, (8, 128)), 0.0), axis=1, keepdims=True)
    m0, m1, m2, m3, m4, m5 = [m[i:i + 1, :] for i in range(6)]
    scale = m0 / m1
    m1 = m1 * scale
    m2 = m2 * scale * scale
    m3 = m3 * scale * scale * scale
    m4 = m4 * scale * scale * scale * scale
    m5 = m5 * scale * scale * scale * scale * scale

    def ratio(a, b):
        return jnp.where((a > 0.0) & (b > 0.0), a / b, 0.0)

    a0 = m0 / m1
    rr1 = a0 * a0 * m2 - m0
    e = 1.0 + rr1 / m0
    p1 = e * e * m1 - 2.0 * e * a0 * m2 + a0 * a0 * m3
    a1 = ratio(rr1, p1)
    c1 = a0 + a1 * e
    c2 = a0 * a1
    rr2 = m0 - 2.0 * c1 * m1 + (c1 * c1 + 2.0 * c2) * m2 - 2.0 * c1 * c2 * m3 + c2 * c2 * m4
    ra2 = m1 - 2.0 * c1 * m2 + (c1 * c1 + 2.0 * c2) * m3 - 2.0 * c1 * c2 * m4 + c2 * c2 * m5
    b1 = ratio(rr2, rr1)
    a2 = ratio(rr2, ra2 - b1 * ratio(rr2, a1))
    x0 = scale * (a0 + a1 * e + a2 * (1.0 + b1 * e))
    x1 = scale * scale * (-(c2 + a2 * (c1 + b1 * a0)))
    x2 = scale * scale * scale * (a2 * c2)
    out_ref[...] = x0 * v_ref[0] + x1 * v_ref[1] + x2 * v_ref[2]
    for base in range(14 - LATE):
        fluid_ref[base * 8:base * 8 + 8, :] = x0 * part_ref[0, base] + x1 * part_ref[1, base] + x2 * part_ref[2, base]
    keep.wait()

def flow(sizes, w, yld, force, xi, vel, mom, new, slots, counts, el):
    bary = bary_table()
    lc, lct, rg, rgt, small, ends, spread = field_consts()
    args = (small, w, force, yld, lc, rg, ends, spread, slots, counts, xi, vel, mom, new, lct, rgt, bary, el)
    vm = lambda *s: pltpu.VMEM(s, jnp.float32)
    sums = sizes[1] - 1 + sizes[0] * sizes[2] - 1
    whole = pl.BlockSpec(memory_space=pltpu.VMEM)
    kept = [pltpu.SMEM(t.shape, t.dtype) if t is counts else pltpu.VMEM(t.shape, t.dtype) for t in args]
    return pl.pallas_call(
        functools.partial(flow_kernel, sizes),
        out_shape=(jax.ShapeDtypeStruct((256, 128), jnp.float32), jax.ShapeDtypeStruct((6, 11, 8, 128), jnp.float32), jax.ShapeDtypeStruct((64, 128), jnp.float32),
                   jax.ShapeDtypeStruct((112 - 8 * LATE, 128), jnp.float32)),
        in_specs=[pl.BlockSpec(memory_space=pl.ANY)] * 18,
        out_specs=(whole, pl.BlockSpec(memory_space=pl.ANY), whole, whole),
        scratch_shapes=kept + [vm(3, 256, 128), vm(3, 256, 128), vm(3, 256, 128), vm(256, 128), vm(256, 128), vm(3, 2, 8, 128), vm(3, 4, 1, 128), vm(3, 2, 2, 1, 128),
                        vm(3, 2, 32, 128), vm(3, 2, 8, 128), vm(3, 4, 1, 128), vm(3, 2, 12, 1, 128), vm(8, 256), vm(2, 1, 128), vm(sums, 1, 128),
                        vm(6, 11, 8, 128), vm(64, 128), vm(6, 11, 8, 128), pltpu.VMEM((3, 128, 768), jnp.bfloat16), vm(2, 4, 64, 128), vm(3, 14, 8, 128),
                        pltpu.SemaphoreType.DMA((3, 26)), pltpu.SemaphoreType.DMA((3, 26)), pltpu.SemaphoreType.DMA((sums,)),
                        pltpu.SemaphoreType.DMA((sums,)), pltpu.SemaphoreType.DMA((6,)), pltpu.SemaphoreType.DMA((6,)), pltpu.SemaphoreType.DMA((18,)), pltpu.SemaphoreType.DMA],
        compiler_params=pltpu.CompilerParams(collective_id=0, has_side_effects=True),
        name="flow",
    )(*args)

def solution(mesh):
    sizes = (mesh.shape["ax"], mesh.shape["circ"], mesh.shape["gap"])

    def shards(w_old, yield_stress, force, xi, vel, mom, el, new, slots, counts):
        flat = lambda t: t.reshape(256, 128)
        xi, vel, mom = [t.reshape(3, 64, 128) for t in (xi, vel, mom)]
        w, arr, dep, fluid = flow(sizes, flat(w_old), flat(yield_stress), flat(force), xi, vel, mom, new.reshape(64, 128), slots.reshape(6, 8, 128), counts.reshape(6), el.reshape(64, 128))
        w_new, kept, arrived = finish(sizes, w, bary_table(), fluid, xi, vel, mom, dep, arr)
        return w_new.reshape(w_old.shape), kept.reshape(1, 1, 1, 9, 8192), arrived.reshape(1, 1, 1, 6, 9, 1024)

    spec = lambda n: P("ax", "circ", "gap", *([None] * n))
    return jax.shard_map(
        shards,
        mesh=mesh,
        in_specs=(spec(0), spec(0), spec(0), spec(2), spec(2), spec(2), spec(1), spec(1), spec(2), spec(1)),
        out_specs=(spec(0), spec(2), spec(3)),
        check_vma=False,
    )
```

```python
import functools
import jax, jax.numpy as jnp, numpy as np
from jax import lax
from jax.experimental import pallas as pl
from jax.experimental.pallas import tpu as pltpu
from jax.sharding import PartitionSpec as P

MESH = pl.DeviceIdType.MESH
GLL_NODES = np.array([-1.0,-0.8717401485096066,-0.5917001814331423,-0.2092992179024789,0.2092992179024789,0.5917001814331423,0.8717401485096066,1.0])
GLL_WEIGHTS = np.array([0.03571428571428571,0.2107042271435061,0.3411226924835044,0.4124587946587038,0.4124587946587038,0.3411226924835044,0.2107042271435061,0.03571428571428571])

def bary_weights():
    eye = np.eye(8, dtype=bool)
    diff = np.where(eye, 1.0, GLL_NODES[:, None] - GLL_NODES[None, :])
    return 1.0 / np.prod(diff, axis=1)

def pick(rows, lanes):
    return jnp.take_along_axis(rows, lanes, axis=1, mode="promise_in_bounds")

def pick_row(rows, at):
    return jnp.take_along_axis(rows, at, axis=0, mode="promise_in_bounds")

def leaving_row(fields, slots_ref, count, row, buf_ref):
    lane = lax.broadcasted_iota(jnp.int32, (8, 128), 1)
    for s in range(8):
        slot = jnp.broadcast_to(slots_ref[row, s:s + 1, :], (8, 128))
        block = lax.shift_right_logical(slot, 10)
        inner = lax.bitwise_and(lax.shift_right_logical(slot, 7), 7)
        within = lax.bitwise_and(slot, 127)
        live = (lane + s * 128 < count).astype(jnp.float32)
        for f, field in enumerate(fields):
            found = None
            for b in range(8):
                got = pick(field(b), within)
                found = got if found is None else jnp.where(block == b, got, found)
            found = pick_row(found, inner) * live
            buf_ref[row, f, s:s + 1, :] = found[0:1]
        buf_ref[row, 10, s:s + 1, :] = live[0:1]

def departed_flags(slots_ref, counts_ref):
    sub64 = lax.broadcasted_iota(jnp.int32, (64, 128), 0)
    sub128 = lax.broadcasted_iota(jnp.int32, (128, 128), 0)
    lanes = lax.broadcasted_iota(jnp.int32, (1, 128), 1)

    def one(row, total):
        count = counts_ref[row]
        blocks, places = [], []
        for s in range(8):
            slot = slots_ref[row, s:s + 1, :]
            block = jnp.where(lanes + s * 128 < count, lax.shift_right_logical(slot, 7), 64)
            within = lax.bitwise_and(slot, 127)
            blocks.append(jnp.where(sub64 == block, 1.0, 0.0).astype(jnp.bfloat16))
            places.append(jnp.where(sub128 == within, 1.0, 0.0).astype(jnp.bfloat16))
        return total + lax.dot_general(jnp.concatenate(blocks, 1), jnp.concatenate(places, 1), (((1,), (1,)), ((), ())), preferred_element_type=jnp.float32)

    return lax.fori_loop(0, 6, one, jnp.zeros((64, 128), jnp.float32))

def ladder(x):
    d = [x - np.float32(n) for n in GLL_NODES]
    pre = [None] * 8
    suf = [None] * 8
    pre[1] = d[0]
    for k in range(2, 8):
        pre[k] = pre[k - 1] * d[k - 1]
    suf[6] = d[7]
    for k in range(5, -1, -1):
        suf[k] = suf[k + 1] * d[k + 1]
    return [suf[0]] + [pre[k] * suf[k] for k in range(1, 7)] + [pre[7]]

LATE = 2

def bary_table():
    b = bary_weights()
    rows = (b[:, None, None] * np.ones((1, 4, 1)) * b[None, None, :]).reshape(256, 1)
    return np.ascontiguousarray(rows * np.tile(b, 16)[None, :], dtype=np.float32)

def make_table(table_ref, k, v, bary):
    v = (v * bary).reshape(16, 2, 8, 128)
    v = jnp.concatenate([v[:, 0].reshape(128, 128), v[:, 1].reshape(128, 128)], axis=1)
    high = v.astype(jnp.bfloat16)
    low = (v - high.astype(jnp.float32)).astype(jnp.bfloat16)
    table_ref[k, :, 0:256] = high
    table_ref[k, :, 256:512] = low
    table_ref[k, :, 512:768] = high

def sample(table_ref, first, count, ids, points, basis_ref, put):
    for d in range(2):
        for k, value in enumerate(ladder(points[d])):
            basis_ref[d, k * 8:k * 8 + 8, :] = value
    for k, value in enumerate(ladder(points[2])):
        rounded = value.astype(jnp.bfloat16).astype(jnp.float32)
        basis_ref[2, k * 8:k * 8 + 8, :] = rounded
        basis_ref[3, k * 8:k * 8 + 8, :] = value - rounded
    second_half = jnp.where(lax.broadcasted_iota(jnp.int32, (16, 128), 0) >= 8, 1.0, 0.0)
    zero = jnp.zeros((16, 128), jnp.bfloat16)
    circ = lax.shift_right_logical(ids, 5)
    radial = lax.bitwise_and(ids, 31).astype(jnp.float32)
    table = table_ref[first:first + count].reshape(count * 128, 768)
    for q in range(4):
        right, weights = [], []
        for s in (2 * q, 2 * q + 1):
            mine = (jnp.broadcast_to(radial[s:s + 1], (16, 128)) - second_half).astype(jnp.bfloat16)
            high16 = jnp.concatenate([basis_ref[2, pl.ds(s, 8, stride=8), :]] * 2, axis=0).astype(jnp.bfloat16)
            low16 = jnp.concatenate([basis_ref[3, pl.ds(s, 8, stride=8), :]] * 2, axis=0).astype(jnp.bfloat16)
            same = [mine == jnp.bfloat16(2 * t) for t in range(16)]
            b_high = jnp.concatenate([jnp.where(m, high16, zero) for m in same], axis=0)
            b_low = jnp.concatenate([jnp.where(m, low16, zero) for m in same], axis=0)
            right.append(jnp.concatenate([b_high, b_high, b_low], axis=0))
            second = basis_ref[1, pl.ds(s, 8, stride=8), :]
            cc = jnp.broadcast_to(circ[s:s + 1], (8, 128))
            weights.append([jnp.where(cc == c, second, 0.0) for c in range(2)])
        values = jnp.dot(table, jnp.concatenate(right, axis=1), preferred_element_type=jnp.float32)
        for h, s in enumerate((2 * q, 2 * q + 1)):
            for n in range(count):
                total = None
                for i in range(8):
                    line = None
                    for c in range(2):
                        at = n * 128 + i * 16 + c * 8
                        term = values[at:at + 8, h * 128:h * 128 + 128] * weights[h][c]
                        line = term if line is None else line + term
                    line = line * jnp.broadcast_to(basis_ref[0, i * 8 + s:i * 8 + s + 1, :], (8, 128))
                    total = line if total is None else total + line
                put(first + n, s, jnp.sum(total, axis=0, keepdims=True))

def finish_kernel(sizes, w_ref, bary_ref, fluid_ref, xi_ref, vel_ref, mom_ref, dep_ref, arr_ref, w_out, kept_ref, arrived_ref, table_ref, basis_ref, late_ref):
    w_out[...] = w_ref[...]
    make_table(table_ref, 0, w_ref[...], bary_ref[...])

    def keeper(row):
        def put(k, s, value):
            late_ref[row, s:s + 1, :] = value

        return put

    for row in range(LATE):
        at = 6 - LATE + row
        sample(table_ref, 0, 1, arr_ref[at, 9].astype(jnp.int32), [arr_ref[at, d] for d in range(3)], basis_ref.at[row], keeper(row))
    ax, gap = lax.axis_index("ax"), lax.axis_index("gap")
    absent = [ax == 0, ax == sizes[0] - 1, None, None, gap == 0, gap == sizes[2] - 1]

    def update(xi, vel, fluid):
        axial = vel[0] + 0.4 * (fluid - vel[0])
        circ = vel[1] * (1.0 - 0.4)
        radial = vel[2] * (1.0 - 0.4)
        return [xi[0] + 0.25 * axial, xi[1] + 0.25 * circ, xi[2] + 1.0 * radial, axial, circ, radial]

    stay = 1.0 - dep_ref[...]
    state = update([xi_ref[d] for d in range(3)], [vel_ref[d] for d in range(3)], fluid_ref[0:64]) + [mom_ref[d] for d in range(3)]
    for at, value in enumerate(state):
        kept_ref[at] = value * stay
    for row in range(6):
        state = [arr_ref[row, d] for d in range(11)]
        live = state[10] if absent[row] is None else state[10] * jnp.where(absent[row], 0.0, 1.0)
        fluid = fluid_ref[64 + 8 * row:72 + 8 * row] if row < 6 - LATE else late_ref[row - 6 + LATE]
        for at, value in enumerate(update(state[0:3], state[3:6], fluid) + state[6:9]):
            arrived_ref[row, at] = value * live

def finish(sizes, w, bary, fluid, xi, vel, mom, dep, arr):
    return pl.pallas_call(
        functools.partial(finish_kernel, sizes),
        out_shape=(jax.ShapeDtypeStruct((256, 128), jnp.float32), jax.ShapeDtypeStruct((9, 64, 128), jnp.float32), jax.ShapeDtypeStruct((6, 9, 8, 128), jnp.float32)),
        in_specs=[pl.BlockSpec(memory_space=pltpu.VMEM)] * 8,
        out_specs=(pl.BlockSpec(memory_space=pltpu.VMEM),) * 3,
        scratch_shapes=[pltpu.VMEM((1, 128, 768), jnp.bfloat16), pltpu.VMEM((LATE, 4, 64, 128), jnp.float32), pltpu.VMEM((LATE, 8, 128), jnp.float32)],
        name="finish",
    )(w, bary, fluid, xi, vel, mom, dep, arr)


def diff_table():
    b = bary_weights()
    eye = np.eye(8, dtype=bool)
    diff = np.where(eye, 1.0, GLL_NODES[:, None] - GLL_NODES[None, :])
    off = np.where(eye, 0.0, b[None, :] / b[:, None] / diff)
    return (off - np.eye(8) * np.sum(off, axis=1)[:, None]).astype(np.float32)

def pieces(a, count=2):
    parts = []
    rest = a.astype(np.float32)
    for _ in range(count):
        part = rest.astype(jnp.bfloat16)
        parts.append(part)
        rest = rest - part.astype(np.float32)
    return parts

def field_consts():
    d = diff_table()
    eye = np.eye(16, dtype=np.float32)

    def left(m):
        h, l = pieces(np.kron(eye, m))
        return np.block([[h, h], [l, l]])

    def right(m):
        h, l = pieces(4.0 * np.kron(eye, m))
        return np.block([[h, l], [h, l]])

    w8 = GLL_WEIGHTS.astype(np.float32)
    half = np.where((np.arange(8) == 0) | (np.arange(8) == 7), 0.5, 1.0)
    r = np.arange(32)[:, None] + np.zeros((1, 128))
    c = np.arange(128)[None, :] + np.zeros((32, 1))
    small = np.stack([np.tile(w8, 4)[:, None] * np.tile(w8, 16)[None, :], np.tile(half, 4)[:, None] * np.tile(half, 16)[None, :],
                      (r % 8 == 0) & (r > 0), (r % 8 == 7) & (r < 31), (c % 8 == 0) & (c > 0), (c % 8 == 7) & (c < 127)]).astype(np.float32)
    ends = np.zeros((8, 384), np.float32)
    for piece in range(3):
        ends[0, piece * 128] = 1.0
        ends[1, piece * 128 + 127] = 1.0
    spread = np.zeros((32, 128), np.float32)
    for piece in range(3):
        spread[piece * 8, 0] = 1.0
        spread[piece * 8 + 1, 127] = 1.0
    bf = lambda t: np.ascontiguousarray(t).astype(jnp.bfloat16)
    return [bf(left(d)), bf(left(d.T)), bf(right(d.T)), bf(right(d)), small, bf(ends), bf(spread)]

def halves(x):
    high = x.astype(jnp.bfloat16)
    return high, (x - high.astype(jnp.float32)).astype(jnp.bfloat16)

def thirds(x):
    high, rest = x.astype(jnp.bfloat16), None
    rest = x - high.astype(jnp.float32)
    mid = rest.astype(jnp.bfloat16)
    return high, mid, (rest - mid.astype(jnp.float32)).astype(jnp.bfloat16)

def mix(a, b, dims=((1,), (0,))):
    return lax.dot_general(a, b, (dims, ((), ())), preferred_element_type=jnp.float32)

def along_circ(x, left):
    x = jnp.concatenate([x[0:128], x[128:256]], axis=1)
    y = mix(left, jnp.concatenate(halves(x), axis=0))
    y = y[0:128] + y[128:256]
    return jnp.concatenate([y[:, 0:128], y[:, 128:256]], axis=0)

def along_gap(x, right):
    y = mix(jnp.concatenate(halves(x), axis=1), right)
    return y[:, 0:128] + y[:, 128:256]

def along_ax(x, d):
    x = [x[i * 32:i * 32 + 32] for i in range(8)]
    even = [x[j] + x[7 - j] for j in range(4)]
    odd = [x[j] - x[7 - j] for j in range(4)]
    out = [None] * 8
    for i in range(4):
        a = b = None
        for j in range(4):
            p = np.float32(0.5 * (float(d[i, j]) - float(d[i, 7 - j]))) * odd[j]
            q = np.float32(0.5 * (float(d[i, j]) + float(d[i, 7 - j]))) * even[j]
            a = p if a is None else a + p
            b = q if b is None else b + q
        out[i] = a + b
        out[7 - i] = a - b
    return jnp.concatenate(out, axis=0)

def flow_kernel(sizes, *refs):
    sources, (out_ref, arr_out, dep_ref, fluid_ref), held, rest = refs[0:18], refs[18:22], refs[22:40], refs[40:]
    small_ref, w_ref, force_ref, ends_ref, yield_ref, lc_ref, rg_ref, spread_ref, slots_ref, counts_ref, xi_ref, vel_ref, mom_ref, new_ref, lct_ref, rgt_ref, bary_ref, el_ref = held
    (v_ref, f_ref, z_ref, quad_ref, stiff_ref, edge_c, edge_e, edge_g, got_a, got_c, got_e, got_g, pair_ref, sum_ref, got_sum, buf_ref, id_ref, arr_ref, table_ref, basis_ref, part_ref,
     send_sem, recv_sem, sum_send, sum_recv, mig_send, mig_recv, load_sem, keep_sem) = rest
    loads = [pltpu.make_async_copy(source, mine, load_sem.at[i]) for i, (source, mine) in enumerate(zip(sources, held))]
    for load in loads:
        load.start()
    n_ax, n_circ, n_gap = sizes
    d8 = diff_table()
    ax, circ, gap = lax.axis_index("ax"), lax.axis_index("circ"), lax.axis_index("gap")

    def at(da=0, dc=0, dg=0):
        place = {}
        if da:
            place["ax"] = lax.rem(ax + (da + n_ax), n_ax)
        if dc:
            place["circ"] = lax.rem(circ + (dc + n_circ), n_circ)
        if dg:
            place["gap"] = lax.rem(gap + (dg + n_gap), n_gap)
        return place

    around = [(a, c, g) for a in (0, -1, 1) for c in (0, -1, 1) for g in (0, -1, 1) if (a, c, g) != (0, 0, 0)]
    plane = [(a, g) for a in range(n_ax) for g in range(n_gap) if (a, g) != (0, 0)]
    near = [(a % n_ax, g % n_gap) for a in (0, -1, 1) for g in (0, -1, 1)]
    peers = [at(*d) for d in around] + [at(dc=o) for o in range(2, n_circ - 1)] + [at(da=o[0], dg=o[1]) for o in plane if o not in near]
    hops = lambda d, n: min(d, n - d)
    far_circ = sorted(range(1, n_circ), key=lambda o: -hops(o, n_circ))
    far_plane = sorted(plane, key=lambda o: -(hops(o[0], n_ax) + hops(o[1], n_gap)))
    barrier = pltpu.get_barrier_semaphore()
    for peer in peers:
        pl.semaphore_signal(barrier, inc=1, device_id=peer, device_id_type=MESH)

    for load in loads[0:4]:
        load.wait()
    weights = GLL_WEIGHTS.astype(np.float32)
    quad = jnp.concatenate([small_ref[0] * weights[i] for i in range(8)], axis=0)
    quad_ref[...] = quad
    col = lax.broadcasted_iota(jnp.int32, (32, 128), 1)
    at_wall = ((col == 0) & (gap == 0)) | ((col == 127) & (gap == n_gap - 1))
    wall = jnp.where(at_wall, 0.0, 1.0)
    share = small_ref[1] * jnp.where(at_wall, 2.0, 1.0)
    low_ax = jnp.where(ax == 0, 0.0, 1.0)
    high_ax = jnp.where(ax == n_ax - 1, 0.0, 1.0)
    low_gap = jnp.where(gap == 0, 0.0, 1.0)
    high_gap = jnp.where(gap == n_gap - 1, 0.0, 1.0)
    ax_share = [jnp.where(ax == 0, 1.0, 0.5)] + [1.0] * 6 + [jnp.where(ax == n_ax - 1, 1.0, 0.5)]
    pair_ref[...] = jnp.zeros((8, 256), jnp.float32)

    def every(tile):
        return jnp.concatenate([tile] * 8, axis=0)

    def gather_inner(f):
        f = f + every(small_ref[2]) * pltpu.roll(f, 1, 0) + every(small_ref[3]) * pltpu.roll(f, 255, 0)
        return f + every(small_ref[4]) * pltpu.roll(f, 1, 1) + every(small_ref[5]) * pltpu.roll(f, 127, 1)

    def remote(src, dst, k, t, place):
        return pltpu.make_async_remote_copy(src_ref=src, dst_ref=dst, send_sem=send_sem.at[k, t], recv_sem=recv_sem.at[k, t],
                                            device_id=place, device_id_type=MESH)

    def stage(k, f):
        f = gather_inner(f)
        f_ref[k] = f
        z_ref[k] = f
        edge_c[k, 0] = f_ref[k, pl.ds(0, 8, stride=32), :]
        edge_c[k, 1] = f_ref[k, pl.ds(31, 8, stride=32), :]
        for e, at_row in enumerate((0, 31, 224, 255)):
            edge_e[k, e] = f_ref[k, at_row:at_row + 1, :]
        return mix(ends_ref[...], jnp.concatenate(thirds(f), axis=1), ((1,), (1,)))

    def send(k, faces):
        copies = [remote(edge_e.at[k, e], got_e.at[k, 3 - e], k, 4 + e, at(da=1 if e >= 2 else -1, dc=1 if e % 2 else -1)) for e in range(4)]
        copies += [remote(edge_c.at[k, 0], got_c.at[k, 1], k, 2, at(dc=-1)),
                   remote(edge_c.at[k, 1], got_c.at[k, 0], k, 3, at(dc=1)),
                   remote(f_ref.at[k, 0:32], got_a.at[k, 1], k, 0, at(da=-1)),
                   remote(f_ref.at[k, 224:256], got_a.at[k, 0], k, 1, at(da=1))]
        for s in range(2):
            for h in range(2):
                edge_g[k, s, h] = faces[s:s + 1, h * 128:h * 128 + 128]
        later = []
        for s in range(2):
            dg = 1 if s else -1
            t = 8 + 9 * s
            for a in (-1, 1):
                for c in (-1, 1):
                    slot = 8 + (2 if a < 0 else 0) + (1 if c < 0 else 0)
                    later.append(remote(edge_g.at[k, s, 1 if a > 0 else 0], got_g.at[k, 1 - s, slot], k, t + slot - 3, at(da=a, dc=c, dg=dg)))
            for a in (-1, 1):
                slot = 7 if a < 0 else 6
                later.append(remote(edge_g.at[k, s, 1 if a > 0 else 0], got_g.at[k, 1 - s, slot], k, t + slot - 3, at(da=a, dg=dg)))
            for c in (0, -1, 1):
                slot = {0: 0, 1: 1, -1: 2}[c]
                later.append(remote(edge_g.at[k, s], got_g.at[k, 1 - s, 2 * slot:2 * slot + 2], k, t + slot, at(dc=c, dg=dg)))
        for copy in later + copies:
            copy.start()
        return copies + later

    lane = lax.broadcasted_iota(jnp.int32, (1, 128), 1)
    place_of = lax.bitwise_and(lane, 31)

    def receive(k, copies):
        for copy in copies:
            copy.wait_recv()
        z_ref[k, 0:32, :] = z_ref[k, 0:32, :] + got_a[k, 0] * low_ax
        z_ref[k, 224:256, :] = z_ref[k, 224:256, :] + got_a[k, 1] * high_ax
        z_ref[k, pl.ds(0, 8, stride=32), :] = z_ref[k, pl.ds(0, 8, stride=32), :] + got_c[k, 0]
        z_ref[k, pl.ds(31, 8, stride=32), :] = z_ref[k, pl.ds(31, 8, stride=32), :] + got_c[k, 1]
        for e, at_row in enumerate((0, 31, 224, 255)):
            z_ref[k, at_row:at_row + 1, :] = z_ref[k, at_row:at_row + 1, :] + got_e[k, e] * (low_ax if e < 2 else high_ax)
        for s in range(2):
            def moved(slot, shift, keep):
                return jnp.where(keep, pltpu.roll(got_g[k, s, slot], shift, 1), 0.0)

            low = moved(6, 32, lane < 32) + moved(8, 1, lane == 0) + moved(9, 63, lane == 31)
            high = moved(7, 96, lane >= 96) + moved(10, 65, lane == 96) + moved(11, 127, lane == 127)
            sides = []
            for h, extra in ((0, low * low_ax), (1, high * high_ax)):
                sides.append(got_g[k, s, h] + moved(2 + h, 97, place_of == 0) + moved(4 + h, 31, place_of == 31) + extra)
            for h in range(2):
                pair_ref[s:s + 1, h * 128:h * 128 + 128] = sides[h] * (high_gap if s else low_gap)
        pair = pair_ref[...]
        pair = jnp.concatenate(thirds(pair) + (jnp.zeros((8, 256), jnp.bfloat16),), axis=0)
        v_ref[k] = (z_ref[k] + mix(pair, spread_ref[...], ((0,), (0,)))) * every(wall)

    fields = [lambda b, ref=ref, d=d: ref[d, b * 8:b * 8 + 8, :] for ref in (xi_ref, vel_ref, mom_ref) for d in range(3)]
    fields.append(lambda b: id_ref[b * 8:b * 8 + 8, :])
    moves = [at(da=1), at(da=-1), at(dc=1), at(dc=-1), at(dg=1), at(dg=-1)]
    moving = [pltpu.make_async_remote_copy(src_ref=buf_ref.at[r], dst_ref=arr_ref.at[r], send_sem=mig_send.at[r], recv_sem=mig_recv.at[r],
                                           device_id=place, device_id_type=MESH) for r, place in enumerate(moves)]

    def pack_rows(first, last):
        @pl.loop(first, last)
        def _(row):
            leaving_row(fields, slots_ref, counts_ref[row], row, buf_ref)

        for copy in moving[first:last]:
            copy.start()

    faces = stage(0, quad * 0.25 * (4.0 * w_ref[...] + force_ref[...]))
    pl.semaphore_wait(barrier, len(peers))
    for load in loads[4:7]:
        load.wait()
    copies = send(0, faces)
    w = w_ref[...]
    slope_a, slope_c, slope_g = along_ax(w, d8), along_circ(w, lc_ref[...]), along_gap(w, rg_ref[...])
    squares = 1.0 + slope_a * slope_a + slope_c * slope_c + slope_g * slope_g
    stiff_ref[...] = quad * 0.25 * (0.05 + yield_ref[...] / jnp.sqrt(squares))
    for load in loads[7:]:
        load.wait()
    id_ref[...] = new_ref[...].astype(jnp.float32)
    pack_rows(0, 3)
    dep_ref[...] = departed_flags(slots_ref, counts_ref)
    receive(0, copies)

    def keeper(base, half):
        def put(k, s, value):
            part_ref[k, base, s:s + 1, :] = value

        return put

    def sample_kept(first, count, block, half):
        rows = pl.ds(pl.multiple_of(block * 8, 8), 8)
        sample(table_ref, first, count, el_ref[rows, :], [xi_ref[d, rows, :] for d in range(3)], basis_ref.at[half], keeper(block, half))

    def sample_arrived(first, count, row, half):
        sample(table_ref, first, count, arr_ref[row, 9].astype(jnp.int32), [arr_ref[row, d] for d in range(3)], basis_ref.at[half], keeper(row + 8, half))

    def sample_pairs(first, count):
        @pl.loop(0, 3)
        def _(two):
            for half in range(2):
                sample_kept(first, count, two * 2 + half, half)

    def total(x):
        return jnp.sum(x.reshape(32, 8, 128), axis=0)

    sums = []
    for k in range(3):
        v = v_ref[k]
        stiff = stiff_ref[...]
        slope_a, slope_c, slope_g = along_ax(v, d8), along_circ(v, lc_ref[...]), along_gap(v, rg_ref[...])
        if k < 2:
            image = quad_ref[...] * v + along_ax(stiff * slope_a, d8.T)
            image = image + along_circ(stiff * slope_c, lct_ref[...]) + along_gap(stiff * slope_g, rgt_ref[...])
            faces = stage(k + 1, image)
            sent, copies = copies, send(k + 1, faces)
        square = v * v
        sums.append(total(jnp.concatenate([square[i * 32:i * 32 + 32] * (share * ax_share[i]) for i in range(8)], axis=0)))
        sums.append(total(quad_ref[...] * square + stiff * (slope_a * slope_a + slope_c * slope_c + slope_g * slope_g)))
        if k == 0:
            pack_rows(3, 6)
            make_table(table_ref, 0, v_ref[0], bary_ref[...])
            sample_kept(0, 1, 6, 0)
            sample_kept(0, 1, 7, 1)
        if k == 1:
            make_table(table_ref, 1, v_ref[1], bary_ref[...])
            sample_pairs(0, 2)
        if k < 2:
            for copy in sent:
                copy.wait_send()
            receive(k + 1, copies)

    sub = lax.broadcasted_iota(jnp.int32, (8, 128), 0)
    part = lax.broadcasted_iota(jnp.int32, (8, 128), 1) // 16
    rows = jnp.zeros((8, 128), jnp.float32)
    for m, value in enumerate(sums):
        rows = jnp.where(sub == m, jnp.broadcast_to(jnp.sum(value, axis=0, keepdims=True), (8, 128)), rows)
    for shift in (64, 32, 16):
        rows = rows + pltpu.roll(rows, shift, 1)
    line = jnp.sum(jnp.where(sub == part, rows, 0.0), axis=0, keepdims=True)
    keep = pltpu.make_async_copy(arr_ref, arr_out, keep_sem)
    slot = 0
    for step, places in enumerate(([at(dc=o) for o in far_circ], [at(da=a, dg=g) for a, g in far_plane])):
        sum_ref[step] = line
        rounds = []
        for place in places:
            rounds.append(pltpu.make_async_remote_copy(src_ref=sum_ref.at[step], dst_ref=got_sum.at[slot], send_sem=sum_send.at[slot],
                                                       recv_sem=sum_recv.at[slot], device_id=place, device_id_type=MESH))
            slot += 1
        for copy in rounds:
            copy.start()
        if step == 0:
            for copy in copies:
                copy.wait_send()
            make_table(table_ref, 2, v_ref[2], bary_ref[...])
            sample_pairs(2, 1)
            sample_kept(1, 2, 6, 0)
        else:
            for copy in moving:
                copy.wait()
            keep.start()
            sample_arrived(0, 3, 0, 0)
            sample_arrived(0, 3, 1, 1)
            sample_arrived(0, 3, 2, 0)
            sample_arrived(0, 3, 3, 1)
            sample_kept(1, 2, 7, 0)
        for copy in rounds:
            copy.wait_recv()
        for o in range(len(places)):
            line = line + got_sum[slot - 1 - o]
        for copy in rounds:
            copy.wait_send()
    m = jnp.sum(jnp.where(sub == part, jnp.broadcast_to(line, (8, 128)), 0.0), axis=1, keepdims=True)
    m0, m1, m2, m3, m4, m5 = [m[i:i + 1, :] for i in range(6)]
    scale = m0 / m1
    m1 = m1 * scale
    m2 = m2 * scale * scale
    m3 = m3 * scale * scale * scale
    m4 = m4 * scale * scale * scale * scale
    m5 = m5 * scale * scale * scale * scale * scale

    def ratio(a, b):
        return jnp.where((a > 0.0) & (b > 0.0), a / b, 0.0)

    a0 = m0 / m1
    rr1 = a0 * a0 * m2 - m0
    e = 1.0 + rr1 / m0
    p1 = e * e * m1 - 2.0 * e * a0 * m2 + a0 * a0 * m3
    a1 = ratio(rr1, p1)
    c1 = a0 + a1 * e
    c2 = a0 * a1
    rr2 = m0 - 2.0 * c1 * m1 + (c1 * c1 + 2.0 * c2) * m2 - 2.0 * c1 * c2 * m3 + c2 * c2 * m4
    ra2 = m1 - 2.0 * c1 * m2 + (c1 * c1 + 2.0 * c2) * m3 - 2.0 * c1 * c2 * m4 + c2 * c2 * m5
    b1 = ratio(rr2, rr1)
    a2 = ratio(rr2, ra2 - b1 * ratio(rr2, a1))
    x0 = scale * (a0 + a1 * e + a2 * (1.0 + b1 * e))
    x1 = scale * scale * (-(c2 + a2 * (c1 + b1 * a0)))
    x2 = scale * scale * scale * (a2 * c2)
    out_ref[...] = x0 * v_ref[0] + x1 * v_ref[1] + x2 * v_ref[2]
    for base in range(14 - LATE):
        fluid_ref[base * 8:base * 8 + 8, :] = x0 * part_ref[0, base] + x1 * part_ref[1, base] + x2 * part_ref[2, base]
    keep.wait()

def flow(sizes, w, yld, force, xi, vel, mom, new, slots, counts, el):
    bary = bary_table()
    lc, lct, rg, rgt, small, ends, spread = field_consts()
    args = (small, w, force, ends, yld, lc, rg, spread, slots, counts, xi, vel, mom, new, lct, rgt, bary, el)
    vm = lambda *s: pltpu.VMEM(s, jnp.float32)
    sums = sizes[1] - 1 + sizes[0] * sizes[2] - 1
    whole = pl.BlockSpec(memory_space=pltpu.VMEM)
    kept = [pltpu.SMEM(t.shape, t.dtype) if t is counts else pltpu.VMEM(t.shape, t.dtype) for t in args]
    return pl.pallas_call(
        functools.partial(flow_kernel, sizes),
        out_shape=(jax.ShapeDtypeStruct((256, 128), jnp.float32), jax.ShapeDtypeStruct((6, 11, 8, 128), jnp.float32), jax.ShapeDtypeStruct((64, 128), jnp.float32),
                   jax.ShapeDtypeStruct((112 - 8 * LATE, 128), jnp.float32)),
        in_specs=[pl.BlockSpec(memory_space=pl.ANY)] * 18,
        out_specs=(whole, pl.BlockSpec(memory_space=pl.ANY), whole, whole),
        scratch_shapes=kept + [vm(3, 256, 128), vm(3, 256, 128), vm(3, 256, 128), vm(256, 128), vm(256, 128), vm(3, 2, 8, 128), vm(3, 4, 1, 128), vm(3, 2, 2, 1, 128),
                        vm(3, 2, 32, 128), vm(3, 2, 8, 128), vm(3, 4, 1, 128), vm(3, 2, 12, 1, 128), vm(8, 256), vm(2, 1, 128), vm(sums, 1, 128),
                        vm(6, 11, 8, 128), vm(64, 128), vm(6, 11, 8, 128), pltpu.VMEM((3, 128, 768), jnp.bfloat16), vm(2, 4, 64, 128), vm(3, 14, 8, 128),
                        pltpu.SemaphoreType.DMA((3, 26)), pltpu.SemaphoreType.DMA((3, 26)), pltpu.SemaphoreType.DMA((sums,)),
                        pltpu.SemaphoreType.DMA((sums,)), pltpu.SemaphoreType.DMA((6,)), pltpu.SemaphoreType.DMA((6,)), pltpu.SemaphoreType.DMA((18,)), pltpu.SemaphoreType.DMA],
        compiler_params=pltpu.CompilerParams(collective_id=0, has_side_effects=True),
        name="flow",
    )(*args)

def solution(mesh):
    sizes = (mesh.shape["ax"], mesh.shape["circ"], mesh.shape["gap"])

    def shards(w_old, yield_stress, force, xi, vel, mom, el, new, slots, counts):
        flat = lambda t: t.reshape(256, 128)
        xi, vel, mom = [t.reshape(3, 64, 128) for t in (xi, vel, mom)]
        w, arr, dep, fluid = flow(sizes, flat(w_old), flat(yield_stress), flat(force), xi, vel, mom, new.reshape(64, 128), slots.reshape(6, 8, 128), counts.reshape(6), el.reshape(64, 128))
        w_new, kept, arrived = finish(sizes, w, bary_table(), fluid, xi, vel, mom, dep, arr)
        return w_new.reshape(w_old.shape), kept.reshape(1, 1, 1, 9, 8192), arrived.reshape(1, 1, 1, 6, 9, 1024)

    spec = lambda n: P("ax", "circ", "gap", *([None] * n))
    return jax.shard_map(
        shards,
        mesh=mesh,
        in_specs=(spec(0), spec(0), spec(0), spec(2), spec(2), spec(2), spec(1), spec(1), spec(2), spec(1)),
        out_specs=(spec(0), spec(2), spec(3)),
        check_vma=False,
    )
```

```python
import functools
import jax, jax.numpy as jnp, numpy as np
from jax import lax
from jax.experimental import pallas as pl
from jax.experimental.pallas import tpu as pltpu
from jax.sharding import PartitionSpec as P

MESH = pl.DeviceIdType.MESH
GLL_NODES = np.array([-1.0,-0.8717401485096066,-0.5917001814331423,-0.2092992179024789,0.2092992179024789,0.5917001814331423,0.8717401485096066,1.0])
GLL_WEIGHTS = np.array([0.03571428571428571,0.2107042271435061,0.3411226924835044,0.4124587946587038,0.4124587946587038,0.3411226924835044,0.2107042271435061,0.03571428571428571])

def bary_weights():
    eye = np.eye(8, dtype=bool)
    diff = np.where(eye, 1.0, GLL_NODES[:, None] - GLL_NODES[None, :])
    return 1.0 / np.prod(diff, axis=1)

def pick(rows, lanes):
    return jnp.take_along_axis(rows, lanes, axis=1, mode="promise_in_bounds")

def pick_row(rows, at):
    return jnp.take_along_axis(rows, at, axis=0, mode="promise_in_bounds")

def leaving_row(fields, slots_ref, count, row, buf_ref):
    lane = lax.broadcasted_iota(jnp.int32, (8, 128), 1)
    for s in range(8):
        slot = jnp.broadcast_to(slots_ref[row, s:s + 1, :], (8, 128))
        block = lax.shift_right_logical(slot, 10)
        inner = lax.bitwise_and(lax.shift_right_logical(slot, 7), 7)
        within = lax.bitwise_and(slot, 127)
        live = (lane + s * 128 < count).astype(jnp.float32)
        for f, field in enumerate(fields):
            found = None
            for b in range(8):
                got = pick(field(b), within)
                found = got if found is None else jnp.where(block == b, got, found)
            found = pick_row(found, inner) * live
            buf_ref[row, f, s:s + 1, :] = found[0:1]
        buf_ref[row, 10, s:s + 1, :] = live[0:1]

def departed_flags(slots_ref, counts_ref):
    sub64 = lax.broadcasted_iota(jnp.int32, (64, 128), 0)
    sub128 = lax.broadcasted_iota(jnp.int32, (128, 128), 0)
    lanes = lax.broadcasted_iota(jnp.int32, (1, 128), 1)

    def one(row, total):
        count = counts_ref[row]
        blocks, places = [], []
        for s in range(8):
            slot = slots_ref[row, s:s + 1, :]
            block = jnp.where(lanes + s * 128 < count, lax.shift_right_logical(slot, 7), 64)
            within = lax.bitwise_and(slot, 127)
            blocks.append(jnp.where(sub64 == block, 1.0, 0.0).astype(jnp.bfloat16))
            places.append(jnp.where(sub128 == within, 1.0, 0.0).astype(jnp.bfloat16))
        return total + lax.dot_general(jnp.concatenate(blocks, 1), jnp.concatenate(places, 1), (((1,), (1,)), ((), ())), preferred_element_type=jnp.float32)

    return lax.fori_loop(0, 6, one, jnp.zeros((64, 128), jnp.float32))

def ladder(x):
    d = [x - np.float32(n) for n in GLL_NODES]
    pre = [None] * 8
    suf = [None] * 8
    pre[1] = d[0]
    for k in range(2, 8):
        pre[k] = pre[k - 1] * d[k - 1]
    suf[6] = d[7]
    for k in range(5, -1, -1):
        suf[k] = suf[k + 1] * d[k + 1]
    return [suf[0]] + [pre[k] * suf[k] for k in range(1, 7)] + [pre[7]]

LATE = 2

def bary_table():
    b = bary_weights()
    rows = (b[:, None, None] * np.ones((1, 4, 1)) * b[None, None, :]).reshape(256, 1)
    return np.ascontiguousarray(rows * np.tile(b, 16)[None, :], dtype=np.float32)

def make_table(table_ref, k, v, bary):
    v = (v * bary).reshape(16, 2, 8, 128)
    v = jnp.concatenate([v[:, 0].reshape(128, 128), v[:, 1].reshape(128, 128)], axis=1)
    high = v.astype(jnp.bfloat16)
    low = (v - high.astype(jnp.float32)).astype(jnp.bfloat16)
    table_ref[k, :, 0:256] = high
    table_ref[k, :, 256:512] = low
    table_ref[k, :, 512:768] = high

def sample(table_ref, first, count, ids, points, basis_ref, put):
    for d in range(2):
        for k, value in enumerate(ladder(points[d])):
            basis_ref[d, k * 8:k * 8 + 8, :] = value
    for k, value in enumerate(ladder(points[2])):
        rounded = value.astype(jnp.bfloat16).astype(jnp.float32)
        basis_ref[2, k * 8:k * 8 + 8, :] = rounded
        basis_ref[3, k * 8:k * 8 + 8, :] = value - rounded
    second_half = jnp.where(lax.broadcasted_iota(jnp.int32, (16, 128), 0) >= 8, 1.0, 0.0)
    zero = jnp.zeros((16, 128), jnp.bfloat16)
    circ = lax.shift_right_logical(ids, 5)
    radial = lax.bitwise_and(ids, 31).astype(jnp.float32)
    table = table_ref[first:first + count].reshape(count * 128, 768)
    for q in range(4):
        right, weights = [], []
        for s in (2 * q, 2 * q + 1):
            mine = (jnp.broadcast_to(radial[s:s + 1], (16, 128)) - second_half).astype(jnp.bfloat16)
            high16 = jnp.concatenate([basis_ref[2, pl.ds(s, 8, stride=8), :]] * 2, axis=0).astype(jnp.bfloat16)
            low16 = jnp.concatenate([basis_ref[3, pl.ds(s, 8, stride=8), :]] * 2, axis=0).astype(jnp.bfloat16)
            same = [mine == jnp.bfloat16(2 * t) for t in range(16)]
            b_high = jnp.concatenate([jnp.where(m, high16, zero) for m in same], axis=0)
            b_low = jnp.concatenate([jnp.where(m, low16, zero) for m in same], axis=0)
            right.append(jnp.concatenate([b_high, b_high, b_low], axis=0))
            second = basis_ref[1, pl.ds(s, 8, stride=8), :]
            cc = jnp.broadcast_to(circ[s:s + 1], (8, 128))
            weights.append([jnp.where(cc == c, second, 0.0) for c in range(2)])
        values = jnp.dot(table, jnp.concatenate(right, axis=1), preferred_element_type=jnp.float32)
        for h, s in enumerate((2 * q, 2 * q + 1)):
            for n in range(count):
                total = None
                for i in range(8):
                    line = None
                    for c in range(2):
                        at = n * 128 + i * 16 + c * 8
                        term = values[at:at + 8, h * 128:h * 128 + 128] * weights[h][c]
                        line = term if line is None else line + term
                    line = line * jnp.broadcast_to(basis_ref[0, i * 8 + s:i * 8 + s + 1, :], (8, 128))
                    total = line if total is None else total + line
                put(first + n, s, jnp.sum(total, axis=0, keepdims=True))

def finish_kernel(sizes, *refs):
    sources, outs, held, (kept_ref, arrived_ref, table_ref, basis_ref, late_ref, load_sem, save_sem) = refs[0:8], refs[8:11], refs[11:19], refs[19:]
    fluid_ref, vel_ref, xi_ref, mom_ref, dep_ref, w_ref, bary_ref, arr_ref = held
    loads = [pltpu.make_async_copy(source, mine, load_sem.at[i]) for i, (source, mine) in enumerate(zip(sources, held))]
    for load in loads:
        load.start()
    saves = [pltpu.make_async_copy(mine, out, save_sem.at[i]) for i, (mine, out) in enumerate(zip((w_ref, kept_ref, arrived_ref), outs))]

    def keeper(row):
        def put(k, s, value):
            late_ref[row, s:s + 1, :] = value

        return put

    ax, gap = lax.axis_index("ax"), lax.axis_index("gap")
    absent = [ax == 0, ax == sizes[0] - 1, None, None, gap == 0, gap == sizes[2] - 1]

    def update(xi, vel, fluid):
        axial = vel[0] + 0.4 * (fluid - vel[0])
        circ = vel[1] * (1.0 - 0.4)
        radial = vel[2] * (1.0 - 0.4)
        return [xi[0] + 0.25 * axial, xi[1] + 0.25 * circ, xi[2] + 1.0 * radial, axial, circ, radial]

    for load in loads[0:5]:
        load.wait()
    stay = 1.0 - dep_ref[...]
    state = update([xi_ref[d] for d in range(3)], [vel_ref[d] for d in range(3)], fluid_ref[0:64]) + [mom_ref[d] for d in range(3)]
    for at, value in enumerate(state):
        kept_ref[at] = value * stay
    saves[1].start()
    for load in loads[5:]:
        load.wait()
    saves[0].start()
    make_table(table_ref, 0, w_ref[...], bary_ref[...])
    for row in range(LATE):
        at = 6 - LATE + row
        sample(table_ref, 0, 1, arr_ref[at, 9].astype(jnp.int32), [arr_ref[at, d] for d in range(3)], basis_ref.at[row], keeper(row))
    for row in range(6):
        state = [arr_ref[row, d] for d in range(11)]
        live = state[10] if absent[row] is None else state[10] * jnp.where(absent[row], 0.0, 1.0)
        fluid = fluid_ref[64 + 8 * row:72 + 8 * row] if row < 6 - LATE else late_ref[row - 6 + LATE]
        for at, value in enumerate(update(state[0:3], state[3:6], fluid) + state[6:9]):
            arrived_ref[row, at] = value * live
    saves[2].start()
    for save in saves:
        save.wait()

def finish(sizes, w, bary, fluid, xi, vel, mom, dep, arr):
    args = (fluid, vel, xi, mom, dep, w, bary, arr)
    outs = (jax.ShapeDtypeStruct((256, 128), jnp.float32), jax.ShapeDtypeStruct((9, 64, 128), jnp.float32), jax.ShapeDtypeStruct((6, 9, 8, 128), jnp.float32))
    return pl.pallas_call(
        functools.partial(finish_kernel, sizes),
        out_shape=outs,
        in_specs=[pl.BlockSpec(memory_space=pl.ANY)] * 8,
        out_specs=(pl.BlockSpec(memory_space=pl.ANY),) * 3,
        scratch_shapes=[pltpu.VMEM(t.shape, t.dtype) for t in args + outs[1:]]
        + [pltpu.VMEM((1, 128, 768), jnp.bfloat16), pltpu.VMEM((LATE, 4, 64, 128), jnp.float32), pltpu.VMEM((LATE, 8, 128), jnp.float32),
           pltpu.SemaphoreType.DMA((8,)), pltpu.SemaphoreType.DMA((3,))],
        name="finish",
    )(*args)

def diff_table():
    b = bary_weights()
    eye = np.eye(8, dtype=bool)
    diff = np.where(eye, 1.0, GLL_NODES[:, None] - GLL_NODES[None, :])
    off = np.where(eye, 0.0, b[None, :] / b[:, None] / diff)
    return (off - np.eye(8) * np.sum(off, axis=1)[:, None]).astype(np.float32)

def pieces(a, count=2):
    parts = []
    rest = a.astype(np.float32)
    for _ in range(count):
        part = rest.astype(jnp.bfloat16)
        parts.append(part)
        rest = rest - part.astype(np.float32)
    return parts

def field_consts():
    d = diff_table()
    eye = np.eye(16, dtype=np.float32)

    def left(m):
        h, l = pieces(np.kron(eye, m))
        return np.block([[h, h], [l, l]])

    def right(m):
        h, l = pieces(4.0 * np.kron(eye, m))
        return np.block([[h, l], [h, l]])

    w8 = GLL_WEIGHTS.astype(np.float32)
    half = np.where((np.arange(8) == 0) | (np.arange(8) == 7), 0.5, 1.0)
    r = np.arange(32)[:, None] + np.zeros((1, 128))
    c = np.arange(128)[None, :] + np.zeros((32, 1))
    small = np.stack([np.tile(w8, 4)[:, None] * np.tile(w8, 16)[None, :], np.tile(half, 4)[:, None] * np.tile(half, 16)[None, :],
                      (r % 8 == 0) & (r > 0), (r % 8 == 7) & (r < 31), (c % 8 == 0) & (c > 0), (c % 8 == 7) & (c < 127)]).astype(np.float32)
    ends = np.zeros((8, 384), np.float32)
    for piece in range(3):
        ends[0, piece * 128] = 1.0
        ends[1, piece * 128 + 127] = 1.0
    spread = np.zeros((32, 128), np.float32)
    for piece in range(3):
        spread[piece * 8, 0] = 1.0
        spread[piece * 8 + 1, 127] = 1.0
    bf = lambda t: np.ascontiguousarray(t).astype(jnp.bfloat16)
    return [bf(left(d)), bf(left(d.T)), bf(right(d.T)), bf(right(d)), small, bf(ends), bf(spread)]

def halves(x):
    high = x.astype(jnp.bfloat16)
    return high, (x - high.astype(jnp.float32)).astype(jnp.bfloat16)

def thirds(x):
    high, rest = x.astype(jnp.bfloat16), None
    rest = x - high.astype(jnp.float32)
    mid = rest.astype(jnp.bfloat16)
    return high, mid, (rest - mid.astype(jnp.float32)).astype(jnp.bfloat16)

def mix(a, b, dims=((1,), (0,))):
    return lax.dot_general(a, b, (dims, ((), ())), preferred_element_type=jnp.float32)

def along_circ(x, left):
    x = jnp.concatenate([x[0:128], x[128:256]], axis=1)
    y = mix(left, jnp.concatenate(halves(x), axis=0))
    y = y[0:128] + y[128:256]
    return jnp.concatenate([y[:, 0:128], y[:, 128:256]], axis=0)

def along_gap(x, right):
    y = mix(jnp.concatenate(halves(x), axis=1), right)
    return y[:, 0:128] + y[:, 128:256]

def along_ax(x, d):
    x = [x[i * 32:i * 32 + 32] for i in range(8)]
    even = [x[j] + x[7 - j] for j in range(4)]
    odd = [x[j] - x[7 - j] for j in range(4)]
    out = [None] * 8
    for i in range(4):
        a = b = None
        for j in range(4):
            p = np.float32(0.5 * (float(d[i, j]) - float(d[i, 7 - j]))) * odd[j]
            q = np.float32(0.5 * (float(d[i, j]) + float(d[i, 7 - j]))) * even[j]
            a = p if a is None else a + p
            b = q if b is None else b + q
        out[i] = a + b
        out[7 - i] = a - b
    return jnp.concatenate(out, axis=0)

def flow_kernel(sizes, *refs):
    sources, (out_ref, arr_out, dep_ref, fluid_ref), held, rest = refs[0:18], refs[18:22], refs[22:40], refs[40:]
    small_ref, w_ref, force_ref, ends_ref, yield_ref, lc_ref, rg_ref, spread_ref, slots_ref, counts_ref, xi_ref, vel_ref, mom_ref, new_ref, lct_ref, rgt_ref, bary_ref, el_ref = held
    (v_ref, f_ref, z_ref, quad_ref, stiff_ref, edge_c, edge_e, edge_g, got_a, got_c, got_e, got_g, pair_ref, sum_ref, got_sum, buf_ref, id_ref, arr_ref, table_ref, basis_ref, part_ref,
     send_sem, recv_sem, sum_send, sum_recv, mig_send, mig_recv, load_sem, keep_sem) = rest
    loads = [pltpu.make_async_copy(source, mine, load_sem.at[i]) for i, (source, mine) in enumerate(zip(sources, held))]
    for load in loads:
        load.start()
    n_ax, n_circ, n_gap = sizes
    d8 = diff_table()
    ax, circ, gap = lax.axis_index("ax"), lax.axis_index("circ"), lax.axis_index("gap")

    def at(da=0, dc=0, dg=0):
        place = {}
        if da:
            place["ax"] = lax.rem(ax + (da + n_ax), n_ax)
        if dc:
            place["circ"] = lax.rem(circ + (dc + n_circ), n_circ)
        if dg:
            place["gap"] = lax.rem(gap + (dg + n_gap), n_gap)
        return place

    around = [(a, c, g) for a in (0, -1, 1) for c in (0, -1, 1) for g in (0, -1, 1) if (a, c, g) != (0, 0, 0)]
    plane = [(a, g) for a in range(n_ax) for g in range(n_gap) if (a, g) != (0, 0)]
    near = [(a % n_ax, g % n_gap) for a in (0, -1, 1) for g in (0, -1, 1)]
    peers = [at(*d) for d in around] + [at(dc=o) for o in range(2, n_circ - 1)] + [at(da=o[0], dg=o[1]) for o in plane if o not in near]
    hops = lambda d, n: min(d, n - d)
    far_circ = sorted(range(1, n_circ), key=lambda o: -hops(o, n_circ))
    far_plane = sorted(plane, key=lambda o: -(hops(o[0], n_ax) + hops(o[1], n_gap)))
    barrier = pltpu.get_barrier_semaphore()
    for peer in peers:
        pl.semaphore_signal(barrier, inc=1, device_id=peer, device_id_type=MESH)

    for load in loads[0:4]:
        load.wait()
    weights = GLL_WEIGHTS.astype(np.float32)
    quad = jnp.concatenate([small_ref[0] * weights[i] for i in range(8)], axis=0)
    quad_ref[...] = quad
    col = lax.broadcasted_iota(jnp.int32, (32, 128), 1)
    at_wall = ((col == 0) & (gap == 0)) | ((col == 127) & (gap == n_gap - 1))
    wall = jnp.where(at_wall, 0.0, 1.0)
    share = small_ref[1] * jnp.where(at_wall, 2.0, 1.0)
    low_ax = jnp.where(ax == 0, 0.0, 1.0)
    high_ax = jnp.where(ax == n_ax - 1, 0.0, 1.0)
    low_gap = jnp.where(gap == 0, 0.0, 1.0)
    high_gap = jnp.where(gap == n_gap - 1, 0.0, 1.0)
    ax_share = [jnp.where(ax == 0, 1.0, 0.5)] + [1.0] * 6 + [jnp.where(ax == n_ax - 1, 1.0, 0.5)]
    pair_ref[...] = jnp.zeros((8, 256), jnp.float32)

    def every(tile):
        return jnp.concatenate([tile] * 8, axis=0)

    def gather_inner(f):
        f = f + every(small_ref[2]) * pltpu.roll(f, 1, 0) + every(small_ref[3]) * pltpu.roll(f, 255, 0)
        return f + every(small_ref[4]) * pltpu.roll(f, 1, 1) + every(small_ref[5]) * pltpu.roll(f, 127, 1)

    def remote(src, dst, k, t, place):
        return pltpu.make_async_remote_copy(src_ref=src, dst_ref=dst, send_sem=send_sem.at[k, t], recv_sem=recv_sem.at[k, t],
                                            device_id=place, device_id_type=MESH)

    def stage(k, f):
        f = gather_inner(f)
        f_ref[k] = f
        z_ref[k] = f
        edge_c[k, 0] = f_ref[k, pl.ds(0, 8, stride=32), :]
        edge_c[k, 1] = f_ref[k, pl.ds(31, 8, stride=32), :]
        for e, at_row in enumerate((0, 31, 224, 255)):
            edge_e[k, e] = f_ref[k, at_row:at_row + 1, :]
        return mix(ends_ref[...], jnp.concatenate(thirds(f), axis=1), ((1,), (1,)))

    def send(k, faces):
        copies = [remote(edge_e.at[k, e], got_e.at[k, 3 - e], k, 4 + e, at(da=1 if e >= 2 else -1, dc=1 if e % 2 else -1)) for e in range(4)]
        copies += [remote(edge_c.at[k, 0], got_c.at[k, 1], k, 2, at(dc=-1)),
                   remote(edge_c.at[k, 1], got_c.at[k, 0], k, 3, at(dc=1)),
                   remote(f_ref.at[k, 0:32], got_a.at[k, 1], k, 0, at(da=-1)),
                   remote(f_ref.at[k, 224:256], got_a.at[k, 0], k, 1, at(da=1))]
        for s in range(2):
            for h in range(2):
                edge_g[k, s, h] = faces[s:s + 1, h * 128:h * 128 + 128]
        later = []
        for s in range(2):
            dg = 1 if s else -1
            t = 8 + 9 * s
            for a in (-1, 1):
                for c in (-1, 1):
                    slot = 8 + (2 if a < 0 else 0) + (1 if c < 0 else 0)
                    later.append(remote(edge_g.at[k, s, 1 if a > 0 else 0], got_g.at[k, 1 - s, slot], k, t + slot - 3, at(da=a, dc=c, dg=dg)))
            for a in (-1, 1):
                slot = 7 if a < 0 else 6
                later.append(remote(edge_g.at[k, s, 1 if a > 0 else 0], got_g.at[k, 1 - s, slot], k, t + slot - 3, at(da=a, dg=dg)))
            for c in (0, -1, 1):
                slot = {0: 0, 1: 1, -1: 2}[c]
                later.append(remote(edge_g.at[k, s], got_g.at[k, 1 - s, 2 * slot:2 * slot + 2], k, t + slot, at(dc=c, dg=dg)))
        for copy in later + copies:
            copy.start()
        return copies + later

    lane = lax.broadcasted_iota(jnp.int32, (1, 128), 1)
    place_of = lax.bitwise_and(lane, 31)

    def receive(k, copies):
        for copy in copies:
            copy.wait_recv()
        z_ref[k, 0:32, :] = z_ref[k, 0:32, :] + got_a[k, 0] * low_ax
        z_ref[k, 224:256, :] = z_ref[k, 224:256, :] + got_a[k, 1] * high_ax
        z_ref[k, pl.ds(0, 8, stride=32), :] = z_ref[k, pl.ds(0, 8, stride=32), :] + got_c[k, 0]
        z_ref[k, pl.ds(31, 8, stride=32), :] = z_ref[k, pl.ds(31, 8, stride=32), :] + got_c[k, 1]
        for e, at_row in enumerate((0, 31, 224, 255)):
            z_ref[k, at_row:at_row + 1, :] = z_ref[k, at_row:at_row + 1, :] + got_e[k, e] * (low_ax if e < 2 else high_ax)
        for s in range(2):
            def moved(slot, shift, keep):
                return jnp.where(keep, pltpu.roll(got_g[k, s, slot], shift, 1), 0.0)

            low = moved(6, 32, lane < 32) + moved(8, 1, lane == 0) + moved(9, 63, lane == 31)
            high = moved(7, 96, lane >= 96) + moved(10, 65, lane == 96) + moved(11, 127, lane == 127)
            sides = []
            for h, extra in ((0, low * low_ax), (1, high * high_ax)):
                sides.append(got_g[k, s, h] + moved(2 + h, 97, place_of == 0) + moved(4 + h, 31, place_of == 31) + extra)
            for h in range(2):
                pair_ref[s:s + 1, h * 128:h * 128 + 128] = sides[h] * (high_gap if s else low_gap)
        pair = pair_ref[...]
        pair = jnp.concatenate(thirds(pair) + (jnp.zeros((8, 256), jnp.bfloat16),), axis=0)
        v_ref[k] = (z_ref[k] + mix(pair, spread_ref[...], ((0,), (0,)))) * every(wall)

    fields = [lambda b, ref=ref, d=d: ref[d, b * 8:b * 8 + 8, :] for ref in (xi_ref, vel_ref, mom_ref) for d in range(3)]
    fields.append(lambda b: id_ref[b * 8:b * 8 + 8, :])
    moves = [at(da=1), at(da=-1), at(dc=1), at(dc=-1), at(dg=1), at(dg=-1)]
    moving = [pltpu.make_async_remote_copy(src_ref=buf_ref.at[r], dst_ref=arr_ref.at[r], send_sem=mig_send.at[r], recv_sem=mig_recv.at[r],
                                           device_id=place, device_id_type=MESH) for r, place in enumerate(moves)]

    def pack_rows(first, last):
        @pl.loop(first, last)
        def _(row):
            leaving_row(fields, slots_ref, counts_ref[row], row, buf_ref)

        for copy in moving[first:last]:
            copy.start()

    faces = stage(0, quad * 0.25 * (4.0 * w_ref[...] + force_ref[...]))
    pl.semaphore_wait(barrier, len(peers))
    for load in loads[4:7]:
        load.wait()
    copies = send(0, faces)
    w = w_ref[...]
    slope_a, slope_c, slope_g = along_ax(w, d8), along_circ(w, lc_ref[...]), along_gap(w, rg_ref[...])
    squares = 1.0 + slope_a * slope_a + slope_c * slope_c + slope_g * slope_g
    stiff_ref[...] = quad * 0.25 * (0.05 + yield_ref[...] / jnp.sqrt(squares))
    for load in loads[7:]:
        load.wait()
    id_ref[...] = new_ref[...].astype(jnp.float32)
    pack_rows(0, 3)
    dep_ref[...] = departed_flags(slots_ref, counts_ref)
    receive(0, copies)

    def keeper(base, half):
        def put(k, s, value):
            part_ref[k, base, s:s + 1, :] = value

        return put

    def sample_kept(first, count, block, half):
        rows = pl.ds(pl.multiple_of(block * 8, 8), 8)
        sample(table_ref, first, count, el_ref[rows, :], [xi_ref[d, rows, :] for d in range(3)], basis_ref.at[half], keeper(block, half))

    def sample_arrived(first, count, row, half):
        sample(table_ref, first, count, arr_ref[row, 9].astype(jnp.int32), [arr_ref[row, d] for d in range(3)], basis_ref.at[half], keeper(row + 8, half))

    def sample_pairs(first, count):
        @pl.loop(0, 3)
        def _(two):
            for half in range(2):
                sample_kept(first, count, two * 2 + half, half)

    def total(x):
        return jnp.sum(x.reshape(32, 8, 128), axis=0)

    sums = []
    for k in range(3):
        v = v_ref[k]
        stiff = stiff_ref[...]
        slope_a, slope_c, slope_g = along_ax(v, d8), along_circ(v, lc_ref[...]), along_gap(v, rg_ref[...])
        if k < 2:
            image = quad_ref[...] * v + along_ax(stiff * slope_a, d8.T)
            image = image + along_circ(stiff * slope_c, lct_ref[...]) + along_gap(stiff * slope_g, rgt_ref[...])
            faces = stage(k + 1, image)
            sent, copies = copies, send(k + 1, faces)
        square = v * v
        sums.append(total(jnp.concatenate([square[i * 32:i * 32 + 32] * (share * ax_share[i]) for i in range(8)], axis=0)))
        sums.append(total(quad_ref[...] * square + stiff * (slope_a * slope_a + slope_c * slope_c + slope_g * slope_g)))
        if k == 0:
            pack_rows(3, 6)
            make_table(table_ref, 0, v_ref[0], bary_ref[...])
            sample_kept(0, 1, 6, 0)
            sample_kept(0, 1, 7, 1)
        if k == 1:
            make_table(table_ref, 1, v_ref[1], bary_ref[...])
            sample_pairs(0, 2)
        if k < 2:
            for copy in sent:
                copy.wait_send()
            receive(k + 1, copies)

    sub = lax.broadcasted_iota(jnp.int32, (8, 128), 0)
    part = lax.broadcasted_iota(jnp.int32, (8, 128), 1) // 16
    rows = jnp.zeros((8, 128), jnp.float32)
    for m, value in enumerate(sums):
        rows = jnp.where(sub == m, jnp.broadcast_to(jnp.sum(value, axis=0, keepdims=True), (8, 128)), rows)
    for shift in (64, 32, 16):
        rows = rows + pltpu.roll(rows, shift, 1)
    line = jnp.sum(jnp.where(sub == part, rows, 0.0), axis=0, keepdims=True)
    keep = pltpu.make_async_copy(arr_ref, arr_out, keep_sem)
    slot = 0
    for step, places in enumerate(([at(dc=o) for o in far_circ], [at(da=a, dg=g) for a, g in far_plane])):
        sum_ref[step] = line
        rounds = []
        for place in places:
            rounds.append(pltpu.make_async_remote_copy(src_ref=sum_ref.at[step], dst_ref=got_sum.at[slot], send_sem=sum_send.at[slot],
                                                       recv_sem=sum_recv.at[slot], device_id=place, device_id_type=MESH))
            slot += 1
        for copy in rounds:
            copy.start()
        if step == 0:
            for copy in copies:
                copy.wait_send()
            make_table(table_ref, 2, v_ref[2], bary_ref[...])
            sample_pairs(2, 1)
            sample_kept(1, 2, 6, 0)
        else:
            for copy in moving:
                copy.wait()
            keep.start()
            sample_arrived(0, 3, 0, 0)
            sample_arrived(0, 3, 1, 1)
            sample_arrived(0, 3, 2, 0)
            sample_arrived(0, 3, 3, 1)
            sample_kept(1, 2, 7, 0)
        for copy in rounds:
            copy.wait_recv()
        for o in range(len(places)):
            line = line + got_sum[slot - 1 - o]
        for copy in rounds:
            copy.wait_send()
    m = jnp.sum(jnp.where(sub == part, jnp.broadcast_to(line, (8, 128)), 0.0), axis=1, keepdims=True)
    m0, m1, m2, m3, m4, m5 = [m[i:i + 1, :] for i in range(6)]
    scale = m0 / m1
    m1 = m1 * scale
    m2 = m2 * scale * scale
    m3 = m3 * scale * scale * scale
    m4 = m4 * scale * scale * scale * scale
    m5 = m5 * scale * scale * scale * scale * scale

    def ratio(a, b):
        return jnp.where((a > 0.0) & (b > 0.0), a / b, 0.0)

    a0 = m0 / m1
    rr1 = a0 * a0 * m2 - m0
    e = 1.0 + rr1 / m0
    p1 = e * e * m1 - 2.0 * e * a0 * m2 + a0 * a0 * m3
    a1 = ratio(rr1, p1)
    c1 = a0 + a1 * e
    c2 = a0 * a1
    rr2 = m0 - 2.0 * c1 * m1 + (c1 * c1 + 2.0 * c2) * m2 - 2.0 * c1 * c2 * m3 + c2 * c2 * m4
    ra2 = m1 - 2.0 * c1 * m2 + (c1 * c1 + 2.0 * c2) * m3 - 2.0 * c1 * c2 * m4 + c2 * c2 * m5
    b1 = ratio(rr2, rr1)
    a2 = ratio(rr2, ra2 - b1 * ratio(rr2, a1))
    x0 = scale * (a0 + a1 * e + a2 * (1.0 + b1 * e))
    x1 = scale * scale * (-(c2 + a2 * (c1 + b1 * a0)))
    x2 = scale * scale * scale * (a2 * c2)
    out_ref[...] = x0 * v_ref[0] + x1 * v_ref[1] + x2 * v_ref[2]
    for base in range(14 - LATE):
        fluid_ref[base * 8:base * 8 + 8, :] = x0 * part_ref[0, base] + x1 * part_ref[1, base] + x2 * part_ref[2, base]
    keep.wait()

def flow(sizes, w, yld, force, xi, vel, mom, new, slots, counts, el):
    bary = bary_table()
    lc, lct, rg, rgt, small, ends, spread = field_consts()
    args = (small, w, force, ends, yld, lc, rg, spread, slots, counts, xi, vel, mom, new, lct, rgt, bary, el)
    vm = lambda *s: pltpu.VMEM(s, jnp.float32)
    sums = sizes[1] - 1 + sizes[0] * sizes[2] - 1
    whole = pl.BlockSpec(memory_space=pltpu.VMEM)
    kept = [pltpu.SMEM(t.shape, t.dtype) if t is counts else pltpu.VMEM(t.shape, t.dtype) for t in args]
    return pl.pallas_call(
        functools.partial(flow_kernel, sizes),
        out_shape=(jax.ShapeDtypeStruct((256, 128), jnp.float32), jax.ShapeDtypeStruct((6, 11, 8, 128), jnp.float32), jax.ShapeDtypeStruct((64, 128), jnp.float32),
                   jax.ShapeDtypeStruct((112 - 8 * LATE, 128), jnp.float32)),
        in_specs=[pl.BlockSpec(memory_space=pl.ANY)] * 18,
        out_specs=(whole, pl.BlockSpec(memory_space=pl.ANY), whole, whole),
        scratch_shapes=kept + [vm(3, 256, 128), vm(3, 256, 128), vm(3, 256, 128), vm(256, 128), vm(256, 128), vm(3, 2, 8, 128), vm(3, 4, 1, 128), vm(3, 2, 2, 1, 128),
                        vm(3, 2, 32, 128), vm(3, 2, 8, 128), vm(3, 4, 1, 128), vm(3, 2, 12, 1, 128), vm(8, 256), vm(2, 1, 128), vm(sums, 1, 128),
                        vm(6, 11, 8, 128), vm(64, 128), vm(6, 11, 8, 128), pltpu.VMEM((3, 128, 768), jnp.bfloat16), vm(2, 4, 64, 128), vm(3, 14, 8, 128),
                        pltpu.SemaphoreType.DMA((3, 26)), pltpu.SemaphoreType.DMA((3, 26)), pltpu.SemaphoreType.DMA((sums,)),
                        pltpu.SemaphoreType.DMA((sums,)), pltpu.SemaphoreType.DMA((6,)), pltpu.SemaphoreType.DMA((6,)), pltpu.SemaphoreType.DMA((18,)), pltpu.SemaphoreType.DMA],
        compiler_params=pltpu.CompilerParams(collective_id=0, has_side_effects=True),
        name="flow",
    )(*args)

def solution(mesh):
    sizes = (mesh.shape["ax"], mesh.shape["circ"], mesh.shape["gap"])

    def shards(w_old, yield_stress, force, xi, vel, mom, el, new, slots, counts):
        flat = lambda t: t.reshape(256, 128)
        xi, vel, mom = [t.reshape(3, 64, 128) for t in (xi, vel, mom)]
        w, arr, dep, fluid = flow(sizes, flat(w_old), flat(yield_stress), flat(force), xi, vel, mom, new.reshape(64, 128), slots.reshape(6, 8, 128), counts.reshape(6), el.reshape(64, 128))
        w_new, kept, arrived = finish(sizes, w, bary_table(), fluid, xi, vel, mom, dep, arr)
        return w_new.reshape(w_old.shape), kept.reshape(1, 1, 1, 9, 8192), arrived.reshape(1, 1, 1, 6, 9, 1024)

    spec = lambda n: P("ax", "circ", "gap", *([None] * n))
    return jax.shard_map(
        shards,
        mesh=mesh,
        in_specs=(spec(0), spec(0), spec(0), spec(2), spec(2), spec(2), spec(1), spec(1), spec(2), spec(1)),
        out_specs=(spec(0), spec(2), spec(3)),
        check_vma=False,
    )
```
